128 devices in a mesh: pipe: 2 (over core), space: 64 (over x, z, y).
Axes of the slice: x: 4, y: 4, z: 4, core: 2. Of those that a mesh axis runs over, the one named last changes fastest.
Arguments:
- saved_inputs: bfloat16 [2, 4, 16384, 512], P('pipe', None, 'space'), may hold values from -50 to 50
- project_in: bfloat16 [2, 512, 1536], P('pipe'), may hold values from -1.5 to 1.5
- project_out: bfloat16 [2, 512, 512], P('pipe'), may hold values from -0.25 to 0.25
- norm_gains: float32 [2, 512], P('pipe'), may hold values from 0.5 to 1.5
- neighbour_blocks: int32 [2, 4, 64, 2], P('pipe', None, 'space'), may hold values from 0 to 127, as said below
- cotangent: bfloat16 [4, 16384, 512], P(None, 'space'), may hold values from -6 to 6
Outputs:
- input_grads: bfloat16 [2, 4, 16384, 512], P('pipe', None, 'space')
The draws below stay inside these ranges and needn't reach their ends.
Inputs may be any that keep to these rules, and one draw needn't show every extreme that they name: `neighbour_blocks`: entry e of patch p names block q * 2 + r of patch q, with q != p and |q - p| <= 2; a distance of 2 occurs; entries of one patch may repeat.
All inputs are finite; a program needn't handle non-finite values.
Results may differ from the reference program's by a relative error of at most 0.014.
Values may be sent and summed in bfloat16 or wider, within the bound.
A program may use at most 128 MiB of HBM per device.

```python
import jax
import jax.numpy as jnp
from jax import lax

D = 512
HEADS = 32
HD = 16
PATCH = 256
BLK = 128
NB = 2
REACH = 2
MICRO = 4
SECTIONS = 2
PATCHES = 64
BLKS = 2
POINTS = 16384


def draw_saved_inputs(key, part):
    first_key = jax.random.fold_in(key, 0)
    layout = (SECTIONS, MICRO, POINTS, D)
    values = jax.random.normal(first_key, layout, jnp.float32)
    return jnp.clip(values, -50.0, 50.0).astype(jnp.bfloat16)


def draw_project_in(key, part):
    first_key = jax.random.fold_in(key, 0)
    values = jax.random.normal(first_key, (SECTIONS, D, 3 * D), jnp.float32) * D ** (-0.5)
    return jnp.clip(values, -1.5, 1.5).astype(jnp.bfloat16)


def draw_neighbour_blocks(key, part):
    first_key, second_key, third_key = jax.random.split(key, 3)
    layout = (SECTIONS, MICRO, PATCHES, NB)
    distance = jax.random.randint(first_key, layout, 1, REACH + 1)
    direction = jax.random.randint(second_key, layout, 0, 2) * 2 - 1
    within = jax.random.randint(third_key, layout, 0, BLKS)
    patch_index = lax.broadcasted_iota(jnp.int32, layout, 2)
    entry_index = lax.broadcasted_iota(jnp.int32, layout, 3)
    distance = jnp.where((patch_index % 4 == 0) & (entry_index == NB - 1), REACH, distance)
    target = patch_index + direction * distance
    target = jnp.where((target < 0) | (target >= PATCHES), patch_index - direction * distance, target)
    lowest = (entry_index == 0) & (patch_index == 1)
    highest = (entry_index == 0) & (patch_index == PATCHES - 2)
    target = jnp.where(lowest, 0, jnp.where(highest, PATCHES - 1, target))
    within = jnp.where(lowest, 0, jnp.where(highest, BLKS - 1, within))
    return (target * BLKS + within).astype(jnp.int32)


def block_scale(rng, shape, cuts, smallest, top_value):
    def one(position, shards_of):
        steps = jax.random.uniform(jax.random.fold_in(jax.random.fold_in(rng, 6), position), (shards_of,), jnp.float32, smallest / len(cuts), top_value / len(cuts))
        return jnp.repeat(jnp.exp(steps), shape[position] // shards_of).reshape((-1,) + (1,) * (len(shape) - position - 1))

    level = one(*cuts[0])
    for cut in cuts[1:]:
        level = level * one(*cut)
    return level


def normal_values(key, extent, scale, reach, pieces=(), kind=jnp.bfloat16):
    level = block_scale(key, extent, pieces, -0.22, 0.18) if pieces else 1.0
    entries = jax.random.normal(key, extent, jnp.float32) * scale * level
    return jnp.minimum(jnp.maximum(entries, -reach), reach).astype(kind)


def setup_inputs(seed: int = 0) -> dict:
    splits = jax.random.split(jax.random.key(seed), 7)
    return {
        "saved_inputs": draw_saved_inputs(jax.random.fold_in(splits[6], 71), 0),
        "project_in": draw_project_in(jax.random.fold_in(splits[6], 71), 0),
        "project_out": normal_values(splits[2], (SECTIONS, D, D), D ** -0.5, 0.25, ((0, 2),)),
        "norm_gains": jnp.clip(1.0 + 0.1 * jax.random.normal(splits[3], (SECTIONS, D), jnp.float32), 0.5, 1.5),
        "neighbour_blocks": draw_neighbour_blocks(jax.random.fold_in(splits[6], 71), 0),
        "cotangent": normal_values(splits[5], (MICRO, POINTS, D), 1.0, 6.0, ((1, 64),)),
    }


epsilon = 1e-05

def normalize(points, gain_row):
    values = points.astype(jnp.float32)
    centre = lax.optimization_barrier(jnp.mean(values, axis=-1, keepdims=True))
    spread = lax.optimization_barrier(jnp.mean(jnp.square(values - centre), axis=-1, keepdims=True))
    inverse = lax.rsqrt(spread + epsilon)
    scaled = (values - centre) * inverse
    return (scaled, inverse, (scaled * gain_row).astype(jnp.bfloat16))

def norm_backward(grad_normed, scaled, inverse, gain_row):
    weighted = grad_normed * gain_row
    return inverse * (weighted - lax.optimization_barrier(jnp.mean(weighted, axis=-1, keepdims=True)) - scaled * lax.optimization_barrier(jnp.mean(weighted * scaled, axis=-1, keepdims=True)))

def mixing(form, first_arg, second_arg):
    return jnp.einsum(form, first_arg.astype(jnp.float32), second_arg.astype(jnp.float32), precision=lax.Precision.HIGHEST)

def attend_backward(queries, key_rows, value_rows, grad_attn):
    group_heads = min(HEADS, max(1, 128 // HD))
    group_width = group_heads * HD
    factor = HD ** (-0.5)
    row_count = queries.shape[0]
    key_count = key_rows.shape[0]
    grad_query, grad_key, grad_value = ([], [], [])
    for column in range(0, D, group_width):
        query_group = queries[:, column:column + group_width].reshape(row_count, group_heads, HD)
        key_group = key_rows[:, column:column + group_width].reshape(key_count, group_heads, HD)
        value_group = value_rows[:, column:column + group_width].reshape(key_count, group_heads, HD)
        grad_group = grad_attn[:, column:column + group_width].reshape(row_count, group_heads, HD)
        scores = mixing('qhd,khd->hqk', query_group, key_group) * factor
        attention = jax.nn.softmax(scores, axis=-1)
        grad_probs = mixing('qhd,khd->hqk', grad_group, value_group)
        grad_scores = (attention * (grad_probs - lax.optimization_barrier(jnp.sum(attention * grad_probs, axis=-1, keepdims=True))) * factor).astype(jnp.bfloat16)
        grad_query.append(mixing('hqk,khd->qhd', grad_scores, key_group).reshape(row_count, group_width))
        grad_key.append(mixing('hqk,qhd->khd', grad_scores, query_group).reshape(key_count, group_width))
        grad_value.append(mixing('hqk,qhd->khd', attention.astype(jnp.bfloat16), grad_group).reshape(key_count, group_width))
    return (jnp.concatenate(grad_query, 1), jnp.concatenate(grad_key, 1), jnp.concatenate(grad_value, 1))

def block_backward(points, gain_row, weight_in, weight_out, block_ids, grad_out):
    scaled, inverse, normed = normalize(points, gain_row)
    projected = jnp.dot(normed, weight_in, preferred_element_type=jnp.float32).astype(jnp.bfloat16)
    grad_attn = jnp.dot(grad_out, weight_out.T, preferred_element_type=jnp.float32).astype(jnp.bfloat16)
    queries = projected[:, :D].reshape(PATCHES, PATCH, D)
    key_value = projected[:, D:].reshape(PATCHES, PATCH, 2 * D)
    pair_blocks = projected[:, D:].reshape(PATCHES * BLKS, BLK, 2 * D)
    grad_rows = grad_attn.reshape(PATCHES, PATCH, D)

    def patch_backward(patch_args):
        query_patch, own_pairs, patch_ids, grad_patch = patch_args
        fetched = jnp.take(pair_blocks, patch_ids.astype(jnp.int32), axis=0).reshape(NB * BLK, 2 * D)
        combined = jnp.concatenate([own_pairs, fetched], 0)
        grad_query, grad_key, grad_value = attend_backward(query_patch, combined[:, :D], combined[:, D:], grad_patch)
        return (grad_query, jnp.concatenate([grad_key, grad_value], 1))
    grad_query, grad_pairs = lax.map(patch_backward, (queries, key_value, block_ids, grad_rows))
    own_part = grad_pairs[:, :PATCH].reshape(PATCHES * BLKS, BLK, 2 * D)
    remote_part = grad_pairs[:, PATCH:].reshape(PATCHES * NB, BLK, 2 * D)
    summed = own_part.at[block_ids.reshape(-1).astype(jnp.int32)].add(remote_part)
    grad_project = jnp.concatenate([grad_query.reshape(POINTS, D), summed.reshape(POINTS, 2 * D)], 1).astype(jnp.bfloat16)
    grad_normed = jnp.dot(grad_project, weight_in.T, preferred_element_type=jnp.float32)
    return (grad_out.astype(jnp.float32) + norm_backward(grad_normed, scaled, inverse, gain_row)).astype(jnp.bfloat16)

def reference(saved_inputs, project_in, project_out, norm_gains, neighbour_blocks, cotangent):
    incoming = cotangent
    results = []
    for section in range(SECTIONS - 1, -1, -1):
        gradients = jnp.stack([block_backward(saved_inputs[section, micro_index], norm_gains[section], project_in[section], project_out[section], neighbour_blocks[section, micro_index], incoming[micro_index]) for micro_index in range(MICRO)])
        results.append(gradients)
        incoming = gradients
    return jnp.stack(results[::-1])
```

```python
import jax
import jax.numpy as jnp
from jax import lax
from jax.experimental import pallas as pl
from jax.experimental.pallas import tpu as pltpu
from jax.sharding import PartitionSpec as P

HEADS = 32
HD = 16
BLK = 128
REACH = 2


epsilon = 1e-05


def shifted(x, axis, by):
    peers = lax.axis_size(axis)
    pairs = [(i, i + by) for i in range(peers) if 0 <= i + by < peers]
    return lax.ppermute(x, axis, pairs)


def normalize(points, gain_row):
    values = points.astype(jnp.float32)
    centre = jnp.mean(values, axis=-1, keepdims=True)
    spread = jnp.mean(jnp.square(values - centre), axis=-1, keepdims=True)
    inverse = lax.rsqrt(spread + epsilon)
    scaled = (values - centre) * inverse
    return (scaled, inverse, (scaled * gain_row).astype(jnp.bfloat16))


def norm_backward(grad_normed, scaled, inverse, gain_row):
    weighted = grad_normed * gain_row
    return inverse * (
        weighted
        - jnp.mean(weighted, axis=-1, keepdims=True)
        - scaled * jnp.mean(weighted * scaled, axis=-1, keepdims=True)
    )


def attention_kernel(q_ref, k_ref, v_ref, g_ref, dq_ref, dk_ref, dv_ref):
    factor = HD ** (-0.5)
    width = q_ref.shape[1]
    q = q_ref[...]
    k = k_ref[...]
    v = v_ref[...]
    g = g_ref[...]
    head_of = lax.broadcasted_iota(jnp.int32, (1, width), 1) // HD
    dq_ref[...] = jnp.zeros_like(dq_ref)
    dk_ref[...] = jnp.zeros_like(dk_ref)
    dv_ref[...] = jnp.zeros_like(dv_ref)
    nt = (((1,), (1,)), ((), ()))
    tn = (((0,), (0,)), ((), ()))

    def head(h, carry):
        mask = head_of == h
        qm = jnp.where(mask, q, jnp.zeros_like(q))
        km = jnp.where(mask, k, jnp.zeros_like(k))
        gm = jnp.where(mask, g, jnp.zeros_like(g))
        scores = lax.dot_general(qm, k, nt, preferred_element_type=jnp.float32) * factor
        top = jnp.max(scores, axis=-1, keepdims=True)
        exps = jnp.exp(scores - top)
        attention = exps / jnp.sum(exps, axis=-1, keepdims=True)
        grad_probs = lax.dot_general(gm, v, nt, preferred_element_type=jnp.float32)
        row = jnp.sum(attention * grad_probs, axis=-1, keepdims=True)
        grad_scores = (attention * (grad_probs - row) * factor).astype(jnp.bfloat16)
        dq_ref[...] += jnp.dot(grad_scores, km, preferred_element_type=jnp.float32)
        dk_ref[...] += lax.dot_general(grad_scores, qm, tn, preferred_element_type=jnp.float32)
        dv_ref[...] += lax.dot_general(
            attention.astype(jnp.bfloat16), gm, tn, preferred_element_type=jnp.float32
        )
        return carry

    lax.fori_loop(0, width // HD, head, 0)


def attend_backward(queries, key_rows, value_rows, grad_attn):
    rows, width = queries.shape
    keys = key_rows.shape[0]
    group = 128
    groups = width // group
    row_spec = pl.BlockSpec((rows, group), lambda i: (0, i))
    key_spec = pl.BlockSpec((keys, group), lambda i: (0, i))
    flops = 2 * 5 * rows * keys * width * (group // HD)
    return pl.pallas_call(
        attention_kernel,
        grid=(groups,),
        in_specs=[row_spec, key_spec, key_spec, row_spec],
        out_specs=[row_spec, key_spec, key_spec],
        out_shape=[
            jax.ShapeDtypeStruct((rows, width), jnp.float32),
            jax.ShapeDtypeStruct((keys, width), jnp.float32),
            jax.ShapeDtypeStruct((keys, width), jnp.float32),
        ],
        cost_estimate=pl.CostEstimate(
            flops=flops,
            transcendentals=rows * keys * width // HD,
            bytes_accessed=2 * (2 * rows + 2 * keys) * width + 4 * (rows + 2 * keys) * width,
        ),
    )(queries, key_rows, value_rows, grad_attn)


def shards(saved_inputs, project_in, project_out, norm_gains, neighbour_blocks, cotangent):
    sections = lax.axis_size("pipe")
    segment_index = lax.axis_index("pipe")
    myself = lax.axis_index("space")
    micro_count = cotangent.shape[0]
    points = cotangent.shape[1]
    model_width = cotangent.shape[2]
    weight_in = project_in[0]
    weight_out = project_out[0]
    gain_row = norm_gains[0]
    block_count = points // BLK
    offsets = [shift_by for shift_by in range(-REACH, REACH + 1) if shift_by != 0]
    local_lists = neighbour_blocks[0, :, 0, :]

    def step(step_index, state_pair):
        incoming, collected = state_pair
        micro_index = step_index - (sections - 1 - segment_index)
        active = (micro_index >= 0) & (micro_index < micro_count)
        chosen = jnp.clip(micro_index, 0, micro_count - 1)
        grad_out = jnp.where(
            segment_index == sections - 1,
            lax.dynamic_index_in_dim(cotangent, chosen, 0, keepdims=False),
            incoming,
        )
        points_in = lax.dynamic_index_in_dim(saved_inputs[0], chosen, 0, keepdims=False)
        block_ids = lax.dynamic_index_in_dim(local_lists, chosen, 0, keepdims=False)
        owners = block_ids // block_count
        within = block_ids % block_count
        distance = owners - myself
        scaled, inverse, normed = normalize(points_in, gain_row)
        projected = jnp.dot(normed, weight_in, preferred_element_type=jnp.float32).astype(
            jnp.bfloat16
        )
        queries = projected[:, :model_width]
        own_pairs = projected[:, model_width:]
        grad_attn = jnp.dot(grad_out, weight_out.T, preferred_element_type=jnp.float32).astype(
            jnp.bfloat16
        )
        received = []
        for shift_by in offsets:
            received.append(shifted(own_pairs, "space", -shift_by))
        window_blocks = jnp.stack(received).reshape(
            len(offsets) * block_count, BLK, 2 * model_width
        )
        position = (
            jnp.where(distance < 0, distance + REACH, distance + REACH - 1) * block_count + within
        )
        fetched = jnp.take(window_blocks, position, axis=0)
        combined = jnp.concatenate([own_pairs, fetched.reshape(-1, 2 * model_width)], 0)
        grad_query, grad_key, grad_value = attend_backward(
            queries, combined[:, :model_width], combined[:, model_width:], grad_attn
        )
        grad_pairs = jnp.concatenate([grad_key, grad_value], 1)
        grad_own = grad_pairs[:points]
        grad_remote = grad_pairs[points:].reshape(-1, BLK, 2 * model_width)
        window_grads = (
            jnp.zeros((len(offsets) * block_count, BLK, 2 * model_width), jnp.float32)
            .at[position]
            .add(grad_remote)
        )
        window_grads = window_grads.reshape(len(offsets), points, 2 * model_width)
        for slot_index, shift_by in enumerate(offsets):
            grad_own = grad_own + shifted(window_grads[slot_index], "space", shift_by)
        grad_project = jnp.concatenate([grad_query, grad_own], 1).astype(jnp.bfloat16)
        grad_normed = jnp.dot(grad_project, weight_in.T, preferred_element_type=jnp.float32)
        result = (
            grad_out.astype(jnp.float32) + norm_backward(grad_normed, scaled, inverse, gain_row)
        ).astype(jnp.bfloat16)
        collected = jnp.where(
            active, lax.dynamic_update_index_in_dim(collected, result, chosen, 0), collected
        )
        passed = shifted(result, "pipe", -1)
        return (passed, collected)

    start_state = (
        jnp.zeros((points, model_width), jnp.bfloat16),
        jnp.zeros((micro_count, points, model_width), jnp.bfloat16),
    )
    final_state = lax.fori_loop(0, micro_count + sections - 1, step, start_state)
    return final_state[1][None]


def solution(mesh):
    return jax.shard_map(
        shards,
        mesh=mesh,
        in_specs=(
            P("pipe", None, "space", None),
            P("pipe", None, None),
            P("pipe", None, None),
            P("pipe", None),
            P("pipe", None, "space", None),
            P(None, "space", None),
        ),
        out_specs=P("pipe", None, "space", None),
        check_vma=False,
    )
```

```python
import jax
import jax.numpy as jnp
from jax import lax
from jax.experimental import pallas as pl
from jax.experimental.pallas import tpu as pltpu
from jax.sharding import PartitionSpec as P

HEADS = 32
HD = 16
BLK = 128
REACH = 2


epsilon = 1e-05


def shifted(x, axis, by):
    peers = lax.axis_size(axis)
    pairs = [(i, i + by) for i in range(peers) if 0 <= i + by < peers]
    return lax.ppermute(x, axis, pairs)


def normalize(points, gain_row):
    values = points.astype(jnp.float32)
    centre = jnp.mean(values, axis=-1, keepdims=True)
    spread = jnp.mean(jnp.square(values - centre), axis=-1, keepdims=True)
    inverse = lax.rsqrt(spread + epsilon)
    scaled = (values - centre) * inverse
    return (scaled, inverse, (scaled * gain_row).astype(jnp.bfloat16))


def norm_backward(grad_normed, scaled, inverse, gain_row):
    weighted = grad_normed * gain_row
    return inverse * (
        weighted
        - jnp.mean(weighted, axis=-1, keepdims=True)
        - scaled * jnp.mean(weighted * scaled, axis=-1, keepdims=True)
    )


def attention_kernel(q_ref, k_ref, v_ref, g_ref, dq_ref, dk_ref, dv_ref):
    factor = HD ** (-0.5)
    width = q_ref.shape[1]
    q = q_ref[...]
    k = k_ref[...]
    v = v_ref[...]
    g = g_ref[...]
    head_of = lax.broadcasted_iota(jnp.int32, (1, width), 1) // HD
    dq_ref[...] = jnp.zeros_like(dq_ref)
    dk_ref[...] = jnp.zeros_like(dk_ref)
    dv_ref[...] = jnp.zeros_like(dv_ref)
    nt = (((1,), (1,)), ((), ()))
    tn = (((0,), (0,)), ((), ()))

    def head(h, carry):
        mask = head_of == h
        qm = jnp.where(mask, q, jnp.zeros_like(q))
        km = jnp.where(mask, k, jnp.zeros_like(k))
        gm = jnp.where(mask, g, jnp.zeros_like(g))
        scores = lax.dot_general(qm, k, nt, preferred_element_type=jnp.float32) * factor
        top = jnp.max(scores, axis=-1, keepdims=True)
        exps = jnp.exp(scores - top)
        attention = exps / jnp.sum(exps, axis=-1, keepdims=True)
        grad_probs = lax.dot_general(gm, v, nt, preferred_element_type=jnp.float32)
        row = jnp.sum(attention * grad_probs, axis=-1, keepdims=True)
        grad_scores = (attention * (grad_probs - row) * factor).astype(jnp.bfloat16)
        dq_ref[...] += jnp.dot(grad_scores, km, preferred_element_type=jnp.float32)
        dk_ref[...] += lax.dot_general(grad_scores, qm, tn, preferred_element_type=jnp.float32)
        dv_ref[...] += lax.dot_general(
            attention.astype(jnp.bfloat16), gm, tn, preferred_element_type=jnp.float32
        )
        return carry

    lax.fori_loop(0, width // HD, head, 0)


def attend_backward(queries, key_rows, value_rows, grad_attn):
    rows, width = queries.shape
    keys = key_rows.shape[0]
    group = 128
    groups = width // group
    row_spec = pl.BlockSpec((rows, group), lambda i: (0, i))
    key_spec = pl.BlockSpec((keys, group), lambda i: (0, i))
    flops = 2 * 5 * rows * keys * width * (group // HD)
    return pl.pallas_call(
        attention_kernel,
        grid=(groups,),
        in_specs=[row_spec, key_spec, key_spec, row_spec],
        out_specs=[row_spec, key_spec, key_spec],
        out_shape=[
            jax.ShapeDtypeStruct((rows, width), jnp.float32),
            jax.ShapeDtypeStruct((keys, width), jnp.float32),
            jax.ShapeDtypeStruct((keys, width), jnp.float32),
        ],
        cost_estimate=pl.CostEstimate(
            flops=flops,
            transcendentals=rows * keys * width // HD,
            bytes_accessed=2 * (2 * rows + 2 * keys) * width + 4 * (rows + 2 * keys) * width,
        ),
    )(queries, key_rows, value_rows, grad_attn)


def shards(saved_inputs, project_in, project_out, norm_gains, neighbour_blocks, cotangent):
    sections = lax.axis_size("pipe")
    segment_index = lax.axis_index("pipe")
    myself = lax.axis_index("space")
    micro_count = cotangent.shape[0]
    points = cotangent.shape[1]
    model_width = cotangent.shape[2]
    weight_in = project_in[0]
    weight_out = project_out[0]
    weight_pairs = weight_in[:, model_width:]
    gain_row = norm_gains[0]
    block_count = points // BLK
    offsets = [shift_by for shift_by in range(-REACH, REACH + 1) if shift_by != 0]
    lists = neighbour_blocks[0, :, 0, :]
    owners = lists // block_count
    within = lists % block_count
    distance = owners - myself
    slot = jnp.where(distance < 0, distance + REACH, distance + REACH - 1)

    scaled, inverse, normed = normalize(saved_inputs[0], gain_row)
    projected = jnp.dot(normed, weight_in, preferred_element_type=jnp.float32).astype(jnp.bfloat16)
    queries = projected[:, :, :model_width]
    own_pairs = projected[:, :, model_width:]
    received = jnp.stack([shifted(normed, "space", -shift_by) for shift_by in offsets])
    received = received.reshape(len(offsets) * micro_count * block_count, BLK, model_width)
    micro_ids = lax.broadcasted_iota(jnp.int32, lists.shape, 0)
    gather_at = (slot * micro_count + micro_ids) * block_count + within
    fetched_normed = jnp.take(received, gather_at.reshape(-1), axis=0).reshape(
        micro_count, -1, model_width
    )
    fetched_pairs = jnp.dot(
        fetched_normed, weight_pairs, preferred_element_type=jnp.float32
    ).astype(jnp.bfloat16)
    pairs = jnp.concatenate([own_pairs, fetched_pairs], 1)
    scatter_at = slot * block_count + within

    def step(step_index, state_pair):
        incoming, collected = state_pair
        micro_index = step_index - (sections - 1 - segment_index)
        active = (micro_index >= 0) & (micro_index < micro_count)
        chosen = jnp.clip(micro_index, 0, micro_count - 1)
        grad_out = jnp.where(
            segment_index == sections - 1,
            lax.dynamic_index_in_dim(cotangent, chosen, 0, keepdims=False),
            incoming,
        )
        query_rows = lax.dynamic_index_in_dim(queries, chosen, 0, keepdims=False)
        pair_rows = lax.dynamic_index_in_dim(pairs, chosen, 0, keepdims=False)
        scaled_rows = lax.dynamic_index_in_dim(scaled, chosen, 0, keepdims=False)
        inverse_rows = lax.dynamic_index_in_dim(inverse, chosen, 0, keepdims=False)
        targets = lax.dynamic_index_in_dim(scatter_at, chosen, 0, keepdims=False)
        grad_attn = jnp.dot(grad_out, weight_out.T, preferred_element_type=jnp.float32).astype(
            jnp.bfloat16
        )
        grad_query, grad_key, grad_value = attend_backward(
            query_rows, pair_rows[:, :model_width], pair_rows[:, model_width:], grad_attn
        )
        grad_pairs = jnp.concatenate([grad_key, grad_value], 1)
        grad_own = grad_pairs[:points]
        grad_remote = jnp.dot(
            grad_pairs[points:].astype(jnp.bfloat16),
            weight_pairs.T,
            preferred_element_type=jnp.float32,
        ).reshape(-1, BLK, model_width)
        window_grads = (
            jnp.zeros((len(offsets) * block_count, BLK, model_width), jnp.float32)
            .at[targets]
            .add(grad_remote)
        )
        window_grads = window_grads.reshape(len(offsets), points, model_width)
        grad_project = jnp.concatenate([grad_query, grad_own], 1).astype(jnp.bfloat16)
        grad_normed = jnp.dot(grad_project, weight_in.T, preferred_element_type=jnp.float32)
        for slot_index, shift_by in enumerate(offsets):
            grad_normed = grad_normed + shifted(window_grads[slot_index], "space", shift_by)
        result = (
            grad_out.astype(jnp.float32)
            + norm_backward(grad_normed, scaled_rows, inverse_rows, gain_row)
        ).astype(jnp.bfloat16)
        collected = jnp.where(
            active, lax.dynamic_update_index_in_dim(collected, result, chosen, 0), collected
        )
        passed = shifted(result, "pipe", -1)
        return (passed, collected)

    start_state = (
        jnp.zeros((points, model_width), jnp.bfloat16),
        jnp.zeros((micro_count, points, model_width), jnp.bfloat16),
    )
    final_state = lax.fori_loop(0, micro_count + sections - 1, step, start_state)
    return final_state[1][None]


def solution(mesh):
    return jax.shard_map(
        shards,
        mesh=mesh,
        in_specs=(
            P("pipe", None, "space", None),
            P("pipe", None, None),
            P("pipe", None, None),
            P("pipe", None),
            P("pipe", None, "space", None),
            P(None, "space", None),
        ),
        out_specs=P("pipe", None, "space", None),
        check_vma=False,
    )
```

```python
import jax
import jax.numpy as jnp
from jax import lax
from jax.experimental import pallas as pl
from jax.experimental.pallas import tpu as pltpu
from jax.sharding import PartitionSpec as P

HEADS = 32
HD = 16
BLK = 128
REACH = 2


epsilon = 1e-05


def shifted(x, axis, by):
    peers = lax.axis_size(axis)
    pairs = [(i, i + by) for i in range(peers) if 0 <= i + by < peers]
    return lax.ppermute(x, axis, pairs)


def normalize(points, gain_row):
    values = points.astype(jnp.float32)
    centre = jnp.mean(values, axis=-1, keepdims=True)
    spread = jnp.mean(jnp.square(values - centre), axis=-1, keepdims=True)
    inverse = lax.rsqrt(spread + epsilon)
    scaled = (values - centre) * inverse
    return (scaled, inverse, (scaled * gain_row).astype(jnp.bfloat16))


def norm_backward(grad_normed, scaled, inverse, gain_row):
    weighted = grad_normed * gain_row
    return inverse * (
        weighted
        - jnp.mean(weighted, axis=-1, keepdims=True)
        - scaled * jnp.mean(weighted * scaled, axis=-1, keepdims=True)
    )


def attention_kernel(q_ref, k_ref, v_ref, g_ref, dq_ref, dk_ref, dv_ref):
    factor = HD ** (-0.5)
    width = q_ref.shape[1]
    q = q_ref[...]
    k = k_ref[...]
    v = v_ref[...]
    g = g_ref[...]
    head_of = lax.broadcasted_iota(jnp.int32, (1, width), 1) // HD
    dq_ref[...] = jnp.zeros_like(dq_ref)
    dk_ref[...] = jnp.zeros_like(dk_ref)
    dv_ref[...] = jnp.zeros_like(dv_ref)
    nt = (((1,), (1,)), ((), ()))
    tn = (((0,), (0,)), ((), ()))

    def head(h, carry):
        mask = head_of == h
        qm = jnp.where(mask, q, jnp.zeros_like(q))
        km = jnp.where(mask, k, jnp.zeros_like(k))
        gm = jnp.where(mask, g, jnp.zeros_like(g))
        scores = lax.dot_general(qm, k, nt, preferred_element_type=jnp.float32) * factor
        top = jnp.max(scores, axis=-1, keepdims=True)
        exps = jnp.exp(scores - top)
        attention = exps / jnp.sum(exps, axis=-1, keepdims=True)
        grad_probs = lax.dot_general(gm, v, nt, preferred_element_type=jnp.float32)
        row = jnp.sum(attention * grad_probs, axis=-1, keepdims=True)
        grad_scores = (attention * (grad_probs - row) * factor).astype(jnp.bfloat16)
        dq_ref[...] += jnp.dot(grad_scores, km, preferred_element_type=jnp.float32)
        dk_ref[...] += lax.dot_general(grad_scores, qm, tn, preferred_element_type=jnp.float32)
        dv_ref[...] += lax.dot_general(
            attention.astype(jnp.bfloat16), gm, tn, preferred_element_type=jnp.float32
        )
        return carry

    lax.fori_loop(0, width // HD, head, 0)


def attend_backward(queries, key_rows, value_rows, grad_attn):
    rows, width = queries.shape
    keys = key_rows.shape[0]
    group = 128
    groups = width // group
    row_spec = pl.BlockSpec((rows, group), lambda i: (0, i))
    key_spec = pl.BlockSpec((keys, group), lambda i: (0, i))
    flops = 2 * 5 * rows * keys * width * (group // HD)
    return pl.pallas_call(
        attention_kernel,
        grid=(groups,),
        in_specs=[row_spec, key_spec, key_spec, row_spec],
        out_specs=[row_spec, key_spec, key_spec],
        out_shape=[
            jax.ShapeDtypeStruct((rows, width), jnp.float32),
            jax.ShapeDtypeStruct((keys, width), jnp.float32),
            jax.ShapeDtypeStruct((keys, width), jnp.float32),
        ],
        cost_estimate=pl.CostEstimate(
            flops=flops,
            transcendentals=rows * keys * width // HD,
            bytes_accessed=2 * (2 * rows + 2 * keys) * width + 4 * (rows + 2 * keys) * width,
        ),
    )(queries, key_rows, value_rows, grad_attn)


def shards(saved_inputs, project_in, project_out, norm_gains, neighbour_blocks, cotangent):
    sections = lax.axis_size("pipe")
    segment_index = lax.axis_index("pipe")
    myself = lax.axis_index("space")
    micro_count = cotangent.shape[0]
    points = cotangent.shape[1]
    model_width = cotangent.shape[2]
    weight_in = project_in[0]
    weight_out = project_out[0]
    weight_pairs = weight_in[:, model_width:]
    gain_row = norm_gains[0]
    block_count = points // BLK
    offsets = [shift_by for shift_by in range(-REACH, REACH + 1) if shift_by != 0]
    lists = neighbour_blocks[0, :, 0, :]
    owners = lists // block_count
    within = lists % block_count
    distance = owners - myself
    slot = jnp.where(distance < 0, distance + REACH, distance + REACH - 1)

    scaled, inverse, normed = normalize(saved_inputs[0], gain_row)
    projected = jnp.dot(normed, weight_in, preferred_element_type=jnp.float32).astype(jnp.bfloat16)
    queries = projected[:, :, :model_width]
    own_pairs = projected[:, :, model_width:]
    received = jnp.stack([shifted(normed, "space", -shift_by) for shift_by in offsets])
    received = received.reshape(len(offsets) * micro_count * block_count, BLK, model_width)
    micro_ids = lax.broadcasted_iota(jnp.int32, lists.shape, 0)
    gather_at = (slot * micro_count + micro_ids) * block_count + within
    fetched_normed = jnp.take(received, gather_at.reshape(-1), axis=0).reshape(
        micro_count, -1, model_width
    )
    fetched_pairs = jnp.dot(
        fetched_normed, weight_pairs, preferred_element_type=jnp.float32
    ).astype(jnp.bfloat16)
    pairs = jnp.concatenate([own_pairs, fetched_pairs], 1)
    scatter_at = slot * block_count + within

    def step(step_index, state_pair):
        incoming, collected = state_pair
        micro_index = step_index - (sections - 1 - segment_index)
        active = (micro_index >= 0) & (micro_index < micro_count)
        chosen = jnp.clip(micro_index, 0, micro_count - 1)
        grad_out = jnp.where(
            segment_index == sections - 1,
            lax.dynamic_index_in_dim(cotangent, chosen, 0, keepdims=False),
            incoming,
        )
        query_rows = lax.dynamic_index_in_dim(queries, chosen, 0, keepdims=False)
        pair_rows = lax.dynamic_index_in_dim(pairs, chosen, 0, keepdims=False)
        scaled_rows = lax.dynamic_index_in_dim(scaled, chosen, 0, keepdims=False)
        inverse_rows = lax.dynamic_index_in_dim(inverse, chosen, 0, keepdims=False)
        targets = lax.dynamic_index_in_dim(scatter_at, chosen, 0, keepdims=False)
        grad_attn = jnp.dot(grad_out, weight_out.T, preferred_element_type=jnp.float32).astype(
            jnp.bfloat16
        )
        grad_query, grad_key, grad_value = attend_backward(
            query_rows, pair_rows[:, :model_width], pair_rows[:, model_width:], grad_attn
        )
        grad_pairs = jnp.concatenate([grad_key, grad_value], 1)
        grad_own = grad_pairs[:points]
        grad_remote = jnp.dot(
            grad_pairs[points:].astype(jnp.bfloat16),
            weight_pairs.T,
            preferred_element_type=jnp.float32,
        ).reshape(-1, BLK, model_width)
        window_grads = (
            jnp.zeros((len(offsets) * block_count, BLK, model_width), jnp.float32)
            .at[targets]
            .add(grad_remote)
        )
        window_grads = window_grads.reshape(len(offsets), points, model_width)
        grad_project = jnp.concatenate([grad_query, grad_own], 1).astype(jnp.bfloat16)
        grad_normed = jnp.dot(grad_project, weight_in.T, preferred_element_type=jnp.float32)
        for slot_index, shift_by in enumerate(offsets):
            grad_normed = grad_normed + shifted(
                window_grads[slot_index].astype(jnp.bfloat16), "space", shift_by
            ).astype(jnp.float32)
        result = (
            grad_out.astype(jnp.float32)
            + norm_backward(grad_normed, scaled_rows, inverse_rows, gain_row)
        ).astype(jnp.bfloat16)
        collected = jnp.where(
            active, lax.dynamic_update_index_in_dim(collected, result, chosen, 0), collected
        )
        passed = shifted(result, "pipe", -1)
        return (passed, collected)

    start_state = (
        jnp.zeros((points, model_width), jnp.bfloat16),
        jnp.zeros((micro_count, points, model_width), jnp.bfloat16),
    )
    final_state = lax.fori_loop(0, micro_count + sections - 1, step, start_state)
    return final_state[1][None]


def solution(mesh):
    return jax.shard_map(
        shards,
        mesh=mesh,
        in_specs=(
            P("pipe", None, "space", None),
            P("pipe", None, None),
            P("pipe", None, None),
            P("pipe", None),
            P("pipe", None, "space", None),
            P(None, "space", None),
        ),
        out_specs=P("pipe", None, "space", None),
        check_vma=False,
    )
```

```python
import jax
import jax.numpy as jnp
from jax import lax
from jax.experimental import pallas as pl
from jax.experimental.pallas import tpu as pltpu
from jax.sharding import PartitionSpec as P

HEADS = 32
HD = 16
BLK = 128
REACH = 2


epsilon = 1e-05


def shifted(x, axis, by):
    peers = lax.axis_size(axis)
    pairs = [(i, i + by) for i in range(peers) if 0 <= i + by < peers]
    return lax.ppermute(x, axis, pairs)


def normalize(points, gain_row):
    values = points.astype(jnp.float32)
    centre = jnp.mean(values, axis=-1, keepdims=True)
    spread = jnp.mean(jnp.square(values - centre), axis=-1, keepdims=True)
    inverse = lax.rsqrt(spread + epsilon)
    scaled = (values - centre) * inverse
    return (scaled, inverse, (scaled * gain_row).astype(jnp.bfloat16))


def norm_backward(grad_normed, scaled, inverse, gain_row):
    weighted = grad_normed * gain_row
    return inverse * (
        weighted
        - jnp.mean(weighted, axis=-1, keepdims=True)
        - scaled * jnp.mean(weighted * scaled, axis=-1, keepdims=True)
    )


def attention_kernel(q_ref, k_ref, v_ref, g_ref, dq_ref, dk_ref, dv_ref):
    factor = HD ** (-0.5)
    width = q_ref.shape[1]
    q = q_ref[...]
    k = k_ref[...]
    v = v_ref[...]
    g = g_ref[...]
    head_of = lax.broadcasted_iota(jnp.int32, (1, width), 1) // HD
    dq_ref[...] = jnp.zeros_like(dq_ref)
    dk_ref[...] = jnp.zeros_like(dk_ref)
    dv_ref[...] = jnp.zeros_like(dv_ref)
    nt = (((1,), (1,)), ((), ()))
    tn = (((0,), (0,)), ((), ()))

    def head(h, carry):
        mask = head_of == h
        qm = jnp.where(mask, q, jnp.zeros_like(q))
        km = jnp.where(mask, k, jnp.zeros_like(k))
        gm = jnp.where(mask, g, jnp.zeros_like(g))
        scores = lax.dot_general(qm, k, nt, preferred_element_type=jnp.float32) * factor
        top = jnp.max(scores, axis=-1, keepdims=True)
        exps = jnp.exp(scores - top)
        attention = exps / jnp.sum(exps, axis=-1, keepdims=True)
        grad_probs = lax.dot_general(gm, v, nt, preferred_element_type=jnp.float32)
        row = jnp.sum(attention * grad_probs, axis=-1, keepdims=True)
        grad_scores = (attention * (grad_probs - row) * factor).astype(jnp.bfloat16)
        dq_ref[...] += jnp.dot(grad_scores, km, preferred_element_type=jnp.float32)
        dk_ref[...] += lax.dot_general(grad_scores, qm, tn, preferred_element_type=jnp.float32)
        dv_ref[...] += lax.dot_general(
            attention.astype(jnp.bfloat16), gm, tn, preferred_element_type=jnp.float32
        )
        return carry

    lax.fori_loop(0, width // HD, head, 0)


def attend_backward(queries, key_rows, value_rows, grad_attn):
    rows, width = queries.shape
    keys = key_rows.shape[0]
    group = 128
    groups = width // group
    row_spec = pl.BlockSpec((rows, group), lambda i: (0, i))
    key_spec = pl.BlockSpec((keys, group), lambda i: (0, i))
    flops = 2 * 5 * rows * keys * width * (group // HD)
    return pl.pallas_call(
        attention_kernel,
        grid=(groups,),
        in_specs=[row_spec, key_spec, key_spec, row_spec],
        out_specs=[row_spec, key_spec, key_spec],
        out_shape=[
            jax.ShapeDtypeStruct((rows, width), jnp.float32),
            jax.ShapeDtypeStruct((keys, width), jnp.float32),
            jax.ShapeDtypeStruct((keys, width), jnp.float32),
        ],
        cost_estimate=pl.CostEstimate(
            flops=flops,
            transcendentals=rows * keys * width // HD,
            bytes_accessed=2 * (2 * rows + 2 * keys) * width + 4 * (rows + 2 * keys) * width,
        ),
    )(queries, key_rows, value_rows, grad_attn)


def swap_cores(value):
    return lax.ppermute(value, "pipe", [(0, 1), (1, 0)])


def pick(own, other, core, section):
    return jnp.where(core == section, own, other)


def prepare(rows, lists, weight_in, gain_row, myself):
    points, model_width = rows.shape
    block_count = points // BLK
    offsets = [shift_by for shift_by in range(-REACH, REACH + 1) if shift_by != 0]
    scaled, inverse, normed = normalize(rows, gain_row)
    projected = jnp.dot(normed, weight_in, preferred_element_type=jnp.float32).astype(jnp.bfloat16)
    received = jnp.stack([shifted(normed, "space", -shift_by) for shift_by in offsets])
    received = received.reshape(len(offsets) * block_count, BLK, model_width)
    owners = lists // block_count
    within = lists % block_count
    distance = owners - myself
    slot = jnp.where(distance < 0, distance + REACH, distance + REACH - 1)
    window_at = slot * block_count + within
    fetched = jnp.take(received, window_at, axis=0).reshape(-1, model_width)
    fetched_pairs = jnp.dot(
        fetched, weight_in[:, model_width:], preferred_element_type=jnp.float32
    ).astype(jnp.bfloat16)
    pairs = jnp.concatenate([projected[:, model_width:], fetched_pairs], 0)
    return scaled, inverse, projected[:, :model_width], pairs, window_at


def block_backward(grad_out, prepared, weight_in, weight_out, gain_row):
    scaled, inverse, queries, pairs, window_at = prepared
    points, model_width = grad_out.shape
    block_count = points // BLK
    offsets = [shift_by for shift_by in range(-REACH, REACH + 1) if shift_by != 0]
    weight_pairs = weight_in[:, model_width:]
    grad_attn = jnp.dot(grad_out, weight_out.T, preferred_element_type=jnp.float32).astype(
        jnp.bfloat16
    )
    grad_query, grad_key, grad_value = attend_backward(
        queries, pairs[:, :model_width], pairs[:, model_width:], grad_attn
    )
    grad_pairs = jnp.concatenate([grad_key, grad_value], 1)
    grad_remote = jnp.dot(
        grad_pairs[points:].astype(jnp.bfloat16), weight_pairs.T, preferred_element_type=jnp.float32
    ).reshape(-1, BLK, model_width)
    window_grads = (
        jnp.zeros((len(offsets) * block_count, BLK, model_width), jnp.float32)
        .at[window_at]
        .add(grad_remote)
    ).reshape(len(offsets), points, model_width)
    grad_project = jnp.concatenate([grad_query, grad_pairs[:points]], 1).astype(jnp.bfloat16)
    grad_normed = jnp.dot(grad_project, weight_in.T, preferred_element_type=jnp.float32)
    for slot_index, shift_by in enumerate(offsets):
        grad_normed = grad_normed + shifted(
            window_grads[slot_index].astype(jnp.bfloat16), "space", shift_by
        ).astype(jnp.float32)
    return (
        grad_out.astype(jnp.float32) + norm_backward(grad_normed, scaled, inverse, gain_row)
    ).astype(jnp.bfloat16)


def shards(saved_inputs, project_in, project_out, norm_gains, neighbour_blocks, cotangent):
    sections = lax.axis_size("pipe")
    core = lax.axis_index("pipe")
    other = sections - 1 - core
    myself = lax.axis_index("space")
    micro_count = cotangent.shape[0]
    half = micro_count // sections

    def mine(array, whose):
        grouped = array.reshape((half, sections) + array.shape[1:])
        return lax.dynamic_index_in_dim(grouped, whose, 1, keepdims=False)

    local_lists = neighbour_blocks[0, :, 0, :]
    own = (
        mine(saved_inputs[0], core),
        mine(local_lists, core),
        project_in[0],
        project_out[0],
        norm_gains[0],
    )
    got = swap_cores(
        (mine(saved_inputs[0], other), mine(local_lists, other), project_in[0], project_out[0], norm_gains[0])
    )
    params = [
        [pick(own_part, got_part, core, section) for own_part, got_part in zip(own, got)]
        for section in range(sections)
    ]
    cotangent_mine = mine(cotangent, core)
    prepared = [
        [
            prepare(params[section][0][j], params[section][1][j], params[section][2], params[section][4], myself)
            for j in range(half)
        ]
        for section in range(sections)
    ]
    results = [[None] * half for _ in range(sections)]
    exchanged = [[None] * half for _ in range(sections)]
    for section in range(sections - 1, -1, -1):
        _, _, weight_in, weight_out, gain_row = params[section]
        for j in range(half):
            grad_out = cotangent_mine[j] if section == sections - 1 else results[section + 1][j]
            results[section][j] = block_backward(
                grad_out, prepared[section][j], weight_in, weight_out, gain_row
            )
            exchanged[section][j] = swap_cores(results[section][j])
    own_out = jnp.stack(
        [pick(results[0][j], results[1][j], core, 0) for j in range(half)]
    )
    other_out = jnp.stack(
        [pick(exchanged[0][j], exchanged[1][j], core, 0) for j in range(half)]
    )
    grouped = jnp.stack(
        [pick(own_out, other_out, core, parity) for parity in range(sections)], 1
    )
    return grouped.reshape((1, micro_count) + grouped.shape[2:])


def solution(mesh):
    return jax.shard_map(
        shards,
        mesh=mesh,
        in_specs=(
            P("pipe", None, "space", None),
            P("pipe", None, None),
            P("pipe", None, None),
            P("pipe", None),
            P("pipe", None, "space", None),
            P(None, "space", None),
        ),
        out_specs=P("pipe", None, "space", None),
        check_vma=False,
    )
```

```python
import functools

import jax
import jax.numpy as jnp
from jax import lax
from jax.experimental import pallas as pl
from jax.experimental.pallas import tpu as pltpu
from jax.sharding import PartitionSpec as P

HEADS = 32
HD = 16
BLK = 128
REACH = 2


epsilon = 1e-05


def shifted(x, axis, by):
    peers = lax.axis_size(axis)
    pairs = [(i, i + by) for i in range(peers) if 0 <= i + by < peers]
    return lax.ppermute(x, axis, pairs)


def normalize(points, gain_row):
    values = points.astype(jnp.float32)
    centre = jnp.mean(values, axis=-1, keepdims=True)
    spread = jnp.mean(jnp.square(values - centre), axis=-1, keepdims=True)
    inverse = lax.rsqrt(spread + epsilon)
    scaled = (values - centre) * inverse
    return (scaled, inverse, (scaled * gain_row).astype(jnp.bfloat16))


def norm_backward(grad_normed, scaled, inverse, gain_row):
    weighted = grad_normed * gain_row
    return inverse * (
        weighted
        - jnp.mean(weighted, axis=-1, keepdims=True)
        - scaled * jnp.mean(weighted * scaled, axis=-1, keepdims=True)
    )


def attention_kernel(q_ref, k_ref, v_ref, g_ref, dq_ref, dk_ref, dv_ref):
    factor = HD ** (-0.5)
    width = q_ref.shape[1]
    q = q_ref[...]
    k = k_ref[...]
    v = v_ref[...]
    g = g_ref[...]
    head_of = lax.broadcasted_iota(jnp.int32, (1, width), 1) // HD
    dq_ref[...] = jnp.zeros_like(dq_ref)
    dk_ref[...] = jnp.zeros_like(dk_ref)
    dv_ref[...] = jnp.zeros_like(dv_ref)
    nt = (((1,), (1,)), ((), ()))
    tn = (((0,), (0,)), ((), ()))

    def head(h, carry):
        mask = head_of == h
        qm = jnp.where(mask, q, jnp.zeros_like(q))
        km = jnp.where(mask, k, jnp.zeros_like(k))
        gm = jnp.where(mask, g, jnp.zeros_like(g))
        scores = lax.dot_general(qm, k, nt, preferred_element_type=jnp.float32) * factor
        top = jnp.max(scores, axis=-1, keepdims=True)
        exps = jnp.exp(scores - top)
        attention = exps / jnp.sum(exps, axis=-1, keepdims=True)
        grad_probs = lax.dot_general(gm, v, nt, preferred_element_type=jnp.float32)
        row = jnp.sum(attention * grad_probs, axis=-1, keepdims=True)
        grad_scores = (attention * (grad_probs - row) * factor).astype(jnp.bfloat16)
        dq_ref[...] += jnp.dot(grad_scores, km, preferred_element_type=jnp.float32)
        dk_ref[...] += lax.dot_general(grad_scores, qm, tn, preferred_element_type=jnp.float32)
        dv_ref[...] += lax.dot_general(
            attention.astype(jnp.bfloat16), gm, tn, preferred_element_type=jnp.float32
        )
        return carry

    lax.fori_loop(0, width // HD, head, 0)


def attend_backward(queries, key_rows, value_rows, grad_attn):
    rows, width = queries.shape
    keys = key_rows.shape[0]
    group = 128
    groups = width // group
    row_spec = pl.BlockSpec((rows, group), lambda i: (0, i))
    key_spec = pl.BlockSpec((keys, group), lambda i: (0, i))
    flops = 2 * 5 * rows * keys * width * (group // HD)
    return pl.pallas_call(
        attention_kernel,
        grid=(groups,),
        in_specs=[row_spec, key_spec, key_spec, row_spec],
        out_specs=[row_spec, key_spec, key_spec],
        out_shape=[
            jax.ShapeDtypeStruct((rows, width), jnp.float32),
            jax.ShapeDtypeStruct((keys, width), jnp.float32),
            jax.ShapeDtypeStruct((keys, width), jnp.float32),
        ],
        cost_estimate=pl.CostEstimate(
            flops=flops,
            transcendentals=rows * keys * width // HD,
            bytes_accessed=2 * (2 * rows + 2 * keys) * width + 4 * (rows + 2 * keys) * width,
        ),
    )(queries, key_rows, value_rows, grad_attn)


MESH = pl.DeviceIdType.MESH
OFFSETS = [shift_by for shift_by in range(-REACH, REACH + 1) if shift_by != 0]


def exchange_kernel(per_target, x_ref, out_ref, send_sems, recv_sems):
    core = lax.axis_index("pipe")
    me = lax.axis_index("space")
    peers = lax.axis_size("space")
    barrier = pltpu.get_barrier_semaphore()

    def exists(shift_by):
        return (me + shift_by >= 0) & (me + shift_by < peers)

    for shift_by in OFFSETS:
        @pl.when(exists(shift_by))
        def _():
            pl.semaphore_signal(barrier, 1, device_id=(core, me + shift_by), device_id_type=MESH)

    pl.semaphore_wait(barrier, sum(jnp.where(exists(shift_by), 1, 0) for shift_by in OFFSETS))

    def copy_to(index, shift_by):
        landing = OFFSETS.index(-shift_by)
        return pltpu.make_async_remote_copy(
            src_ref=x_ref.at[index] if per_target else x_ref,
            dst_ref=out_ref.at[landing],
            send_sem=send_sems.at[index],
            recv_sem=recv_sems.at[landing],
            device_id=(core, me + shift_by),
            device_id_type=MESH,
        )

    def copy_from(index, shift_by):
        return pltpu.make_async_remote_copy(
            src_ref=x_ref.at[index] if per_target else x_ref,
            dst_ref=out_ref.at[index],
            send_sem=send_sems.at[index],
            recv_sem=recv_sems.at[index],
            device_id=(core, me + shift_by),
            device_id_type=MESH,
        )

    for index, shift_by in enumerate(OFFSETS):
        @pl.when(exists(shift_by))
        def _():
            copy_to(index, shift_by).start()

    for index, shift_by in enumerate(OFFSETS):
        @pl.when(jnp.logical_not(exists(shift_by)))
        def _():
            out_ref[index] = jnp.zeros(out_ref.shape[1:], out_ref.dtype)

    for index, shift_by in enumerate(OFFSETS):
        @pl.when(exists(shift_by))
        def _():
            copy_to(index, shift_by).wait_send()

    for index, shift_by in enumerate(OFFSETS):
        @pl.when(exists(shift_by))
        def _():
            copy_from(index, shift_by).wait_recv()


def exchange(payload, per_target, collective_id):
    shape = payload.shape[1:] if per_target else payload.shape
    return pl.pallas_call(
        functools.partial(exchange_kernel, per_target),
        out_shape=jax.ShapeDtypeStruct((len(OFFSETS),) + shape, payload.dtype),
        in_specs=[pl.BlockSpec(memory_space=pltpu.VMEM)],
        out_specs=pl.BlockSpec(memory_space=pltpu.VMEM),
        scratch_shapes=[
            pltpu.SemaphoreType.DMA((len(OFFSETS),)),
            pltpu.SemaphoreType.DMA((len(OFFSETS),)),
        ],
        compiler_params=pltpu.CompilerParams(collective_id=collective_id, has_side_effects=True),
    )(payload)


def swap_cores(value):
    return lax.ppermute(value, "pipe", [(0, 1), (1, 0)])


def pick(own, other, core, section):
    return jnp.where(core == section, own, other)


def prepare(rows, lists, weight_in, gain_row, myself, collective_id):
    points, model_width = rows.shape
    block_count = points // BLK
    offsets = [shift_by for shift_by in range(-REACH, REACH + 1) if shift_by != 0]
    scaled, inverse, normed = normalize(rows, gain_row)
    projected = jnp.dot(normed, weight_in, preferred_element_type=jnp.float32).astype(jnp.bfloat16)
    received = exchange(normed, False, collective_id)
    received = received.reshape(len(offsets) * block_count, BLK, model_width)
    owners = lists // block_count
    within = lists % block_count
    distance = owners - myself
    slot = jnp.where(distance < 0, distance + REACH, distance + REACH - 1)
    window_at = slot * block_count + within
    fetched = jnp.take(received, window_at, axis=0).reshape(-1, model_width)
    fetched_pairs = jnp.dot(
        fetched, weight_in[:, model_width:], preferred_element_type=jnp.float32
    ).astype(jnp.bfloat16)
    pairs = jnp.concatenate([projected[:, model_width:], fetched_pairs], 0)
    return scaled, inverse, projected[:, :model_width], pairs, window_at


def block_backward(grad_out, prepared, weight_in, weight_out, gain_row, collective_id):
    scaled, inverse, queries, pairs, window_at = prepared
    points, model_width = grad_out.shape
    block_count = points // BLK
    offsets = [shift_by for shift_by in range(-REACH, REACH + 1) if shift_by != 0]
    weight_pairs = weight_in[:, model_width:]
    grad_attn = jnp.dot(grad_out, weight_out.T, preferred_element_type=jnp.float32).astype(
        jnp.bfloat16
    )
    grad_query, grad_key, grad_value = attend_backward(
        queries, pairs[:, :model_width], pairs[:, model_width:], grad_attn
    )
    grad_pairs = jnp.concatenate([grad_key, grad_value], 1)
    grad_remote = jnp.dot(
        grad_pairs[points:].astype(jnp.bfloat16), weight_pairs.T, preferred_element_type=jnp.float32
    ).reshape(-1, BLK, model_width)
    window_grads = (
        jnp.zeros((len(offsets) * block_count, BLK, model_width), jnp.float32)
        .at[window_at]
        .add(grad_remote)
    ).reshape(len(offsets), points, model_width)
    grad_project = jnp.concatenate([grad_query, grad_pairs[:points]], 1).astype(jnp.bfloat16)
    grad_normed = jnp.dot(grad_project, weight_in.T, preferred_element_type=jnp.float32)
    returned = exchange(window_grads.astype(jnp.bfloat16), True, collective_id)
    grad_normed = grad_normed + jnp.sum(returned.astype(jnp.float32), axis=0)
    return (
        grad_out.astype(jnp.float32) + norm_backward(grad_normed, scaled, inverse, gain_row)
    ).astype(jnp.bfloat16)


def shards(saved_inputs, project_in, project_out, norm_gains, neighbour_blocks, cotangent):
    sections = lax.axis_size("pipe")
    core = lax.axis_index("pipe")
    other = sections - 1 - core
    myself = lax.axis_index("space")
    micro_count = cotangent.shape[0]
    half = micro_count // sections

    def mine(array, whose):
        grouped = array.reshape((half, sections) + array.shape[1:])
        return lax.dynamic_index_in_dim(grouped, whose, 1, keepdims=False)

    local_lists = neighbour_blocks[0, :, 0, :]
    own = (
        mine(saved_inputs[0], core),
        mine(local_lists, core),
        project_in[0],
        project_out[0],
        norm_gains[0],
    )
    got = swap_cores(
        (mine(saved_inputs[0], other), mine(local_lists, other), project_in[0], project_out[0], norm_gains[0])
    )
    params = [
        [pick(own_part, got_part, core, section) for own_part, got_part in zip(own, got)]
        for section in range(sections)
    ]
    cotangent_mine = mine(cotangent, core)
    prepared = [
        [
            prepare(
                params[section][0][j],
                params[section][1][j],
                params[section][2],
                params[section][4],
                myself,
                section * half + j,
            )
            for j in range(half)
        ]
        for section in range(sections)
    ]
    results = [[None] * half for _ in range(sections)]
    exchanged = [[None] * half for _ in range(sections)]
    for section in range(sections - 1, -1, -1):
        _, _, weight_in, weight_out, gain_row = params[section]
        for j in range(half):
            grad_out = cotangent_mine[j] if section == sections - 1 else results[section + 1][j]
            results[section][j] = block_backward(
                grad_out,
                prepared[section][j],
                weight_in,
                weight_out,
                gain_row,
                sections * half + section * half + j,
            )
            exchanged[section][j] = swap_cores(results[section][j])
    own_out = jnp.stack(
        [pick(results[0][j], results[1][j], core, 0) for j in range(half)]
    )
    other_out = jnp.stack(
        [pick(exchanged[0][j], exchanged[1][j], core, 0) for j in range(half)]
    )
    grouped = jnp.stack(
        [pick(own_out, other_out, core, parity) for parity in range(sections)], 1
    )
    return grouped.reshape((1, micro_count) + grouped.shape[2:])


def solution(mesh):
    return jax.shard_map(
        shards,
        mesh=mesh,
        in_specs=(
            P("pipe", None, "space", None),
            P("pipe", None, None),
            P("pipe", None, None),
            P("pipe", None),
            P("pipe", None, "space", None),
            P(None, "space", None),
        ),
        out_specs=P("pipe", None, "space", None),
        check_vma=False,
    )
```

```python
import functools

import jax
import jax.numpy as jnp
from jax import lax
from jax.experimental import pallas as pl
from jax.experimental.pallas import tpu as pltpu
from jax.sharding import PartitionSpec as P

HEADS = 32
HD = 16
BLK = 128
REACH = 2


epsilon = 1e-05


def shifted(x, axis, by):
    peers = lax.axis_size(axis)
    pairs = [(i, i + by) for i in range(peers) if 0 <= i + by < peers]
    return lax.ppermute(x, axis, pairs)


def normalize(points, gain_row):
    values = points.astype(jnp.float32)
    centre = jnp.mean(values, axis=-1, keepdims=True)
    spread = jnp.mean(jnp.square(values - centre), axis=-1, keepdims=True)
    inverse = lax.rsqrt(spread + epsilon)
    scaled = (values - centre) * inverse
    return (scaled, inverse, (scaled * gain_row).astype(jnp.bfloat16))


def norm_backward(grad_normed, scaled, inverse, gain_row):
    weighted = grad_normed * gain_row
    return inverse * (
        weighted
        - jnp.mean(weighted, axis=-1, keepdims=True)
        - scaled * jnp.mean(weighted * scaled, axis=-1, keepdims=True)
    )


MESH = pl.DeviceIdType.MESH
OFFSETS = [shift_by for shift_by in range(-REACH, REACH + 1) if shift_by != 0]


def attention_body(q_ref, k_ref, v_ref, g_ref, dq_ref, dk_ref, dv_ref):
    factor = HD ** (-0.5)
    group = 128
    nt = (((1,), (1,)), ((), ()))
    tn = (((0,), (0,)), ((), ()))
    head_of = lax.broadcasted_iota(jnp.int32, (1, group), 1) // HD
    dq_ref[...] = jnp.zeros_like(dq_ref)
    dk_ref[...] = jnp.zeros_like(dk_ref)
    dv_ref[...] = jnp.zeros_like(dv_ref)
    for first in range(0, q_ref.shape[1], group):
        cols = slice(first, first + group)
        q = q_ref[:, cols]
        k = k_ref[:, cols]
        v = v_ref[:, cols]
        g = g_ref[:, cols]

        def head(h, carry, q=q, k=k, v=v, g=g, cols=cols):
            mask = head_of == h
            qm = jnp.where(mask, q, jnp.zeros_like(q))
            km = jnp.where(mask, k, jnp.zeros_like(k))
            gm = jnp.where(mask, g, jnp.zeros_like(g))
            scores = lax.dot_general(qm, k, nt, preferred_element_type=jnp.float32) * factor
            top = jnp.max(scores, axis=-1, keepdims=True)
            exps = jnp.exp(scores - top)
            attention = exps / jnp.sum(exps, axis=-1, keepdims=True)
            grad_probs = lax.dot_general(gm, v, nt, preferred_element_type=jnp.float32)
            row = jnp.sum(attention * grad_probs, axis=-1, keepdims=True)
            grad_scores = (attention * (grad_probs - row) * factor).astype(jnp.bfloat16)
            dq_ref[:, cols] += jnp.dot(grad_scores, km, preferred_element_type=jnp.float32)
            dk_ref[:, cols] += lax.dot_general(
                grad_scores, qm, tn, preferred_element_type=jnp.float32
            )
            dv_ref[:, cols] += lax.dot_general(
                attention.astype(jnp.bfloat16), gm, tn, preferred_element_type=jnp.float32
            )
            return carry

        lax.fori_loop(0, group // HD, head, 0)


def exchange_start(spreads, payload_refs, out_refs, send_sems, recv_sems):
    core = lax.axis_index("pipe")
    me = lax.axis_index("space")
    peers = lax.axis_size("space")
    barrier = pltpu.get_barrier_semaphore()

    def exists(shift_by):
        return (me + shift_by >= 0) & (me + shift_by < peers)

    for shift_by in OFFSETS:

        @pl.when(exists(shift_by))
        def _():
            pl.semaphore_signal(barrier, 1, device_id=(core, me + shift_by), device_id_type=MESH)

    pl.semaphore_wait(barrier, sum(jnp.where(exists(shift_by), 1, 0) for shift_by in OFFSETS))

    def describe(which, index, landing, shift_by):
        spread, x_ref, out_ref = spreads[which], payload_refs[which], out_refs[which]
        return pltpu.make_async_remote_copy(
            src_ref=x_ref.at[index] if spread else x_ref,
            dst_ref=out_ref.at[landing],
            send_sem=send_sems.at[which, index],
            recv_sem=recv_sems.at[which, landing],
            device_id=(core, me + shift_by),
            device_id_type=MESH,
        )

    for which in range(len(spreads)):
        for index, shift_by in enumerate(OFFSETS):

            @pl.when(exists(shift_by))
            def _():
                describe(which, index, OFFSETS.index(-shift_by), shift_by).start()

        for index, shift_by in enumerate(OFFSETS):

            @pl.when(jnp.logical_not(exists(shift_by)))
            def _():
                out_refs[which][index] = jnp.zeros(out_refs[which].shape[1:], out_refs[which].dtype)

    def finish():
        for which in range(len(spreads)):
            for index, shift_by in enumerate(OFFSETS):

                @pl.when(exists(shift_by))
                def _():
                    describe(which, index, OFFSETS.index(-shift_by), shift_by).wait_send()

            for index, shift_by in enumerate(OFFSETS):

                @pl.when(exists(shift_by))
                def _():
                    describe(which, index, index, shift_by).wait_recv()

    return finish


def fused_kernel(spreads, with_attention, *refs):
    count = len(spreads)
    inputs = 4 if with_attention else 0
    outputs = 3 if with_attention else 0
    attention_in = refs[:inputs]
    payload_refs = refs[inputs : inputs + count]
    attention_out = refs[inputs + count : inputs + count + outputs]
    out_refs = refs[inputs + count + outputs : inputs + 2 * count + outputs]
    send_sems, recv_sems = refs[inputs + 2 * count + outputs :]
    finish = exchange_start(spreads, payload_refs, out_refs, send_sems, recv_sems)
    if with_attention:
        attention_body(*attention_in, *attention_out)
    finish()


def fused_step(attention_args, payloads, spreads, collective_id):
    vmem = pl.BlockSpec(memory_space=pltpu.VMEM)
    out_shapes = []
    flops = 0
    if attention_args:
        queries, key_rows, value_rows, grad_attn = attention_args
        rows, width = queries.shape
        keys = key_rows.shape[0]
        out_shapes = [
            jax.ShapeDtypeStruct((rows, width), jnp.float32),
            jax.ShapeDtypeStruct((keys, width), jnp.float32),
            jax.ShapeDtypeStruct((keys, width), jnp.float32),
        ]
        flops = 2 * 5 * rows * keys * width * (128 // HD)
    for payload, spread in zip(payloads, spreads):
        shape = payload.shape[1:] if spread else payload.shape
        out_shapes.append(jax.ShapeDtypeStruct((len(OFFSETS),) + shape, payload.dtype))
    moved = sum(len(OFFSETS) * x.size * x.dtype.itemsize for x in payloads)
    outs = pl.pallas_call(
        functools.partial(fused_kernel, tuple(spreads), bool(attention_args)),
        out_shape=out_shapes,
        in_specs=[vmem] * (len(attention_args) + len(payloads)),
        out_specs=[vmem] * len(out_shapes),
        scratch_shapes=[
            pltpu.SemaphoreType.DMA((len(payloads), len(OFFSETS))),
            pltpu.SemaphoreType.DMA((len(payloads), len(OFFSETS))),
        ],
        compiler_params=pltpu.CompilerParams(
            collective_id=collective_id,
            has_side_effects=True,
            vmem_limit_bytes=48 * 1024 * 1024,
        ),
        cost_estimate=pl.CostEstimate(
            flops=flops, transcendentals=flops // 160, bytes_accessed=moved + 1
        ),
    )(*attention_args, *payloads)
    return list(outs)


def swap_cores(value):
    return lax.ppermute(value, "pipe", [(0, 1), (1, 0)])


def pick(own, other, core, section):
    return jnp.where(core == section, own, other)


def prepare(rows, lists, weight_in, gain_row, myself):
    points, model_width = rows.shape
    block_count = points // BLK
    scaled, inverse, normed = normalize(rows, gain_row)
    projected = jnp.dot(normed, weight_in, preferred_element_type=jnp.float32).astype(jnp.bfloat16)
    owners = lists // block_count
    within = lists % block_count
    distance = owners - myself
    slot = jnp.where(distance < 0, distance + REACH, distance + REACH - 1)
    window_at = slot * block_count + within
    return dict(
        scaled=scaled,
        inverse=inverse,
        normed=normed,
        queries=projected[:, :model_width],
        own_pairs=projected[:, model_width:],
        window_at=window_at,
    )


def attach(unit, received, weight_in):
    points, model_width = unit["queries"].shape
    received = received.reshape(len(OFFSETS) * (points // BLK), BLK, model_width)
    fetched = jnp.take(received, unit["window_at"], axis=0).reshape(-1, model_width)
    fetched_pairs = jnp.dot(
        fetched, weight_in[:, model_width:], preferred_element_type=jnp.float32
    ).astype(jnp.bfloat16)
    unit["pairs"] = jnp.concatenate([unit["own_pairs"], fetched_pairs], 0)


def outgoing(unit, grad_key, grad_value, weight_in):
    points, model_width = unit["queries"].shape
    block_count = points // BLK
    grad_pairs = jnp.concatenate([grad_key, grad_value], 1)
    grad_remote = jnp.dot(
        grad_pairs[points:].astype(jnp.bfloat16),
        weight_in[:, model_width:].T,
        preferred_element_type=jnp.float32,
    ).reshape(-1, BLK, model_width)
    window_grads = (
        jnp.zeros((len(OFFSETS) * block_count, BLK, model_width), jnp.float32)
        .at[unit["window_at"]]
        .add(grad_remote)
    ).reshape(len(OFFSETS), points, model_width)
    unit["own_grad"] = grad_pairs[:points]
    return window_grads.astype(jnp.bfloat16)


def complete(unit, grad_out, grad_query, returned, weight_in, gain_row):
    grad_project = jnp.concatenate([grad_query, unit["own_grad"]], 1).astype(jnp.bfloat16)
    grad_normed = jnp.dot(grad_project, weight_in.T, preferred_element_type=jnp.float32)
    grad_normed = grad_normed + jnp.sum(returned.astype(jnp.float32), axis=0)
    return (
        grad_out.astype(jnp.float32)
        + norm_backward(grad_normed, unit["scaled"], unit["inverse"], gain_row)
    ).astype(jnp.bfloat16)


def shards(saved_inputs, project_in, project_out, norm_gains, neighbour_blocks, cotangent):
    sections = lax.axis_size("pipe")
    core = lax.axis_index("pipe")
    other = sections - 1 - core
    myself = lax.axis_index("space")
    micro_count = cotangent.shape[0]
    half = micro_count // sections
    model_width = cotangent.shape[2]

    def mine(array, whose):
        grouped = array.reshape((half, sections) + array.shape[1:])
        return lax.dynamic_index_in_dim(grouped, whose, 1, keepdims=False)

    local_lists = neighbour_blocks[0, :, 0, :]
    own = (
        mine(saved_inputs[0], core),
        mine(local_lists, core),
        project_in[0],
        project_out[0],
        norm_gains[0],
    )
    got = swap_cores(
        (
            mine(saved_inputs[0], other),
            mine(local_lists, other),
            project_in[0],
            project_out[0],
            norm_gains[0],
        )
    )
    params = [
        [pick(own_part, got_part, core, section) for own_part, got_part in zip(own, got)]
        for section in range(sections)
    ]
    cotangent_mine = mine(cotangent, core)
    order = [(section, j) for section in range(sections - 1, -1, -1) for j in range(half)]
    units = [
        prepare(params[section][0][j], params[section][1][j], params[section][2], params[section][4], myself)
        for section, j in order
    ]
    results = {}
    exchanged = {}
    ids = iter(range(len(order) + 2))
    (first_received,) = fused_step((), [units[0]["normed"]], [False], next(ids))
    attach(units[0], first_received, params[order[0][0]][2])
    pending = None
    for step, (section, j) in enumerate(order):
        unit = units[step]
        _, _, weight_in, weight_out, gain_row = params[section]
        grad_out = cotangent_mine[j] if section == sections - 1 else results[(section + 1, j)]
        unit["grad_out"] = grad_out
        grad_attn = jnp.dot(grad_out, weight_out.T, preferred_element_type=jnp.float32).astype(
            jnp.bfloat16
        )
        payloads, spreads = [], []
        if pending is not None:
            payloads.append(pending[1])
            spreads.append(True)
        if step + 1 < len(order):
            payloads.append(units[step + 1]["normed"])
            spreads.append(False)
        outs = fused_step(
            (unit["queries"], unit["pairs"][:, :model_width], unit["pairs"][:, model_width:], grad_attn),
            payloads,
            spreads,
            next(ids),
        )
        grad_query, grad_key, grad_value = outs[:3]
        received = outs[3:]
        if pending is not None:
            done_step, _ = pending
            done_section, done_j = order[done_step]
            done_unit = units[done_step]
            results[(done_section, done_j)] = complete(
                done_unit,
                done_unit["grad_out"],
                done_unit["grad_query"],
                received[0],
                params[done_section][2],
                params[done_section][4],
            )
            exchanged[(done_section, done_j)] = swap_cores(results[(done_section, done_j)])
            received = received[1:]
        if step + 1 < len(order):
            next_section = order[step + 1][0]
            attach(units[step + 1], received[0], params[next_section][2])
        unit["grad_query"] = grad_query
        pending = (step, outgoing(unit, grad_key, grad_value, weight_in))
    done_step, window = pending
    done_section, done_j = order[done_step]
    done_unit = units[done_step]
    (returned,) = fused_step((), [window], [True], next(ids))
    results[(done_section, done_j)] = complete(
        done_unit,
        done_unit["grad_out"],
        done_unit["grad_query"],
        returned,
        params[done_section][2],
        params[done_section][4],
    )
    exchanged[(done_section, done_j)] = swap_cores(results[(done_section, done_j)])
    own_out = jnp.stack([pick(results[(0, j)], results[(1, j)], core, 0) for j in range(half)])
    other_out = jnp.stack(
        [pick(exchanged[(0, j)], exchanged[(1, j)], core, 0) for j in range(half)]
    )
    grouped = jnp.stack([pick(own_out, other_out, core, parity) for parity in range(sections)], 1)
    return grouped.reshape((1, micro_count) + grouped.shape[2:])


def solution(mesh):
    return jax.shard_map(
        shards,
        mesh=mesh,
        in_specs=(
            P("pipe", None, "space", None),
            P("pipe", None, None),
            P("pipe", None, None),
            P("pipe", None),
            P("pipe", None, "space", None),
            P(None, "space", None),
        ),
        out_specs=P("pipe", None, "space", None),
        check_vma=False,
    )
```

```python
import functools

import jax
import jax.numpy as jnp
from jax import lax
from jax.experimental import pallas as pl
from jax.experimental.pallas import tpu as pltpu
from jax.sharding import PartitionSpec as P

HEADS = 32
HD = 16
BLK = 128
REACH = 2


epsilon = 1e-05


def shifted(x, axis, by):
    peers = lax.axis_size(axis)
    pairs = [(i, i + by) for i in range(peers) if 0 <= i + by < peers]
    return lax.ppermute(x, axis, pairs)


def normalize(points, gain_row):
    values = points.astype(jnp.float32)
    centre = jnp.mean(values, axis=-1, keepdims=True)
    spread = jnp.mean(jnp.square(values - centre), axis=-1, keepdims=True)
    inverse = lax.rsqrt(spread + epsilon)
    scaled = (values - centre) * inverse
    return (scaled, inverse, (scaled * gain_row).astype(jnp.bfloat16))


def norm_backward(grad_normed, scaled, inverse, gain_row):
    weighted = grad_normed * gain_row
    return inverse * (
        weighted
        - jnp.mean(weighted, axis=-1, keepdims=True)
        - scaled * jnp.mean(weighted * scaled, axis=-1, keepdims=True)
    )


MESH = pl.DeviceIdType.MESH
OFFSETS = [shift_by for shift_by in range(-REACH, REACH + 1) if shift_by != 0]


def attention_body(q_ref, k_ref, v_ref, g_ref, dq_ref, dk_ref, dv_ref):
    factor = HD ** (-0.5)
    group = 128
    nt = (((1,), (1,)), ((), ()))
    tn = (((0,), (0,)), ((), ()))
    head_of = lax.broadcasted_iota(jnp.int32, (1, group), 1) // HD
    dq_ref[...] = jnp.zeros_like(dq_ref)
    dk_ref[...] = jnp.zeros_like(dk_ref)
    dv_ref[...] = jnp.zeros_like(dv_ref)
    for first in range(0, q_ref.shape[1], group):
        cols = slice(first, first + group)
        q = q_ref[:, cols]
        k = k_ref[:, cols]
        v = v_ref[:, cols]
        g = g_ref[:, cols]

        def head(h, carry, q=q, k=k, v=v, g=g, cols=cols):
            mask = head_of == h
            qm = jnp.where(mask, q, jnp.zeros_like(q))
            km = jnp.where(mask, k, jnp.zeros_like(k))
            gm = jnp.where(mask, g, jnp.zeros_like(g))
            scores = lax.dot_general(qm, k, nt, preferred_element_type=jnp.float32) * factor
            top = jnp.max(scores, axis=-1, keepdims=True)
            exps = jnp.exp(scores - top)
            attention = exps / jnp.sum(exps, axis=-1, keepdims=True)
            grad_probs = lax.dot_general(gm, v, nt, preferred_element_type=jnp.float32)
            row = jnp.sum(attention * grad_probs, axis=-1, keepdims=True)
            grad_scores = (attention * (grad_probs - row) * factor).astype(jnp.bfloat16)
            dq_ref[:, cols] += jnp.dot(grad_scores, km, preferred_element_type=jnp.float32)
            dk_ref[:, cols] += lax.dot_general(
                grad_scores, qm, tn, preferred_element_type=jnp.float32
            )
            dv_ref[:, cols] += lax.dot_general(
                attention.astype(jnp.bfloat16), gm, tn, preferred_element_type=jnp.float32
            )
            return carry

        lax.fori_loop(0, group // HD, head, 0)


def exchange_start(spreads, payload_refs, out_refs, send_sems, recv_sems):
    core = lax.axis_index("pipe")
    me = lax.axis_index("space")
    peers = lax.axis_size("space")
    barrier = pltpu.get_barrier_semaphore()

    def exists(shift_by):
        return (me + shift_by >= 0) & (me + shift_by < peers)

    for shift_by in OFFSETS:

        @pl.when(exists(shift_by))
        def _():
            pl.semaphore_signal(barrier, 1, device_id=(core, me + shift_by), device_id_type=MESH)

    pl.semaphore_wait(barrier, sum(jnp.where(exists(shift_by), 1, 0) for shift_by in OFFSETS))

    def describe(which, index, landing, shift_by):
        spread, x_ref, out_ref = spreads[which], payload_refs[which], out_refs[which]
        return pltpu.make_async_remote_copy(
            src_ref=x_ref.at[index] if spread else x_ref,
            dst_ref=out_ref.at[landing],
            send_sem=send_sems.at[which, index],
            recv_sem=recv_sems.at[which, landing],
            device_id=(core, me + shift_by),
            device_id_type=MESH,
        )

    for which in range(len(spreads)):
        for index, shift_by in enumerate(OFFSETS):

            @pl.when(exists(shift_by))
            def _():
                describe(which, index, OFFSETS.index(-shift_by), shift_by).start()

        for index, shift_by in enumerate(OFFSETS):

            @pl.when(jnp.logical_not(exists(shift_by)))
            def _():
                out_refs[which][index] = jnp.zeros(out_refs[which].shape[1:], out_refs[which].dtype)

    def finish():
        for which in range(len(spreads)):
            for index, shift_by in enumerate(OFFSETS):

                @pl.when(exists(shift_by))
                def _():
                    describe(which, index, OFFSETS.index(-shift_by), shift_by).wait_send()

            for index, shift_by in enumerate(OFFSETS):

                @pl.when(exists(shift_by))
                def _():
                    describe(which, index, index, shift_by).wait_recv()

    return finish


def fused_kernel(spreads, with_attention, *refs):
    count = len(spreads)
    inputs = 4 if with_attention else 0
    outputs = 3 if with_attention else 0
    attention_in = refs[:inputs]
    payload_refs = refs[inputs : inputs + count]
    attention_out = refs[inputs + count : inputs + count + outputs]
    out_refs = refs[inputs + count + outputs : inputs + 2 * count + outputs]
    send_sems, recv_sems = refs[inputs + 2 * count + outputs :]
    finish = exchange_start(spreads, payload_refs, out_refs, send_sems, recv_sems)
    if with_attention:
        attention_body(*attention_in, *attention_out)
    finish()


def fused_step(attention_args, payloads, spreads, collective_id):
    vmem = pl.BlockSpec(memory_space=pltpu.VMEM)
    out_shapes = []
    flops = 0
    if attention_args:
        queries, key_rows, value_rows, grad_attn = attention_args
        rows, width = queries.shape
        keys = key_rows.shape[0]
        out_shapes = [
            jax.ShapeDtypeStruct((rows, width), jnp.float32),
            jax.ShapeDtypeStruct((keys, width), jnp.float32),
            jax.ShapeDtypeStruct((keys, width), jnp.float32),
        ]
        flops = 2 * 5 * rows * keys * width * (128 // HD)
    for payload, spread in zip(payloads, spreads):
        shape = payload.shape[1:] if spread else payload.shape
        out_shapes.append(jax.ShapeDtypeStruct((len(OFFSETS),) + shape, payload.dtype))
    moved = sum(len(OFFSETS) * x.size * x.dtype.itemsize for x in payloads)
    outs = pl.pallas_call(
        functools.partial(fused_kernel, tuple(spreads), bool(attention_args)),
        out_shape=out_shapes,
        in_specs=[vmem] * (len(attention_args) + len(payloads)),
        out_specs=[vmem] * len(out_shapes),
        scratch_shapes=[
            pltpu.SemaphoreType.DMA((len(payloads), len(OFFSETS))),
            pltpu.SemaphoreType.DMA((len(payloads), len(OFFSETS))),
        ],
        compiler_params=pltpu.CompilerParams(
            collective_id=collective_id,
            has_side_effects=True,
            vmem_limit_bytes=48 * 1024 * 1024,
        ),
        cost_estimate=pl.CostEstimate(
            flops=flops, transcendentals=flops // 160, bytes_accessed=moved + 1
        ),
    )(*attention_args, *payloads)
    return list(outs)


def swap_cores(value):
    return lax.ppermute(value, "pipe", [(0, 1), (1, 0)])


def pick(own, other, core, section):
    return jnp.where(core == section, own, other)


def prepare(rows, lists, weight_in, gain_row, myself):
    points, model_width = rows.shape
    block_count = points // BLK
    scaled, inverse, normed = normalize(rows, gain_row)
    projected = jnp.dot(normed, weight_in, preferred_element_type=jnp.float32).astype(jnp.bfloat16)
    owners = lists // block_count
    within = lists % block_count
    distance = owners - myself
    slot = jnp.where(distance < 0, distance + REACH, distance + REACH - 1)
    window_at = slot * block_count + within
    return dict(
        scaled=scaled,
        inverse=inverse,
        normed=normed,
        queries=projected[:, :model_width],
        own_pairs=projected[:, model_width:],
        window_at=window_at,
    )


def attach(unit, received, weight_in):
    points, model_width = unit["queries"].shape
    received = received.reshape(len(OFFSETS) * (points // BLK), BLK, model_width)
    fetched = jnp.take(received, unit["window_at"], axis=0).reshape(-1, model_width)
    fetched_pairs = jnp.dot(
        fetched, weight_in[:, model_width:], preferred_element_type=jnp.float32
    ).astype(jnp.bfloat16)
    unit["pairs"] = jnp.concatenate([unit["own_pairs"], fetched_pairs], 0)


def outgoing(unit, grad_key, grad_value, weight_in):
    points, model_width = unit["queries"].shape
    block_count = points // BLK
    grad_pairs = jnp.concatenate([grad_key, grad_value], 1)
    grad_remote = jnp.dot(
        grad_pairs[points:].astype(jnp.bfloat16),
        weight_in[:, model_width:].T,
        preferred_element_type=jnp.float32,
    ).reshape(-1, BLK, model_width)
    slots = lax.broadcasted_iota(jnp.int32, (len(OFFSETS) * block_count, 1, 1), 0)
    window_grads = sum(
        jnp.where(slots == unit["window_at"][entry], grad_remote[entry][None], 0.0)
        for entry in range(grad_remote.shape[0])
    )
    unit["own_grad"] = grad_pairs[:points]
    return window_grads.astype(jnp.bfloat16).reshape(len(OFFSETS), points, model_width)


def complete(unit, grad_out, grad_query, returned, weight_in, gain_row):
    grad_project = jnp.concatenate([grad_query, unit["own_grad"]], 1).astype(jnp.bfloat16)
    grad_normed = jnp.dot(grad_project, weight_in.T, preferred_element_type=jnp.float32)
    grad_normed = grad_normed + jnp.sum(returned.astype(jnp.float32), axis=0)
    return (
        grad_out.astype(jnp.float32)
        + norm_backward(grad_normed, unit["scaled"], unit["inverse"], gain_row)
    ).astype(jnp.bfloat16)


def shards(saved_inputs, project_in, project_out, norm_gains, neighbour_blocks, cotangent):
    sections = lax.axis_size("pipe")
    core = lax.axis_index("pipe")
    other = sections - 1 - core
    myself = lax.axis_index("space")
    micro_count = cotangent.shape[0]
    half = micro_count // sections
    model_width = cotangent.shape[2]

    def mine(array, whose):
        grouped = array.reshape((half, sections) + array.shape[1:])
        return lax.dynamic_index_in_dim(grouped, whose, 1, keepdims=False)

    local_lists = neighbour_blocks[0, :, 0, :]
    own = (
        mine(saved_inputs[0], core),
        mine(local_lists, core),
        project_in[0],
        project_out[0],
        norm_gains[0],
    )
    got = swap_cores(
        (
            mine(saved_inputs[0], other),
            mine(local_lists, other),
            project_in[0],
            project_out[0],
            norm_gains[0],
        )
    )
    params = [
        [pick(own_part, got_part, core, section) for own_part, got_part in zip(own, got)]
        for section in range(sections)
    ]
    cotangent_mine = mine(cotangent, core)
    order = [(section, j) for section in range(sections - 1, -1, -1) for j in range(half)]
    units = [
        prepare(params[section][0][j], params[section][1][j], params[section][2], params[section][4], myself)
        for section, j in order
    ]
    results = {}
    exchanged = {}
    ids = iter(range(len(order) + 2))
    (first_received,) = fused_step((), [units[0]["normed"]], [False], next(ids))
    attach(units[0], first_received, params[order[0][0]][2])
    pending = None
    for step, (section, j) in enumerate(order):
        unit = units[step]
        _, _, weight_in, weight_out, gain_row = params[section]
        grad_out = cotangent_mine[j] if section == sections - 1 else results[(section + 1, j)]
        unit["grad_out"] = grad_out
        grad_attn = jnp.dot(grad_out, weight_out.T, preferred_element_type=jnp.float32).astype(
            jnp.bfloat16
        )
        payloads, spreads = [], []
        if pending is not None:
            payloads.append(pending[1])
            spreads.append(True)
        if step + 1 < len(order):
            payloads.append(units[step + 1]["normed"])
            spreads.append(False)
        outs = fused_step(
            (unit["queries"], unit["pairs"][:, :model_width], unit["pairs"][:, model_width:], grad_attn),
            payloads,
            spreads,
            next(ids),
        )
        grad_query, grad_key, grad_value = outs[:3]
        received = outs[3:]
        if pending is not None:
            done_step, _ = pending
            done_section, done_j = order[done_step]
            done_unit = units[done_step]
            results[(done_section, done_j)] = complete(
                done_unit,
                done_unit["grad_out"],
                done_unit["grad_query"],
                received[0],
                params[done_section][2],
                params[done_section][4],
            )
            exchanged[(done_section, done_j)] = swap_cores(results[(done_section, done_j)])
            received = received[1:]
        if step + 1 < len(order):
            next_section = order[step + 1][0]
            attach(units[step + 1], received[0], params[next_section][2])
        unit["grad_query"] = grad_query
        pending = (step, outgoing(unit, grad_key, grad_value, weight_in))
    done_step, window = pending
    done_section, done_j = order[done_step]
    done_unit = units[done_step]
    (returned,) = fused_step((), [window], [True], next(ids))
    results[(done_section, done_j)] = complete(
        done_unit,
        done_unit["grad_out"],
        done_unit["grad_query"],
        returned,
        params[done_section][2],
        params[done_section][4],
    )
    exchanged[(done_section, done_j)] = swap_cores(results[(done_section, done_j)])
    own_out = jnp.stack([pick(results[(0, j)], results[(1, j)], core, 0) for j in range(half)])
    other_out = jnp.stack(
        [pick(exchanged[(0, j)], exchanged[(1, j)], core, 0) for j in range(half)]
    )
    grouped = jnp.stack([pick(own_out, other_out, core, parity) for parity in range(sections)], 1)
    return grouped.reshape((1, micro_count) + grouped.shape[2:])


def solution(mesh):
    return jax.shard_map(
        shards,
        mesh=mesh,
        in_specs=(
            P("pipe", None, "space", None),
            P("pipe", None, None),
            P("pipe", None, None),
            P("pipe", None),
            P("pipe", None, "space", None),
            P(None, "space", None),
        ),
        out_specs=P("pipe", None, "space", None),
        check_vma=False,
    )
```

```python
import functools

import jax
import jax.numpy as jnp
from jax import lax
from jax.experimental import pallas as pl
from jax.experimental.pallas import tpu as pltpu
from jax.sharding import PartitionSpec as P

HEADS = 32
HD = 16
BLK = 128
REACH = 2


epsilon = 1e-05


def shifted(x, axis, by):
    peers = lax.axis_size(axis)
    pairs = [(i, i + by) for i in range(peers) if 0 <= i + by < peers]
    return lax.ppermute(x, axis, pairs)


def normalize(points, gain_row):
    values = points.astype(jnp.float32)
    centre = jnp.mean(values, axis=-1, keepdims=True)
    spread = jnp.mean(jnp.square(values - centre), axis=-1, keepdims=True)
    inverse = lax.rsqrt(spread + epsilon)
    scaled = (values - centre) * inverse
    return (scaled, inverse, (scaled * gain_row).astype(jnp.bfloat16))


def norm_backward(grad_normed, scaled, inverse, gain_row):
    weighted = grad_normed * gain_row
    return inverse * (
        weighted
        - jnp.mean(weighted, axis=-1, keepdims=True)
        - scaled * jnp.mean(weighted * scaled, axis=-1, keepdims=True)
    )


MESH = pl.DeviceIdType.MESH
OFFSETS = [shift_by for shift_by in range(-REACH, REACH + 1) if shift_by != 0]


def attention_body(q_ref, k_ref, v_ref, g_ref, dq_ref, dk_ref, dv_ref, after_first):
    factor = HD ** (-0.5)
    group = 128
    nt = (((1,), (1,)), ((), ()))
    tn = (((0,), (0,)), ((), ()))
    head_of = lax.broadcasted_iota(jnp.int32, (1, group), 1) // HD
    dq_ref[...] = jnp.zeros_like(dq_ref)
    dk_ref[...] = jnp.zeros_like(dk_ref)
    dv_ref[...] = jnp.zeros_like(dv_ref)
    for first in range(0, q_ref.shape[1], group):
        cols = slice(first, first + group)
        q = q_ref[:, cols]
        k = k_ref[:, cols]
        v = v_ref[:, cols]
        g = g_ref[:, cols]

        def head(h, carry, q=q, k=k, v=v, g=g, cols=cols):
            mask = head_of == h
            qm = jnp.where(mask, q, jnp.zeros_like(q))
            km = jnp.where(mask, k, jnp.zeros_like(k))
            gm = jnp.where(mask, g, jnp.zeros_like(g))
            scores = lax.dot_general(qm, k, nt, preferred_element_type=jnp.float32) * factor
            top = jnp.max(scores, axis=-1, keepdims=True)
            exps = jnp.exp(scores - top)
            attention = exps / jnp.sum(exps, axis=-1, keepdims=True)
            grad_probs = lax.dot_general(gm, v, nt, preferred_element_type=jnp.float32)
            row = jnp.sum(attention * grad_probs, axis=-1, keepdims=True)
            grad_scores = (attention * (grad_probs - row) * factor).astype(jnp.bfloat16)
            dq_ref[:, cols] += jnp.dot(grad_scores, km, preferred_element_type=jnp.float32)
            dk_ref[:, cols] += lax.dot_general(
                grad_scores, qm, tn, preferred_element_type=jnp.float32
            )
            dv_ref[:, cols] += lax.dot_general(
                attention.astype(jnp.bfloat16), gm, tn, preferred_element_type=jnp.float32
            )
            return carry

        lax.fori_loop(0, group // HD, head, 0)
        if first == 0:
            after_first()


def exchange_start(spreads, payload_refs, out_refs, send_sems, recv_sems):
    core = lax.axis_index("pipe")
    me = lax.axis_index("space")
    peers = lax.axis_size("space")
    barrier = pltpu.get_barrier_semaphore()

    def exists(shift_by):
        return (me + shift_by >= 0) & (me + shift_by < peers)

    def slot(shift_by):
        return OFFSETS.index(shift_by)

    for shift_by in OFFSETS:

        @pl.when(exists(shift_by))
        def _():
            pl.semaphore_signal(barrier, 1, device_id=(core, me + shift_by), device_id_type=MESH)

    pl.semaphore_wait(barrier, sum(jnp.where(exists(shift_by), 1, 0) for shift_by in OFFSETS))

    def describe(which, source, landing, shift_by):
        return pltpu.make_async_remote_copy(
            src_ref=source,
            dst_ref=out_refs[which].at[landing],
            send_sem=send_sems.at[which, landing],
            recv_sem=recv_sems.at[which, landing],
            device_id=(core, me + shift_by),
            device_id_type=MESH,
        )

    def arrival(which, landing):
        return describe(which, out_refs[which].at[landing], landing, OFFSETS[landing])

    direct = []
    relayed = []
    for which, spread in enumerate(spreads):
        x_ref = payload_refs[which]
        targets = OFFSETS if spread else [-1, 1]
        for shift_by in targets:
            source = x_ref.at[slot(shift_by)] if spread else x_ref
            copy = describe(which, source, slot(-shift_by), shift_by)
            direct.append((copy, exists(shift_by)))

            @pl.when(exists(shift_by))
            def _():
                copy.start()

        for shift_by in OFFSETS:

            @pl.when(jnp.logical_not(exists(shift_by)))
            def _():
                out_refs[which][slot(shift_by)] = jnp.zeros(
                    out_refs[which].shape[1:], out_refs[which].dtype
                )

        if not spread:
            for shift_by in (-1, 1):
                forward = describe(
                    which, out_refs[which].at[slot(-shift_by)], slot(-2 * shift_by), shift_by
                )
                relayed.append((which, shift_by, forward, exists(shift_by) & exists(-shift_by)))

    def relay():
        for which, shift_by, forward, valid in relayed:

            @pl.when(exists(-shift_by))
            def _():
                arrival(which, slot(-shift_by)).wait_recv()

        for which, shift_by, forward, valid in relayed:

            @pl.when(valid)
            def _():
                forward.start()

    def finish():
        for copy, valid in direct:

            @pl.when(valid)
            def _():
                copy.wait_send()

        for which, shift_by, forward, valid in relayed:

            @pl.when(valid)
            def _():
                forward.wait_send()

        relayed_slots = {(which, slot(-shift_by)) for which, shift_by, _, _ in relayed}
        for which in range(len(spreads)):
            for landing, shift_by in enumerate(OFFSETS):
                if (which, landing) in relayed_slots:
                    continue

                @pl.when(exists(shift_by))
                def _():
                    arrival(which, landing).wait_recv()

    return relay, finish


def fused_kernel(spreads, with_attention, *refs):
    count = len(spreads)
    inputs = 4 if with_attention else 0
    outputs = 3 if with_attention else 0
    attention_in = refs[:inputs]
    payload_refs = refs[inputs : inputs + count]
    attention_out = refs[inputs + count : inputs + count + outputs]
    out_refs = refs[inputs + count + outputs : inputs + 2 * count + outputs]
    send_sems, recv_sems = refs[inputs + 2 * count + outputs :]
    relay, finish = exchange_start(spreads, payload_refs, out_refs, send_sems, recv_sems)
    if with_attention:
        attention_body(*attention_in, *attention_out, relay)
    else:
        relay()
    finish()


def fused_step(attention_args, payloads, spreads, collective_id):
    vmem = pl.BlockSpec(memory_space=pltpu.VMEM)
    out_shapes = []
    flops = 0
    if attention_args:
        queries, key_rows, value_rows, grad_attn = attention_args
        rows, width = queries.shape
        keys = key_rows.shape[0]
        out_shapes = [
            jax.ShapeDtypeStruct((rows, width), jnp.float32),
            jax.ShapeDtypeStruct((keys, width), jnp.float32),
            jax.ShapeDtypeStruct((keys, width), jnp.float32),
        ]
        flops = 2 * 5 * rows * keys * width * (128 // HD)
    for payload, spread in zip(payloads, spreads):
        shape = payload.shape[1:] if spread else payload.shape
        out_shapes.append(jax.ShapeDtypeStruct((len(OFFSETS),) + shape, payload.dtype))
    moved = sum(len(OFFSETS) * x.size * x.dtype.itemsize for x in payloads)
    outs = pl.pallas_call(
        functools.partial(fused_kernel, tuple(spreads), bool(attention_args)),
        out_shape=out_shapes,
        in_specs=[vmem] * (len(attention_args) + len(payloads)),
        out_specs=[vmem] * len(out_shapes),
        scratch_shapes=[
            pltpu.SemaphoreType.DMA((len(payloads), len(OFFSETS))),
            pltpu.SemaphoreType.DMA((len(payloads), len(OFFSETS))),
        ],
        compiler_params=pltpu.CompilerParams(
            collective_id=collective_id,
            has_side_effects=True,
            vmem_limit_bytes=48 * 1024 * 1024,
        ),
        cost_estimate=pl.CostEstimate(
            flops=flops, transcendentals=flops // 160, bytes_accessed=moved + 1
        ),
    )(*attention_args, *payloads)
    return list(outs)


def swap_cores(value):
    return lax.ppermute(value, "pipe", [(0, 1), (1, 0)])


def pick(own, other, core, section):
    return jnp.where(core == section, own, other)


def prepare(rows, lists, weight_in, gain_row, myself):
    points, model_width = rows.shape
    block_count = points // BLK
    scaled, inverse, normed = normalize(rows, gain_row)
    projected = jnp.dot(normed, weight_in, preferred_element_type=jnp.float32).astype(jnp.bfloat16)
    owners = lists // block_count
    within = lists % block_count
    distance = owners - myself
    slot = jnp.where(distance < 0, distance + REACH, distance + REACH - 1)
    window_at = slot * block_count + within
    return dict(
        scaled=scaled,
        inverse=inverse,
        normed=normed,
        queries=projected[:, :model_width],
        own_pairs=projected[:, model_width:],
        window_at=window_at,
    )


def attach(unit, received, weight_in):
    points, model_width = unit["queries"].shape
    received = received.reshape(len(OFFSETS) * (points // BLK), BLK, model_width)
    fetched = jnp.take(received, unit["window_at"], axis=0).reshape(-1, model_width)
    fetched_pairs = jnp.dot(
        fetched, weight_in[:, model_width:], preferred_element_type=jnp.float32
    ).astype(jnp.bfloat16)
    unit["pairs"] = jnp.concatenate([unit["own_pairs"], fetched_pairs], 0)


def outgoing(unit, grad_key, grad_value, weight_in):
    points, model_width = unit["queries"].shape
    block_count = points // BLK
    grad_pairs = jnp.concatenate([grad_key, grad_value], 1)
    grad_remote = jnp.dot(
        grad_pairs[points:].astype(jnp.bfloat16),
        weight_in[:, model_width:].T,
        preferred_element_type=jnp.float32,
    ).reshape(-1, BLK, model_width)
    slots = lax.broadcasted_iota(jnp.int32, (len(OFFSETS) * block_count, 1, 1), 0)
    window_grads = sum(
        jnp.where(slots == unit["window_at"][entry], grad_remote[entry][None], 0.0)
        for entry in range(grad_remote.shape[0])
    )
    unit["own_grad"] = grad_pairs[:points]
    return window_grads.astype(jnp.bfloat16).reshape(len(OFFSETS), points, model_width)


def complete(unit, grad_out, grad_query, returned, weight_in, gain_row):
    grad_project = jnp.concatenate([grad_query, unit["own_grad"]], 1).astype(jnp.bfloat16)
    grad_normed = jnp.dot(grad_project, weight_in.T, preferred_element_type=jnp.float32)
    grad_normed = grad_normed + jnp.sum(returned.astype(jnp.float32), axis=0)
    return (
        grad_out.astype(jnp.float32)
        + norm_backward(grad_normed, unit["scaled"], unit["inverse"], gain_row)
    ).astype(jnp.bfloat16)


def shards(saved_inputs, project_in, project_out, norm_gains, neighbour_blocks, cotangent):
    sections = lax.axis_size("pipe")
    core = lax.axis_index("pipe")
    other = sections - 1 - core
    myself = lax.axis_index("space")
    micro_count = cotangent.shape[0]
    half = micro_count // sections
    model_width = cotangent.shape[2]

    def mine(array, whose):
        grouped = array.reshape((half, sections) + array.shape[1:])
        return lax.dynamic_index_in_dim(grouped, whose, 1, keepdims=False)

    local_lists = neighbour_blocks[0, :, 0, :]
    own = (
        mine(saved_inputs[0], core),
        mine(local_lists, core),
        project_in[0],
        project_out[0],
        norm_gains[0],
    )
    got = swap_cores(
        (
            mine(saved_inputs[0], other),
            mine(local_lists, other),
            project_in[0],
            project_out[0],
            norm_gains[0],
        )
    )
    params = [
        [pick(own_part, got_part, core, section) for own_part, got_part in zip(own, got)]
        for section in range(sections)
    ]
    cotangent_mine = mine(cotangent, core)
    order = [(section, j) for section in range(sections - 1, -1, -1) for j in range(half)]
    units = [
        prepare(params[section][0][j], params[section][1][j], params[section][2], params[section][4], myself)
        for section, j in order
    ]
    results = {}
    exchanged = {}
    ids = iter(range(len(order) + 2))
    (first_received,) = fused_step((), [units[0]["normed"]], [False], next(ids))
    attach(units[0], first_received, params[order[0][0]][2])
    pending = None
    for step, (section, j) in enumerate(order):
        unit = units[step]
        _, _, weight_in, weight_out, gain_row = params[section]
        grad_out = cotangent_mine[j] if section == sections - 1 else results[(section + 1, j)]
        unit["grad_out"] = grad_out
        grad_attn = jnp.dot(grad_out, weight_out.T, preferred_element_type=jnp.float32).astype(
            jnp.bfloat16
        )
        payloads, spreads = [], []
        if pending is not None:
            payloads.append(pending[1])
            spreads.append(True)
        if step + 1 < len(order):
            payloads.append(units[step + 1]["normed"])
            spreads.append(False)
        outs = fused_step(
            (unit["queries"], unit["pairs"][:, :model_width], unit["pairs"][:, model_width:], grad_attn),
            payloads,
            spreads,
            next(ids),
        )
        grad_query, grad_key, grad_value = outs[:3]
        received = outs[3:]
        if pending is not None:
            done_step, _ = pending
            done_section, done_j = order[done_step]
            done_unit = units[done_step]
            results[(done_section, done_j)] = complete(
                done_unit,
                done_unit["grad_out"],
                done_unit["grad_query"],
                received[0],
                params[done_section][2],
                params[done_section][4],
            )
            exchanged[(done_section, done_j)] = swap_cores(results[(done_section, done_j)])
            received = received[1:]
        if step + 1 < len(order):
            next_section = order[step + 1][0]
            attach(units[step + 1], received[0], params[next_section][2])
        unit["grad_query"] = grad_query
        pending = (step, outgoing(unit, grad_key, grad_value, weight_in))
    done_step, window = pending
    done_section, done_j = order[done_step]
    done_unit = units[done_step]
    (returned,) = fused_step((), [window], [True], next(ids))
    results[(done_section, done_j)] = complete(
        done_unit,
        done_unit["grad_out"],
        done_unit["grad_query"],
        returned,
        params[done_section][2],
        params[done_section][4],
    )
    exchanged[(done_section, done_j)] = swap_cores(results[(done_section, done_j)])
    own_out = jnp.stack([pick(results[(0, j)], results[(1, j)], core, 0) for j in range(half)])
    other_out = jnp.stack(
        [pick(exchanged[(0, j)], exchanged[(1, j)], core, 0) for j in range(half)]
    )
    grouped = jnp.stack([pick(own_out, other_out, core, parity) for parity in range(sections)], 1)
    return grouped.reshape((1, micro_count) + grouped.shape[2:])


def solution(mesh):
    return jax.shard_map(
        shards,
        mesh=mesh,
        in_specs=(
            P("pipe", None, "space", None),
            P("pipe", None, None),
            P("pipe", None, None),
            P("pipe", None),
            P("pipe", None, "space", None),
            P(None, "space", None),
        ),
        out_specs=P("pipe", None, "space", None),
        check_vma=False,
    )
```

```python
import functools

import jax
import jax.numpy as jnp
from jax import lax
from jax.experimental import pallas as pl
from jax.experimental.pallas import tpu as pltpu
from jax.sharding import PartitionSpec as P

HEADS = 32
HD = 16
BLK = 128
REACH = 2


epsilon = 1e-05


def shifted(x, axis, by):
    peers = lax.axis_size(axis)
    pairs = [(i, i + by) for i in range(peers) if 0 <= i + by < peers]
    return lax.ppermute(x, axis, pairs)


def normalize(points, gain_row):
    values = points.astype(jnp.float32)
    centre = jnp.mean(values, axis=-1, keepdims=True)
    spread = jnp.mean(jnp.square(values - centre), axis=-1, keepdims=True)
    inverse = lax.rsqrt(spread + epsilon)
    scaled = (values - centre) * inverse
    return (scaled, inverse, (scaled * gain_row).astype(jnp.bfloat16))


def norm_backward(grad_normed, scaled, inverse, gain_row):
    weighted = grad_normed * gain_row
    return inverse * (
        weighted
        - jnp.mean(weighted, axis=-1, keepdims=True)
        - scaled * jnp.mean(weighted * scaled, axis=-1, keepdims=True)
    )


MESH = pl.DeviceIdType.MESH
OFFSETS = [shift_by for shift_by in range(-REACH, REACH + 1) if shift_by != 0]


def attention_body(q_ref, k_ref, v_ref, g_ref, dq_ref, dk_ref, dv_ref, after_first):
    factor = HD ** (-0.5)
    group = 128
    nt = (((1,), (1,)), ((), ()))
    tn = (((0,), (0,)), ((), ()))
    head_of = lax.broadcasted_iota(jnp.int32, (1, group), 1) // HD
    dq_ref[...] = jnp.zeros_like(dq_ref)
    dk_ref[...] = jnp.zeros_like(dk_ref)
    dv_ref[...] = jnp.zeros_like(dv_ref)
    for first in range(0, q_ref.shape[1], group):
        cols = slice(first, first + group)
        q = q_ref[:, cols]
        k = k_ref[:, cols]
        v = v_ref[:, cols]
        g = g_ref[:, cols]

        def head(h, carry, q=q, k=k, v=v, g=g, cols=cols):
            mask = head_of == h
            qm = jnp.where(mask, q, jnp.zeros_like(q))
            km = jnp.where(mask, k, jnp.zeros_like(k))
            gm = jnp.where(mask, g, jnp.zeros_like(g))
            scores = lax.dot_general(qm, k, nt, preferred_element_type=jnp.float32) * factor
            top = jnp.max(scores, axis=-1, keepdims=True)
            exps = jnp.exp(scores - top)
            attention = exps / jnp.sum(exps, axis=-1, keepdims=True)
            grad_probs = lax.dot_general(gm, v, nt, preferred_element_type=jnp.float32)
            row = jnp.sum(attention * grad_probs, axis=-1, keepdims=True)
            grad_scores = (attention * (grad_probs - row) * factor).astype(jnp.bfloat16)
            dq_ref[:, cols] += jnp.dot(grad_scores, km, preferred_element_type=jnp.float32)
            dk_ref[:, cols] += lax.dot_general(
                grad_scores, qm, tn, preferred_element_type=jnp.float32
            )
            dv_ref[:, cols] += lax.dot_general(
                attention.astype(jnp.bfloat16), gm, tn, preferred_element_type=jnp.float32
            )
            return carry

        lax.fori_loop(0, group // HD, head, 0)
        if first == 0:
            after_first()


def exchange_start(spreads, payload_refs, out_refs, send_sems, recv_sems):
    core = lax.axis_index("pipe")
    me = lax.axis_index("space")
    peers = lax.axis_size("space")
    barrier = pltpu.get_barrier_semaphore()

    def exists(shift_by):
        return (me + shift_by >= 0) & (me + shift_by < peers)

    def slot(shift_by):
        return OFFSETS.index(shift_by)

    for shift_by in OFFSETS:

        @pl.when(exists(shift_by))
        def _():
            pl.semaphore_signal(barrier, 1, device_id=(core, me + shift_by), device_id_type=MESH)

    pl.semaphore_wait(barrier, sum(jnp.where(exists(shift_by), 1, 0) for shift_by in OFFSETS))

    def describe(which, source, landing, shift_by):
        return pltpu.make_async_remote_copy(
            src_ref=source,
            dst_ref=out_refs[which].at[landing],
            send_sem=send_sems.at[which, landing],
            recv_sem=recv_sems.at[which, landing],
            device_id=(core, me + shift_by),
            device_id_type=MESH,
        )

    def arrival(which, landing):
        return describe(which, out_refs[which].at[landing], landing, OFFSETS[landing])

    direct = []
    relayed = []
    relaying = not any(spreads)
    for which, spread in enumerate(spreads):
        x_ref = payload_refs[which]
        targets = OFFSETS if spread or not relaying else [-1, 1]
        for shift_by in targets:
            source = x_ref.at[slot(shift_by)] if spread else x_ref
            copy = describe(which, source, slot(-shift_by), shift_by)
            direct.append((copy, exists(shift_by)))

            @pl.when(exists(shift_by))
            def _():
                copy.start()

        for shift_by in OFFSETS:

            @pl.when(jnp.logical_not(exists(shift_by)))
            def _():
                out_refs[which][slot(shift_by)] = jnp.zeros(
                    out_refs[which].shape[1:], out_refs[which].dtype
                )

        if relaying and not spread:
            for shift_by in (-1, 1):
                forward = describe(
                    which, out_refs[which].at[slot(-shift_by)], slot(-2 * shift_by), shift_by
                )
                relayed.append((which, shift_by, forward, exists(shift_by) & exists(-shift_by)))

    def relay():
        for which, shift_by, forward, valid in relayed:

            @pl.when(exists(-shift_by))
            def _():
                arrival(which, slot(-shift_by)).wait_recv()

        for which, shift_by, forward, valid in relayed:

            @pl.when(valid)
            def _():
                forward.start()

    def finish():
        for copy, valid in direct:

            @pl.when(valid)
            def _():
                copy.wait_send()

        for which, shift_by, forward, valid in relayed:

            @pl.when(valid)
            def _():
                forward.wait_send()

        relayed_slots = {(which, slot(-shift_by)) for which, shift_by, _, _ in relayed}
        for which in range(len(spreads)):
            for landing, shift_by in enumerate(OFFSETS):
                if (which, landing) in relayed_slots:
                    continue

                @pl.when(exists(shift_by))
                def _():
                    arrival(which, landing).wait_recv()

    return relay, finish


def fused_kernel(spreads, with_attention, *refs):
    count = len(spreads)
    inputs = 4 if with_attention else 0
    outputs = 3 if with_attention else 0
    attention_in = refs[:inputs]
    payload_refs = refs[inputs : inputs + count]
    attention_out = refs[inputs + count : inputs + count + outputs]
    out_refs = refs[inputs + count + outputs : inputs + 2 * count + outputs]
    send_sems, recv_sems = refs[inputs + 2 * count + outputs :]
    relay, finish = exchange_start(spreads, payload_refs, out_refs, send_sems, recv_sems)
    if with_attention:
        attention_body(*attention_in, *attention_out, relay)
    else:
        relay()
    finish()


def fused_step(attention_args, payloads, spreads, collective_id):
    vmem = pl.BlockSpec(memory_space=pltpu.VMEM)
    out_shapes = []
    flops = 0
    if attention_args:
        queries, key_rows, value_rows, grad_attn = attention_args
        rows, width = queries.shape
        keys = key_rows.shape[0]
        out_shapes = [
            jax.ShapeDtypeStruct((rows, width), jnp.float32),
            jax.ShapeDtypeStruct((keys, width), jnp.float32),
            jax.ShapeDtypeStruct((keys, width), jnp.float32),
        ]
        flops = 2 * 5 * rows * keys * width * (128 // HD)
    for payload, spread in zip(payloads, spreads):
        shape = payload.shape[1:] if spread else payload.shape
        out_shapes.append(jax.ShapeDtypeStruct((len(OFFSETS),) + shape, payload.dtype))
    moved = sum(len(OFFSETS) * x.size * x.dtype.itemsize for x in payloads)
    outs = pl.pallas_call(
        functools.partial(fused_kernel, tuple(spreads), bool(attention_args)),
        out_shape=out_shapes,
        in_specs=[vmem] * (len(attention_args) + len(payloads)),
        out_specs=[vmem] * len(out_shapes),
        scratch_shapes=[
            pltpu.SemaphoreType.DMA((len(payloads), len(OFFSETS))),
            pltpu.SemaphoreType.DMA((len(payloads), len(OFFSETS))),
        ],
        compiler_params=pltpu.CompilerParams(
            collective_id=collective_id,
            has_side_effects=True,
            vmem_limit_bytes=48 * 1024 * 1024,
        ),
        cost_estimate=pl.CostEstimate(
            flops=flops, transcendentals=flops // 160, bytes_accessed=moved + 1
        ),
    )(*attention_args, *payloads)
    return list(outs)


def swap_cores(value):
    return lax.ppermute(value, "pipe", [(0, 1), (1, 0)])


def pick(own, other, core, section):
    return jnp.where(core == section, own, other)


def prepare(rows, lists, weight_in, gain_row, myself):
    points, model_width = rows.shape
    block_count = points // BLK
    scaled, inverse, normed = normalize(rows, gain_row)
    projected = jnp.dot(normed, weight_in, preferred_element_type=jnp.float32).astype(jnp.bfloat16)
    owners = lists // block_count
    within = lists % block_count
    distance = owners - myself
    slot = jnp.where(distance < 0, distance + REACH, distance + REACH - 1)
    window_at = slot * block_count + within
    return dict(
        scaled=scaled,
        inverse=inverse,
        normed=normed,
        queries=projected[:, :model_width],
        own_pairs=projected[:, model_width:],
        window_at=window_at,
    )


def attach(unit, received, weight_in):
    points, model_width = unit["queries"].shape
    received = received.reshape(len(OFFSETS) * (points // BLK), BLK, model_width)
    fetched = jnp.take(received, unit["window_at"], axis=0).reshape(-1, model_width)
    fetched_pairs = jnp.dot(
        fetched, weight_in[:, model_width:], preferred_element_type=jnp.float32
    ).astype(jnp.bfloat16)
    unit["pairs"] = jnp.concatenate([unit["own_pairs"], fetched_pairs], 0)


def outgoing(unit, grad_key, grad_value, weight_in):
    points, model_width = unit["queries"].shape
    block_count = points // BLK
    grad_pairs = jnp.concatenate([grad_key, grad_value], 1)
    grad_remote = jnp.dot(
        grad_pairs[points:].astype(jnp.bfloat16),
        weight_in[:, model_width:].T,
        preferred_element_type=jnp.float32,
    ).reshape(-1, BLK, model_width)
    slots = lax.broadcasted_iota(jnp.int32, (len(OFFSETS) * block_count, 1, 1), 0)
    window_grads = sum(
        jnp.where(slots == unit["window_at"][entry], grad_remote[entry][None], 0.0)
        for entry in range(grad_remote.shape[0])
    )
    unit["own_grad"] = grad_pairs[:points]
    return window_grads.astype(jnp.bfloat16).reshape(len(OFFSETS), points, model_width)


def complete(unit, grad_out, grad_query, returned, weight_in, gain_row):
    grad_project = jnp.concatenate([grad_query, unit["own_grad"]], 1).astype(jnp.bfloat16)
    grad_normed = jnp.dot(grad_project, weight_in.T, preferred_element_type=jnp.float32)
    grad_normed = grad_normed + jnp.sum(returned.astype(jnp.float32), axis=0)
    return (
        grad_out.astype(jnp.float32)
        + norm_backward(grad_normed, unit["scaled"], unit["inverse"], gain_row)
    ).astype(jnp.bfloat16)


def shards(saved_inputs, project_in, project_out, norm_gains, neighbour_blocks, cotangent):
    sections = lax.axis_size("pipe")
    core = lax.axis_index("pipe")
    other = sections - 1 - core
    myself = lax.axis_index("space")
    micro_count = cotangent.shape[0]
    half = micro_count // sections
    model_width = cotangent.shape[2]

    def mine(array, whose):
        grouped = array.reshape((half, sections) + array.shape[1:])
        return lax.dynamic_index_in_dim(grouped, whose, 1, keepdims=False)

    local_lists = neighbour_blocks[0, :, 0, :]
    own = (
        mine(saved_inputs[0], core),
        mine(local_lists, core),
        project_in[0],
        project_out[0],
        norm_gains[0],
    )
    got = swap_cores(
        (
            mine(saved_inputs[0], other),
            mine(local_lists, other),
            project_in[0],
            project_out[0],
            norm_gains[0],
        )
    )
    params = [
        [pick(own_part, got_part, core, section) for own_part, got_part in zip(own, got)]
        for section in range(sections)
    ]
    cotangent_mine = mine(cotangent, core)
    order = [(section, j) for section in range(sections - 1, -1, -1) for j in range(half)]
    units = [
        prepare(params[section][0][j], params[section][1][j], params[section][2], params[section][4], myself)
        for section, j in order
    ]
    results = {}
    exchanged = {}
    ids = iter(range(len(order) + 2))
    (first_received,) = fused_step((), [units[0]["normed"]], [False], next(ids))
    attach(units[0], first_received, params[order[0][0]][2])
    pending = None
    for step, (section, j) in enumerate(order):
        unit = units[step]
        _, _, weight_in, weight_out, gain_row = params[section]
        grad_out = cotangent_mine[j] if section == sections - 1 else results[(section + 1, j)]
        unit["grad_out"] = grad_out
        grad_attn = jnp.dot(grad_out, weight_out.T, preferred_element_type=jnp.float32).astype(
            jnp.bfloat16
        )
        payloads, spreads = [], []
        if pending is not None:
            payloads.append(pending[1])
            spreads.append(True)
        if step + 1 < len(order):
            payloads.append(units[step + 1]["normed"])
            spreads.append(False)
        outs = fused_step(
            (unit["queries"], unit["pairs"][:, :model_width], unit["pairs"][:, model_width:], grad_attn),
            payloads,
            spreads,
            next(ids),
        )
        grad_query, grad_key, grad_value = outs[:3]
        received = outs[3:]
        if pending is not None:
            done_step, _ = pending
            done_section, done_j = order[done_step]
            done_unit = units[done_step]
            results[(done_section, done_j)] = complete(
                done_unit,
                done_unit["grad_out"],
                done_unit["grad_query"],
                received[0],
                params[done_section][2],
                params[done_section][4],
            )
            exchanged[(done_section, done_j)] = swap_cores(results[(done_section, done_j)])
            received = received[1:]
        if step + 1 < len(order):
            next_section = order[step + 1][0]
            attach(units[step + 1], received[0], params[next_section][2])
        unit["grad_query"] = grad_query
        pending = (step, outgoing(unit, grad_key, grad_value, weight_in))
    done_step, window = pending
    done_section, done_j = order[done_step]
    done_unit = units[done_step]
    (returned,) = fused_step((), [window], [True], next(ids))
    results[(done_section, done_j)] = complete(
        done_unit,
        done_unit["grad_out"],
        done_unit["grad_query"],
        returned,
        params[done_section][2],
        params[done_section][4],
    )
    exchanged[(done_section, done_j)] = swap_cores(results[(done_section, done_j)])
    own_out = jnp.stack([pick(results[(0, j)], results[(1, j)], core, 0) for j in range(half)])
    other_out = jnp.stack(
        [pick(exchanged[(0, j)], exchanged[(1, j)], core, 0) for j in range(half)]
    )
    grouped = jnp.stack([pick(own_out, other_out, core, parity) for parity in range(sections)], 1)
    return grouped.reshape((1, micro_count) + grouped.shape[2:])


def solution(mesh):
    return jax.shard_map(
        shards,
        mesh=mesh,
        in_specs=(
            P("pipe", None, "space", None),
            P("pipe", None, None),
            P("pipe", None, None),
            P("pipe", None),
            P("pipe", None, "space", None),
            P(None, "space", None),
        ),
        out_specs=P("pipe", None, "space", None),
        check_vma=False,
    )
```

```python
import functools

import jax
import jax.numpy as jnp
from jax import lax
from jax.experimental import pallas as pl
from jax.experimental.pallas import tpu as pltpu
from jax.sharding import PartitionSpec as P

HEADS = 32
HD = 16
BLK = 128
REACH = 2


epsilon = 1e-05


def shifted(x, axis, by):
    peers = lax.axis_size(axis)
    pairs = [(i, i + by) for i in range(peers) if 0 <= i + by < peers]
    return lax.ppermute(x, axis, pairs)


def normalize(points, gain_row):
    values = points.astype(jnp.float32)
    centre = jnp.mean(values, axis=-1, keepdims=True)
    spread = jnp.mean(jnp.square(values - centre), axis=-1, keepdims=True)
    inverse = lax.rsqrt(spread + epsilon)
    scaled = (values - centre) * inverse
    return (scaled, inverse, (scaled * gain_row).astype(jnp.bfloat16))


def norm_backward(grad_normed, scaled, inverse, gain_row):
    weighted = grad_normed * gain_row
    return inverse * (
        weighted
        - jnp.mean(weighted, axis=-1, keepdims=True)
        - scaled * jnp.mean(weighted * scaled, axis=-1, keepdims=True)
    )


MESH = pl.DeviceIdType.MESH
OFFSETS = [shift_by for shift_by in range(-REACH, REACH + 1) if shift_by != 0]


def attention_body(q_ref, k_ref, v_ref, g_ref, dq_ref, dk_ref, dv_ref, after_first):
    factor = HD ** (-0.5)
    group = 128
    nt = (((1,), (1,)), ((), ()))
    tn = (((0,), (0,)), ((), ()))
    head_of = lax.broadcasted_iota(jnp.int32, (1, group), 1) // HD
    dq_ref[...] = jnp.zeros_like(dq_ref)
    dk_ref[...] = jnp.zeros_like(dk_ref)
    dv_ref[...] = jnp.zeros_like(dv_ref)
    for first in range(0, q_ref.shape[1], group):
        cols = slice(first, first + group)
        q = q_ref[:, cols]
        k = k_ref[:, cols]
        v = v_ref[:, cols]
        g = g_ref[:, cols]

        def head(h, carry, q=q, k=k, v=v, g=g, cols=cols):
            mask = head_of == h
            qm = jnp.where(mask, q, jnp.zeros_like(q))
            km = jnp.where(mask, k, jnp.zeros_like(k))
            gm = jnp.where(mask, g, jnp.zeros_like(g))
            scores = lax.dot_general(qm, k, nt, preferred_element_type=jnp.float32) * factor
            top = jnp.max(scores, axis=-1, keepdims=True)
            exps = jnp.exp(scores - top)
            attention = exps / jnp.sum(exps, axis=-1, keepdims=True)
            grad_probs = lax.dot_general(gm, v, nt, preferred_element_type=jnp.float32)
            row = jnp.sum(attention * grad_probs, axis=-1, keepdims=True)
            grad_scores = (attention * (grad_probs - row) * factor).astype(jnp.bfloat16)
            dq_ref[:, cols] += jnp.dot(grad_scores, km, preferred_element_type=jnp.float32)
            dk_ref[:, cols] += lax.dot_general(
                grad_scores, qm, tn, preferred_element_type=jnp.float32
            )
            dv_ref[:, cols] += lax.dot_general(
                attention.astype(jnp.bfloat16), gm, tn, preferred_element_type=jnp.float32
            )
            return carry

        lax.fori_loop(0, group // HD, head, 0)
        if first == group:
            after_first()


def exchange_start(spreads, payload_refs, out_refs, send_sems, recv_sems):
    core = lax.axis_index("pipe")
    me = lax.axis_index("space")
    peers = lax.axis_size("space")
    barrier = pltpu.get_barrier_semaphore()

    def exists(shift_by):
        return (me + shift_by >= 0) & (me + shift_by < peers)

    def slot(shift_by):
        return OFFSETS.index(shift_by)

    for shift_by in OFFSETS:

        @pl.when(exists(shift_by))
        def _():
            pl.semaphore_signal(barrier, 1, device_id=(core, me + shift_by), device_id_type=MESH)

    pl.semaphore_wait(barrier, sum(jnp.where(exists(shift_by), 1, 0) for shift_by in OFFSETS))

    def describe(which, source, landing, shift_by):
        return pltpu.make_async_remote_copy(
            src_ref=source,
            dst_ref=out_refs[which].at[landing],
            send_sem=send_sems.at[which, landing],
            recv_sem=recv_sems.at[which, landing],
            device_id=(core, me + shift_by),
            device_id_type=MESH,
        )

    def arrival(which, landing):
        return describe(which, out_refs[which].at[landing], landing, OFFSETS[landing])

    direct = []
    relayed = []
    relaying = not any(spreads)
    for which, spread in enumerate(spreads):
        x_ref = payload_refs[which]
        targets = OFFSETS if spread or not relaying else [-1, 1]
        for shift_by in targets:
            source = x_ref.at[slot(shift_by)] if spread else x_ref
            copy = describe(which, source, slot(-shift_by), shift_by)
            direct.append((copy, exists(shift_by)))

            @pl.when(exists(shift_by))
            def _():
                copy.start()

        for shift_by in OFFSETS:

            @pl.when(jnp.logical_not(exists(shift_by)))
            def _():
                out_refs[which][slot(shift_by)] = jnp.zeros(
                    out_refs[which].shape[1:], out_refs[which].dtype
                )

        if relaying and not spread:
            for shift_by in (-1, 1):
                forward = describe(
                    which, out_refs[which].at[slot(-shift_by)], slot(-2 * shift_by), shift_by
                )
                relayed.append((which, shift_by, forward, exists(shift_by) & exists(-shift_by)))

    def relay():
        for which, shift_by, forward, valid in relayed:

            @pl.when(exists(-shift_by))
            def _():
                arrival(which, slot(-shift_by)).wait_recv()

        for which, shift_by, forward, valid in relayed:

            @pl.when(valid)
            def _():
                forward.start()

    def finish():
        for copy, valid in direct:

            @pl.when(valid)
            def _():
                copy.wait_send()

        for which, shift_by, forward, valid in relayed:

            @pl.when(valid)
            def _():
                forward.wait_send()

        relayed_slots = {(which, slot(-shift_by)) for which, shift_by, _, _ in relayed}
        for which in range(len(spreads)):
            for landing, shift_by in enumerate(OFFSETS):
                if (which, landing) in relayed_slots:
                    continue

                @pl.when(exists(shift_by))
                def _():
                    arrival(which, landing).wait_recv()

    return relay, finish


def fused_kernel(spreads, with_attention, *refs):
    count = len(spreads)
    inputs = 4 if with_attention else 0
    outputs = 3 if with_attention else 0
    attention_in = refs[:inputs]
    payload_refs = refs[inputs : inputs + count]
    attention_out = refs[inputs + count : inputs + count + outputs]
    out_refs = refs[inputs + count + outputs : inputs + 2 * count + outputs]
    send_sems, recv_sems = refs[inputs + 2 * count + outputs :]
    relay, finish = exchange_start(spreads, payload_refs, out_refs, send_sems, recv_sems)
    if with_attention:
        attention_body(*attention_in, *attention_out, relay)
    else:
        relay()
    finish()


def fused_step(attention_args, payloads, spreads, collective_id):
    vmem = pl.BlockSpec(memory_space=pltpu.VMEM)
    out_shapes = []
    flops = 0
    if attention_args:
        queries, key_rows, value_rows, grad_attn = attention_args
        rows, width = queries.shape
        keys = key_rows.shape[0]
        out_shapes = [
            jax.ShapeDtypeStruct((rows, width), jnp.float32),
            jax.ShapeDtypeStruct((keys, width), jnp.float32),
            jax.ShapeDtypeStruct((keys, width), jnp.float32),
        ]
        flops = 2 * 5 * rows * keys * width * (128 // HD)
    for payload, spread in zip(payloads, spreads):
        shape = payload.shape[1:] if spread else payload.shape
        out_shapes.append(jax.ShapeDtypeStruct((len(OFFSETS),) + shape, payload.dtype))
    moved = sum(len(OFFSETS) * x.size * x.dtype.itemsize for x in payloads)
    outs = pl.pallas_call(
        functools.partial(fused_kernel, tuple(spreads), bool(attention_args)),
        out_shape=out_shapes,
        in_specs=[vmem] * (len(attention_args) + len(payloads)),
        out_specs=[vmem] * len(out_shapes),
        scratch_shapes=[
            pltpu.SemaphoreType.DMA((len(payloads), len(OFFSETS))),
            pltpu.SemaphoreType.DMA((len(payloads), len(OFFSETS))),
        ],
        compiler_params=pltpu.CompilerParams(
            collective_id=collective_id,
            has_side_effects=True,
            vmem_limit_bytes=48 * 1024 * 1024,
        ),
        cost_estimate=pl.CostEstimate(
            flops=flops, transcendentals=flops // 160, bytes_accessed=moved + 1
        ),
    )(*attention_args, *payloads)
    return list(outs)


def swap_cores(value):
    return lax.ppermute(value, "pipe", [(0, 1), (1, 0)])


def pick(own, other, core, section):
    return jnp.where(core == section, own, other)


def prepare(rows, lists, weight_in, gain_row, myself):
    points, model_width = rows.shape
    block_count = points // BLK
    scaled, inverse, normed = normalize(rows, gain_row)
    projected = jnp.dot(normed, weight_in, preferred_element_type=jnp.float32).astype(jnp.bfloat16)
    owners = lists // block_count
    within = lists % block_count
    distance = owners - myself
    slot = jnp.where(distance < 0, distance + REACH, distance + REACH - 1)
    window_at = slot * block_count + within
    return dict(
        scaled=scaled,
        inverse=inverse,
        normed=normed,
        queries=projected[:, :model_width],
        own_pairs=projected[:, model_width:],
        window_at=window_at,
    )


def attach(unit, received, weight_in):
    points, model_width = unit["queries"].shape
    received = received.reshape(len(OFFSETS) * (points // BLK), BLK, model_width)
    fetched = jnp.take(received, unit["window_at"], axis=0).reshape(-1, model_width)
    fetched_pairs = jnp.dot(
        fetched, weight_in[:, model_width:], preferred_element_type=jnp.float32
    ).astype(jnp.bfloat16)
    unit["pairs"] = jnp.concatenate([unit["own_pairs"], fetched_pairs], 0)


def outgoing(unit, grad_key, grad_value, weight_in):
    points, model_width = unit["queries"].shape
    block_count = points // BLK
    grad_pairs = jnp.concatenate([grad_key, grad_value], 1)
    grad_remote = jnp.dot(
        grad_pairs[points:].astype(jnp.bfloat16),
        weight_in[:, model_width:].T,
        preferred_element_type=jnp.float32,
    ).reshape(-1, BLK, model_width)
    slots = lax.broadcasted_iota(jnp.int32, (len(OFFSETS) * block_count, 1, 1), 0)
    window_grads = sum(
        jnp.where(slots == unit["window_at"][entry], grad_remote[entry][None], 0.0)
        for entry in range(grad_remote.shape[0])
    )
    unit["own_grad"] = grad_pairs[:points]
    return window_grads.astype(jnp.bfloat16).reshape(len(OFFSETS), points, model_width)


def complete(unit, grad_out, grad_query, returned, weight_in, gain_row):
    grad_project = jnp.concatenate([grad_query, unit["own_grad"]], 1).astype(jnp.bfloat16)
    grad_normed = jnp.dot(grad_project, weight_in.T, preferred_element_type=jnp.float32)
    grad_normed = grad_normed + jnp.sum(returned.astype(jnp.float32), axis=0)
    return (
        grad_out.astype(jnp.float32)
        + norm_backward(grad_normed, unit["scaled"], unit["inverse"], gain_row)
    ).astype(jnp.bfloat16)


def shards(saved_inputs, project_in, project_out, norm_gains, neighbour_blocks, cotangent):
    sections = lax.axis_size("pipe")
    core = lax.axis_index("pipe")
    other = sections - 1 - core
    myself = lax.axis_index("space")
    micro_count = cotangent.shape[0]
    half = micro_count // sections
    model_width = cotangent.shape[2]

    def mine(array, whose):
        grouped = array.reshape((half, sections) + array.shape[1:])
        return lax.dynamic_index_in_dim(grouped, whose, 1, keepdims=False)

    local_lists = neighbour_blocks[0, :, 0, :]
    own = (
        mine(saved_inputs[0], core),
        mine(local_lists, core),
        project_in[0],
        project_out[0],
        norm_gains[0],
    )
    got = swap_cores(
        (
            mine(saved_inputs[0], other),
            mine(local_lists, other),
            project_in[0],
            project_out[0],
            norm_gains[0],
        )
    )
    params = [
        [pick(own_part, got_part, core, section) for own_part, got_part in zip(own, got)]
        for section in range(sections)
    ]
    cotangent_mine = mine(cotangent, core)
    order = [(section, j) for section in range(sections - 1, -1, -1) for j in range(half)]
    units = [
        prepare(params[section][0][j], params[section][1][j], params[section][2], params[section][4], myself)
        for section, j in order
    ]
    results = {}
    exchanged = {}
    ids = iter(range(len(order) + 2))
    (first_received,) = fused_step((), [units[0]["normed"]], [False], next(ids))
    attach(units[0], first_received, params[order[0][0]][2])
    pending = None
    for step, (section, j) in enumerate(order):
        unit = units[step]
        _, _, weight_in, weight_out, gain_row = params[section]
        grad_out = cotangent_mine[j] if section == sections - 1 else results[(section + 1, j)]
        unit["grad_out"] = grad_out
        grad_attn = jnp.dot(grad_out, weight_out.T, preferred_element_type=jnp.float32).astype(
            jnp.bfloat16
        )
        payloads, spreads = [], []
        if pending is not None:
            payloads.append(pending[1])
            spreads.append(True)
        if step == 0:
            for later in units[1:]:
                payloads.append(later["normed"])
                spreads.append(False)
        outs = fused_step(
            (unit["queries"], unit["pairs"][:, :model_width], unit["pairs"][:, model_width:], grad_attn),
            payloads,
            spreads,
            next(ids),
        )
        grad_query, grad_key, grad_value = outs[:3]
        received = outs[3:]
        if pending is not None:
            done_step, _ = pending
            done_section, done_j = order[done_step]
            done_unit = units[done_step]
            results[(done_section, done_j)] = complete(
                done_unit,
                done_unit["grad_out"],
                done_unit["grad_query"],
                received[0],
                params[done_section][2],
                params[done_section][4],
            )
            exchanged[(done_section, done_j)] = swap_cores(results[(done_section, done_j)])
            received = received[1:]
        if step == 0:
            for later, (later_section, _), arrived in zip(units[1:], order[1:], received):
                attach(later, arrived, params[later_section][2])
        unit["grad_query"] = grad_query
        pending = (step, outgoing(unit, grad_key, grad_value, weight_in))
    done_step, window = pending
    done_section, done_j = order[done_step]
    done_unit = units[done_step]
    (returned,) = fused_step((), [window], [True], next(ids))
    results[(done_section, done_j)] = complete(
        done_unit,
        done_unit["grad_out"],
        done_unit["grad_query"],
        returned,
        params[done_section][2],
        params[done_section][4],
    )
    exchanged[(done_section, done_j)] = swap_cores(results[(done_section, done_j)])
    own_out = jnp.stack([pick(results[(0, j)], results[(1, j)], core, 0) for j in range(half)])
    other_out = jnp.stack(
        [pick(exchanged[(0, j)], exchanged[(1, j)], core, 0) for j in range(half)]
    )
    grouped = jnp.stack([pick(own_out, other_out, core, parity) for parity in range(sections)], 1)
    return grouped.reshape((1, micro_count) + grouped.shape[2:])


def solution(mesh):
    return jax.shard_map(
        shards,
        mesh=mesh,
        in_specs=(
            P("pipe", None, "space", None),
            P("pipe", None, None),
            P("pipe", None, None),
            P("pipe", None),
            P("pipe", None, "space", None),
            P(None, "space", None),
        ),
        out_specs=P("pipe", None, "space", None),
        check_vma=False,
    )
```

```python
import functools

import jax
import jax.numpy as jnp
from jax import lax
from jax.experimental import pallas as pl
from jax.experimental.pallas import tpu as pltpu
from jax.sharding import PartitionSpec as P

HEADS = 32
HD = 16
BLK = 128
REACH = 2


epsilon = 1e-05


def shifted(x, axis, by):
    peers = lax.axis_size(axis)
    pairs = [(i, i + by) for i in range(peers) if 0 <= i + by < peers]
    return lax.ppermute(x, axis, pairs)


def normalize(points, gain_row):
    values = points.astype(jnp.float32)
    centre = jnp.mean(values, axis=-1, keepdims=True)
    spread = jnp.mean(jnp.square(values - centre), axis=-1, keepdims=True)
    inverse = lax.rsqrt(spread + epsilon)
    scaled = (values - centre) * inverse
    return (scaled, inverse, (scaled * gain_row).astype(jnp.bfloat16))


def norm_backward(grad_normed, scaled, inverse, gain_row):
    weighted = grad_normed * gain_row
    return inverse * (
        weighted
        - jnp.mean(weighted, axis=-1, keepdims=True)
        - scaled * jnp.mean(weighted * scaled, axis=-1, keepdims=True)
    )


MESH = pl.DeviceIdType.MESH
OFFSETS = [shift_by for shift_by in range(-REACH, REACH + 1) if shift_by != 0]


def attention_body(q_ref, k_ref, v_ref, g_ref, dq_ref, dk_ref, dv_ref, after_first):
    factor = HD ** (-0.5)
    group = 128
    nt = (((1,), (1,)), ((), ()))
    tn = (((0,), (0,)), ((), ()))
    head_of = lax.broadcasted_iota(jnp.int32, (1, group), 1) // HD
    dq_ref[...] = jnp.zeros_like(dq_ref)
    dk_ref[...] = jnp.zeros_like(dk_ref)
    dv_ref[...] = jnp.zeros_like(dv_ref)
    for first in range(0, q_ref.shape[1], group):
        cols = slice(first, first + group)
        q = q_ref[:, cols]
        k = k_ref[:, cols]
        v = v_ref[:, cols]
        g = g_ref[:, cols]

        def head(h, carry, q=q, k=k, v=v, g=g, cols=cols):
            mask = head_of == h
            qm = jnp.where(mask, q, jnp.zeros_like(q))
            km = jnp.where(mask, k, jnp.zeros_like(k))
            gm = jnp.where(mask, g, jnp.zeros_like(g))
            scores = lax.dot_general(qm, k, nt, preferred_element_type=jnp.float32) * factor
            top = jnp.max(scores, axis=-1, keepdims=True)
            exps = jnp.exp(scores - top)
            attention = exps * (1.0 / jnp.sum(exps, axis=-1, keepdims=True))
            grad_probs = lax.dot_general(gm, v, nt, preferred_element_type=jnp.float32)
            row = jnp.sum(attention * grad_probs, axis=-1, keepdims=True)
            grad_scores = (attention * (grad_probs - row) * factor).astype(jnp.bfloat16)
            dq_ref[:, cols] += jnp.dot(grad_scores, km, preferred_element_type=jnp.float32)
            dk_ref[:, cols] += lax.dot_general(
                grad_scores, qm, tn, preferred_element_type=jnp.float32
            )
            dv_ref[:, cols] += lax.dot_general(
                attention.astype(jnp.bfloat16), gm, tn, preferred_element_type=jnp.float32
            )
            return carry

        lax.fori_loop(0, group // HD, head, 0)
        if first == group:
            after_first()


def exchange_start(spreads, payload_refs, out_refs, send_sems, recv_sems):
    core = lax.axis_index("pipe")
    me = lax.axis_index("space")
    peers = lax.axis_size("space")
    barrier = pltpu.get_barrier_semaphore()

    def exists(shift_by):
        return (me + shift_by >= 0) & (me + shift_by < peers)

    def slot(shift_by):
        return OFFSETS.index(shift_by)

    for shift_by in OFFSETS:

        @pl.when(exists(shift_by))
        def _():
            pl.semaphore_signal(barrier, 1, device_id=(core, me + shift_by), device_id_type=MESH)

    pl.semaphore_wait(barrier, sum(jnp.where(exists(shift_by), 1, 0) for shift_by in OFFSETS))

    def describe(which, source, landing, shift_by):
        return pltpu.make_async_remote_copy(
            src_ref=source,
            dst_ref=out_refs[which].at[landing],
            send_sem=send_sems.at[which, landing],
            recv_sem=recv_sems.at[which, landing],
            device_id=(core, me + shift_by),
            device_id_type=MESH,
        )

    def arrival(which, landing):
        return describe(which, out_refs[which].at[landing], landing, OFFSETS[landing])

    direct = []
    relayed = []
    relaying = not any(spreads)
    for which, spread in enumerate(spreads):
        x_ref = payload_refs[which]
        targets = OFFSETS if spread or not relaying else [-1, 1]
        for shift_by in targets:
            source = x_ref.at[slot(shift_by)] if spread else x_ref
            copy = describe(which, source, slot(-shift_by), shift_by)
            direct.append((copy, exists(shift_by)))

            @pl.when(exists(shift_by))
            def _():
                copy.start()

        for shift_by in OFFSETS:

            @pl.when(jnp.logical_not(exists(shift_by)))
            def _():
                out_refs[which][slot(shift_by)] = jnp.zeros(
                    out_refs[which].shape[1:], out_refs[which].dtype
                )

        if relaying and not spread:
            for shift_by in (-1, 1):
                forward = describe(
                    which, out_refs[which].at[slot(-shift_by)], slot(-2 * shift_by), shift_by
                )
                relayed.append((which, shift_by, forward, exists(shift_by) & exists(-shift_by)))

    def relay():
        for which, shift_by, forward, valid in relayed:

            @pl.when(exists(-shift_by))
            def _():
                arrival(which, slot(-shift_by)).wait_recv()

        for which, shift_by, forward, valid in relayed:

            @pl.when(valid)
            def _():
                forward.start()

    def finish():
        for copy, valid in direct:

            @pl.when(valid)
            def _():
                copy.wait_send()

        for which, shift_by, forward, valid in relayed:

            @pl.when(valid)
            def _():
                forward.wait_send()

        relayed_slots = {(which, slot(-shift_by)) for which, shift_by, _, _ in relayed}
        for which in range(len(spreads)):
            for landing, shift_by in enumerate(OFFSETS):
                if (which, landing) in relayed_slots:
                    continue

                @pl.when(exists(shift_by))
                def _():
                    arrival(which, landing).wait_recv()

    return relay, finish


def fused_kernel(spreads, with_attention, *refs):
    count = len(spreads)
    inputs = 4 if with_attention else 0
    outputs = 3 if with_attention else 0
    attention_in = refs[:inputs]
    payload_refs = refs[inputs : inputs + count]
    attention_out = refs[inputs + count : inputs + count + outputs]
    out_refs = refs[inputs + count + outputs : inputs + 2 * count + outputs]
    send_sems, recv_sems = refs[inputs + 2 * count + outputs :]
    relay, finish = exchange_start(spreads, payload_refs, out_refs, send_sems, recv_sems)
    if with_attention:
        attention_body(*attention_in, *attention_out, relay)
    else:
        relay()
    finish()


def fused_step(attention_args, payloads, spreads, collective_id):
    vmem = pl.BlockSpec(memory_space=pltpu.VMEM)
    out_shapes = []
    flops = 0
    if attention_args:
        queries, key_rows, value_rows, grad_attn = attention_args
        rows, width = queries.shape
        keys = key_rows.shape[0]
        out_shapes = [
            jax.ShapeDtypeStruct((rows, width), jnp.float32),
            jax.ShapeDtypeStruct((keys, width), jnp.float32),
            jax.ShapeDtypeStruct((keys, width), jnp.float32),
        ]
        flops = 2 * 5 * rows * keys * width * (128 // HD)
    for payload, spread in zip(payloads, spreads):
        shape = payload.shape[1:] if spread else payload.shape
        out_shapes.append(jax.ShapeDtypeStruct((len(OFFSETS),) + shape, payload.dtype))
    moved = sum(len(OFFSETS) * x.size * x.dtype.itemsize for x in payloads)
    outs = pl.pallas_call(
        functools.partial(fused_kernel, tuple(spreads), bool(attention_args)),
        out_shape=out_shapes,
        in_specs=[vmem] * (len(attention_args) + len(payloads)),
        out_specs=[vmem] * len(out_shapes),
        scratch_shapes=[
            pltpu.SemaphoreType.DMA((len(payloads), len(OFFSETS))),
            pltpu.SemaphoreType.DMA((len(payloads), len(OFFSETS))),
        ],
        compiler_params=pltpu.CompilerParams(
            collective_id=collective_id,
            has_side_effects=True,
            vmem_limit_bytes=48 * 1024 * 1024,
        ),
        cost_estimate=pl.CostEstimate(
            flops=flops, transcendentals=flops // 160, bytes_accessed=moved + 1
        ),
    )(*attention_args, *payloads)
    return list(outs)


def swap_cores(value):
    return lax.ppermute(value, "pipe", [(0, 1), (1, 0)])


def pick(own, other, core, section):
    return jnp.where(core == section, own, other)


def prepare(rows, lists, weight_in, gain_row, myself):
    points, model_width = rows.shape
    block_count = points // BLK
    scaled, inverse, normed = normalize(rows, gain_row)
    projected = jnp.dot(normed, weight_in, preferred_element_type=jnp.float32).astype(jnp.bfloat16)
    owners = lists // block_count
    within = lists % block_count
    distance = owners - myself
    slot = jnp.where(distance < 0, distance + REACH, distance + REACH - 1)
    window_at = slot * block_count + within
    return dict(
        scaled=scaled,
        inverse=inverse,
        normed=normed,
        queries=projected[:, :model_width],
        own_pairs=projected[:, model_width:],
        window_at=window_at,
    )


def attach(unit, received, weight_in):
    points, model_width = unit["queries"].shape
    received = received.reshape(len(OFFSETS) * (points // BLK), BLK, model_width)
    fetched = jnp.take(received, unit["window_at"], axis=0).reshape(-1, model_width)
    fetched_pairs = jnp.dot(
        fetched, weight_in[:, model_width:], preferred_element_type=jnp.float32
    ).astype(jnp.bfloat16)
    unit["pairs"] = jnp.concatenate([unit["own_pairs"], fetched_pairs], 0)


def outgoing(unit, grad_key, grad_value, weight_in):
    points, model_width = unit["queries"].shape
    block_count = points // BLK
    grad_pairs = jnp.concatenate([grad_key, grad_value], 1)
    grad_remote = jnp.dot(
        grad_pairs[points:].astype(jnp.bfloat16),
        weight_in[:, model_width:].T,
        preferred_element_type=jnp.float32,
    ).reshape(-1, BLK, model_width)
    slots = lax.broadcasted_iota(jnp.int32, (len(OFFSETS) * block_count, 1, 1), 0)
    window_grads = sum(
        jnp.where(slots == unit["window_at"][entry], grad_remote[entry][None], 0.0)
        for entry in range(grad_remote.shape[0])
    )
    unit["own_grad"] = grad_pairs[:points]
    return window_grads.astype(jnp.bfloat16).reshape(len(OFFSETS), points, model_width)


def complete(unit, grad_out, grad_query, returned, weight_in, gain_row):
    grad_project = jnp.concatenate([grad_query, unit["own_grad"]], 1).astype(jnp.bfloat16)
    grad_normed = jnp.dot(grad_project, weight_in.T, preferred_element_type=jnp.float32)
    grad_normed = grad_normed + jnp.sum(returned.astype(jnp.float32), axis=0)
    return (
        grad_out.astype(jnp.float32)
        + norm_backward(grad_normed, unit["scaled"], unit["inverse"], gain_row)
    ).astype(jnp.bfloat16)


def shards(saved_inputs, project_in, project_out, norm_gains, neighbour_blocks, cotangent):
    sections = lax.axis_size("pipe")
    core = lax.axis_index("pipe")
    other = sections - 1 - core
    myself = lax.axis_index("space")
    micro_count = cotangent.shape[0]
    half = micro_count // sections
    model_width = cotangent.shape[2]

    def mine(array, whose):
        grouped = array.reshape((half, sections) + array.shape[1:])
        return lax.dynamic_index_in_dim(grouped, whose, 1, keepdims=False)

    local_lists = neighbour_blocks[0, :, 0, :]
    own = (
        mine(saved_inputs[0], core),
        mine(local_lists, core),
        project_in[0],
        project_out[0],
        norm_gains[0],
    )
    got = swap_cores(
        (
            mine(saved_inputs[0], other),
            mine(local_lists, other),
            project_in[0],
            project_out[0],
            norm_gains[0],
        )
    )
    params = [
        [pick(own_part, got_part, core, section) for own_part, got_part in zip(own, got)]
        for section in range(sections)
    ]
    cotangent_mine = mine(cotangent, core)
    order = [(section, j) for section in range(sections - 1, -1, -1) for j in range(half)]
    units = [
        prepare(params[section][0][j], params[section][1][j], params[section][2], params[section][4], myself)
        for section, j in order
    ]
    results = {}
    exchanged = {}
    ids = iter(range(len(order) + 2))
    (first_received,) = fused_step((), [units[0]["normed"]], [False], next(ids))
    attach(units[0], first_received, params[order[0][0]][2])
    pending = None
    for step, (section, j) in enumerate(order):
        unit = units[step]
        _, _, weight_in, weight_out, gain_row = params[section]
        grad_out = cotangent_mine[j] if section == sections - 1 else results[(section + 1, j)]
        unit["grad_out"] = grad_out
        grad_attn = jnp.dot(grad_out, weight_out.T, preferred_element_type=jnp.float32).astype(
            jnp.bfloat16
        )
        payloads, spreads = [], []
        if pending is not None:
            payloads.append(pending[1])
            spreads.append(True)
        if step == 0:
            for later in units[1:]:
                payloads.append(later["normed"])
                spreads.append(False)
        outs = fused_step(
            (unit["queries"], unit["pairs"][:, :model_width], unit["pairs"][:, model_width:], grad_attn),
            payloads,
            spreads,
            next(ids),
        )
        grad_query, grad_key, grad_value = outs[:3]
        received = outs[3:]
        if pending is not None:
            done_step, _ = pending
            done_section, done_j = order[done_step]
            done_unit = units[done_step]
            results[(done_section, done_j)] = complete(
                done_unit,
                done_unit["grad_out"],
                done_unit["grad_query"],
                received[0],
                params[done_section][2],
                params[done_section][4],
            )
            exchanged[(done_section, done_j)] = swap_cores(results[(done_section, done_j)])
            received = received[1:]
        if step == 0:
            for later, (later_section, _), arrived in zip(units[1:], order[1:], received):
                attach(later, arrived, params[later_section][2])
        unit["grad_query"] = grad_query
        pending = (step, outgoing(unit, grad_key, grad_value, weight_in))
    done_step, window = pending
    done_section, done_j = order[done_step]
    done_unit = units[done_step]
    (returned,) = fused_step((), [window], [True], next(ids))
    results[(done_section, done_j)] = complete(
        done_unit,
        done_unit["grad_out"],
        done_unit["grad_query"],
        returned,
        params[done_section][2],
        params[done_section][4],
    )
    exchanged[(done_section, done_j)] = swap_cores(results[(done_section, done_j)])
    own_out = jnp.stack([pick(results[(0, j)], results[(1, j)], core, 0) for j in range(half)])
    other_out = jnp.stack(
        [pick(exchanged[(0, j)], exchanged[(1, j)], core, 0) for j in range(half)]
    )
    grouped = jnp.stack([pick(own_out, other_out, core, parity) for parity in range(sections)], 1)
    return grouped.reshape((1, micro_count) + grouped.shape[2:])


def solution(mesh):
    return jax.shard_map(
        shards,
        mesh=mesh,
        in_specs=(
            P("pipe", None, "space", None),
            P("pipe", None, None),
            P("pipe", None, None),
            P("pipe", None),
            P("pipe", None, "space", None),
            P(None, "space", None),
        ),
        out_specs=P("pipe", None, "space", None),
        check_vma=False,
    )
```

```python
import functools

import jax
import jax.numpy as jnp
from jax import lax
from jax.experimental import pallas as pl
from jax.experimental.pallas import tpu as pltpu
from jax.sharding import PartitionSpec as P

HEADS = 32
HD = 16
BLK = 128
REACH = 2


epsilon = 1e-05


def shifted(x, axis, by):
    peers = lax.axis_size(axis)
    pairs = [(i, i + by) for i in range(peers) if 0 <= i + by < peers]
    return lax.ppermute(x, axis, pairs)


def normalize(points, gain_row):
    values = points.astype(jnp.float32)
    centre = jnp.mean(values, axis=-1, keepdims=True)
    spread = jnp.mean(jnp.square(values - centre), axis=-1, keepdims=True)
    inverse = lax.rsqrt(spread + epsilon)
    scaled = (values - centre) * inverse
    return (scaled, inverse, (scaled * gain_row).astype(jnp.bfloat16))


def norm_backward(grad_normed, scaled, inverse, gain_row):
    weighted = grad_normed * gain_row
    return inverse * (
        weighted
        - jnp.mean(weighted, axis=-1, keepdims=True)
        - scaled * jnp.mean(weighted * scaled, axis=-1, keepdims=True)
    )


MESH = pl.DeviceIdType.MESH
OFFSETS = [shift_by for shift_by in range(-REACH, REACH + 1) if shift_by != 0]


def attention_body(q_ref, k_ref, v_ref, g_ref, dq_ref, dk_ref, dv_ref, after_first):
    factor = HD ** (-0.5)
    group = 128
    nt = (((1,), (1,)), ((), ()))
    tn = (((0,), (0,)), ((), ()))
    head_of = lax.broadcasted_iota(jnp.int32, (1, group), 1) // HD
    dq_ref[...] = jnp.zeros_like(dq_ref)
    dk_ref[...] = jnp.zeros_like(dk_ref)
    dv_ref[...] = jnp.zeros_like(dv_ref)
    for first in range(0, q_ref.shape[1], group):
        cols = slice(first, first + group)
        q = q_ref[:, cols]
        k = k_ref[:, cols]
        v = v_ref[:, cols]
        g = g_ref[:, cols]

        def head(h, carry, q=q, k=k, v=v, g=g, cols=cols):
            mask = head_of == h
            qm = jnp.where(mask, q, jnp.zeros_like(q))
            km = jnp.where(mask, k, jnp.zeros_like(k))
            gm = jnp.where(mask, g, jnp.zeros_like(g))
            scores = lax.dot_general(qm, k, nt, preferred_element_type=jnp.float32) * factor
            top = jnp.max(scores, axis=-1, keepdims=True)
            exps = jnp.exp(scores - top)
            attention = exps * (1.0 / jnp.sum(exps, axis=-1, keepdims=True))
            grad_probs = lax.dot_general(gm, v, nt, preferred_element_type=jnp.float32)
            row = jnp.sum(attention * grad_probs, axis=-1, keepdims=True)
            grad_scores = (attention * (grad_probs - row) * factor).astype(jnp.bfloat16)
            dq_ref[:, cols] += jnp.dot(grad_scores, km, preferred_element_type=jnp.float32)
            dk_ref[:, cols] += lax.dot_general(
                grad_scores, qm, tn, preferred_element_type=jnp.float32
            )
            dv_ref[:, cols] += lax.dot_general(
                attention.astype(jnp.bfloat16), gm, tn, preferred_element_type=jnp.float32
            )
            return carry

        lax.fori_loop(0, group // HD, head, 0, unroll=2)
        if first == group:
            after_first()


def exchange_start(spreads, payload_refs, out_refs, send_sems, recv_sems):
    core = lax.axis_index("pipe")
    me = lax.axis_index("space")
    peers = lax.axis_size("space")
    barrier = pltpu.get_barrier_semaphore()

    def exists(shift_by):
        return (me + shift_by >= 0) & (me + shift_by < peers)

    def slot(shift_by):
        return OFFSETS.index(shift_by)

    for shift_by in OFFSETS:

        @pl.when(exists(shift_by))
        def _():
            pl.semaphore_signal(barrier, 1, device_id=(core, me + shift_by), device_id_type=MESH)

    pl.semaphore_wait(barrier, sum(jnp.where(exists(shift_by), 1, 0) for shift_by in OFFSETS))

    def describe(which, source, landing, shift_by):
        return pltpu.make_async_remote_copy(
            src_ref=source,
            dst_ref=out_refs[which].at[landing],
            send_sem=send_sems.at[which, landing],
            recv_sem=recv_sems.at[which, landing],
            device_id=(core, me + shift_by),
            device_id_type=MESH,
        )

    def arrival(which, landing):
        return describe(which, out_refs[which].at[landing], landing, OFFSETS[landing])

    direct = []
    relayed = []
    relaying = not any(spreads)
    for which, spread in enumerate(spreads):
        x_ref = payload_refs[which]
        targets = OFFSETS if spread or not relaying else [-1, 1]
        for shift_by in targets:
            source = x_ref.at[slot(shift_by)] if spread else x_ref
            copy = describe(which, source, slot(-shift_by), shift_by)
            direct.append((copy, exists(shift_by)))

            @pl.when(exists(shift_by))
            def _():
                copy.start()

        for shift_by in OFFSETS:

            @pl.when(jnp.logical_not(exists(shift_by)))
            def _():
                out_refs[which][slot(shift_by)] = jnp.zeros(
                    out_refs[which].shape[1:], out_refs[which].dtype
                )

        if relaying and not spread:
            for shift_by in (-1, 1):
                forward = describe(
                    which, out_refs[which].at[slot(-shift_by)], slot(-2 * shift_by), shift_by
                )
                relayed.append((which, shift_by, forward, exists(shift_by) & exists(-shift_by)))

    def relay():
        for which, shift_by, forward, valid in relayed:

            @pl.when(exists(-shift_by))
            def _():
                arrival(which, slot(-shift_by)).wait_recv()

        for which, shift_by, forward, valid in relayed:

            @pl.when(valid)
            def _():
                forward.start()

    def finish():
        for copy, valid in direct:

            @pl.when(valid)
            def _():
                copy.wait_send()

        for which, shift_by, forward, valid in relayed:

            @pl.when(valid)
            def _():
                forward.wait_send()

        relayed_slots = {(which, slot(-shift_by)) for which, shift_by, _, _ in relayed}
        for which in range(len(spreads)):
            for landing, shift_by in enumerate(OFFSETS):
                if (which, landing) in relayed_slots:
                    continue

                @pl.when(exists(shift_by))
                def _():
                    arrival(which, landing).wait_recv()

    return relay, finish


def fused_kernel(spreads, with_attention, *refs):
    count = len(spreads)
    inputs = 4 if with_attention else 0
    outputs = 3 if with_attention else 0
    attention_in = refs[:inputs]
    payload_refs = refs[inputs : inputs + count]
    attention_out = refs[inputs + count : inputs + count + outputs]
    out_refs = refs[inputs + count + outputs : inputs + 2 * count + outputs]
    send_sems, recv_sems = refs[inputs + 2 * count + outputs :]
    relay, finish = exchange_start(spreads, payload_refs, out_refs, send_sems, recv_sems)
    if with_attention:
        attention_body(*attention_in, *attention_out, relay)
    else:
        relay()
    finish()


def fused_step(attention_args, payloads, spreads, collective_id):
    vmem = pl.BlockSpec(memory_space=pltpu.VMEM)
    out_shapes = []
    flops = 0
    if attention_args:
        queries, key_rows, value_rows, grad_attn = attention_args
        rows, width = queries.shape
        keys = key_rows.shape[0]
        out_shapes = [
            jax.ShapeDtypeStruct((rows, width), jnp.float32),
            jax.ShapeDtypeStruct((keys, width), jnp.float32),
            jax.ShapeDtypeStruct((keys, width), jnp.float32),
        ]
        flops = 2 * 5 * rows * keys * width * (128 // HD)
    for payload, spread in zip(payloads, spreads):
        shape = payload.shape[1:] if spread else payload.shape
        out_shapes.append(jax.ShapeDtypeStruct((len(OFFSETS),) + shape, payload.dtype))
    moved = sum(len(OFFSETS) * x.size * x.dtype.itemsize for x in payloads)
    outs = pl.pallas_call(
        functools.partial(fused_kernel, tuple(spreads), bool(attention_args)),
        out_shape=out_shapes,
        in_specs=[vmem] * (len(attention_args) + len(payloads)),
        out_specs=[vmem] * len(out_shapes),
        scratch_shapes=[
            pltpu.SemaphoreType.DMA((len(payloads), len(OFFSETS))),
            pltpu.SemaphoreType.DMA((len(payloads), len(OFFSETS))),
        ],
        compiler_params=pltpu.CompilerParams(
            collective_id=collective_id,
            has_side_effects=True,
            vmem_limit_bytes=48 * 1024 * 1024,
        ),
        cost_estimate=pl.CostEstimate(
            flops=flops, transcendentals=flops // 160, bytes_accessed=moved + 1
        ),
    )(*attention_args, *payloads)
    return list(outs)


def swap_cores(value):
    return lax.ppermute(value, "pipe", [(0, 1), (1, 0)])


def pick(own, other, core, section):
    return jnp.where(core == section, own, other)


def prepare(rows, lists, weight_in, gain_row, myself):
    points, model_width = rows.shape
    block_count = points // BLK
    scaled, inverse, normed = normalize(rows, gain_row)
    projected = jnp.dot(normed, weight_in, preferred_element_type=jnp.float32).astype(jnp.bfloat16)
    owners = lists // block_count
    within = lists % block_count
    distance = owners - myself
    slot = jnp.where(distance < 0, distance + REACH, distance + REACH - 1)
    window_at = slot * block_count + within
    return dict(
        scaled=scaled,
        inverse=inverse,
        normed=normed,
        queries=projected[:, :model_width],
        own_pairs=projected[:, model_width:],
        window_at=window_at,
    )


def attach(unit, received, weight_in):
    points, model_width = unit["queries"].shape
    received = received.reshape(len(OFFSETS) * (points // BLK), BLK, model_width)
    fetched = jnp.take(received, unit["window_at"], axis=0).reshape(-1, model_width)
    fetched_pairs = jnp.dot(
        fetched, weight_in[:, model_width:], preferred_element_type=jnp.float32
    ).astype(jnp.bfloat16)
    unit["pairs"] = jnp.concatenate([unit["own_pairs"], fetched_pairs], 0)


def outgoing(unit, grad_key, grad_value, weight_in):
    points, model_width = unit["queries"].shape
    block_count = points // BLK
    grad_pairs = jnp.concatenate([grad_key, grad_value], 1)
    grad_remote = jnp.dot(
        grad_pairs[points:].astype(jnp.bfloat16),
        weight_in[:, model_width:].T,
        preferred_element_type=jnp.float32,
    ).reshape(-1, BLK, model_width)
    slots = lax.broadcasted_iota(jnp.int32, (len(OFFSETS) * block_count, 1, 1), 0)
    window_grads = sum(
        jnp.where(slots == unit["window_at"][entry], grad_remote[entry][None], 0.0)
        for entry in range(grad_remote.shape[0])
    )
    unit["own_grad"] = grad_pairs[:points]
    return window_grads.astype(jnp.bfloat16).reshape(len(OFFSETS), points, model_width)


def complete(unit, grad_out, grad_query, returned, weight_in, gain_row):
    grad_project = jnp.concatenate([grad_query, unit["own_grad"]], 1).astype(jnp.bfloat16)
    grad_normed = jnp.dot(grad_project, weight_in.T, preferred_element_type=jnp.float32)
    grad_normed = grad_normed + jnp.sum(returned.astype(jnp.float32), axis=0)
    return (
        grad_out.astype(jnp.float32)
        + norm_backward(grad_normed, unit["scaled"], unit["inverse"], gain_row)
    ).astype(jnp.bfloat16)


def shards(saved_inputs, project_in, project_out, norm_gains, neighbour_blocks, cotangent):
    sections = lax.axis_size("pipe")
    core = lax.axis_index("pipe")
    other = sections - 1 - core
    myself = lax.axis_index("space")
    micro_count = cotangent.shape[0]
    half = micro_count // sections
    model_width = cotangent.shape[2]

    def mine(array, whose):
        grouped = array.reshape((half, sections) + array.shape[1:])
        return lax.dynamic_index_in_dim(grouped, whose, 1, keepdims=False)

    local_lists = neighbour_blocks[0, :, 0, :]
    own = (
        mine(saved_inputs[0], core),
        mine(local_lists, core),
        project_in[0],
        project_out[0],
        norm_gains[0],
    )
    got = swap_cores(
        (
            mine(saved_inputs[0], other),
            mine(local_lists, other),
            project_in[0],
            project_out[0],
            norm_gains[0],
        )
    )
    params = [
        [pick(own_part, got_part, core, section) for own_part, got_part in zip(own, got)]
        for section in range(sections)
    ]
    cotangent_mine = mine(cotangent, core)
    order = [(section, j) for section in range(sections - 1, -1, -1) for j in range(half)]
    units = [
        prepare(params[section][0][j], params[section][1][j], params[section][2], params[section][4], myself)
        for section, j in order
    ]
    results = {}
    exchanged = {}
    ids = iter(range(len(order) + 2))
    (first_received,) = fused_step((), [units[0]["normed"]], [False], next(ids))
    attach(units[0], first_received, params[order[0][0]][2])
    pending = None
    for step, (section, j) in enumerate(order):
        unit = units[step]
        _, _, weight_in, weight_out, gain_row = params[section]
        grad_out = cotangent_mine[j] if section == sections - 1 else results[(section + 1, j)]
        unit["grad_out"] = grad_out
        grad_attn = jnp.dot(grad_out, weight_out.T, preferred_element_type=jnp.float32).astype(
            jnp.bfloat16
        )
        payloads, spreads = [], []
        if pending is not None:
            payloads.append(pending[1])
            spreads.append(True)
        if step == 0:
            for later in units[1:]:
                payloads.append(later["normed"])
                spreads.append(False)
        outs = fused_step(
            (unit["queries"], unit["pairs"][:, :model_width], unit["pairs"][:, model_width:], grad_attn),
            payloads,
            spreads,
            next(ids),
        )
        grad_query, grad_key, grad_value = outs[:3]
        received = outs[3:]
        if pending is not None:
            done_step, _ = pending
            done_section, done_j = order[done_step]
            done_unit = units[done_step]
            results[(done_section, done_j)] = complete(
                done_unit,
                done_unit["grad_out"],
                done_unit["grad_query"],
                received[0],
                params[done_section][2],
                params[done_section][4],
            )
            exchanged[(done_section, done_j)] = swap_cores(results[(done_section, done_j)])
            received = received[1:]
        if step == 0:
            for later, (later_section, _), arrived in zip(units[1:], order[1:], received):
                attach(later, arrived, params[later_section][2])
        unit["grad_query"] = grad_query
        pending = (step, outgoing(unit, grad_key, grad_value, weight_in))
    done_step, window = pending
    done_section, done_j = order[done_step]
    done_unit = units[done_step]
    (returned,) = fused_step((), [window], [True], next(ids))
    results[(done_section, done_j)] = complete(
        done_unit,
        done_unit["grad_out"],
        done_unit["grad_query"],
        returned,
        params[done_section][2],
        params[done_section][4],
    )
    exchanged[(done_section, done_j)] = swap_cores(results[(done_section, done_j)])
    own_out = jnp.stack([pick(results[(0, j)], results[(1, j)], core, 0) for j in range(half)])
    other_out = jnp.stack(
        [pick(exchanged[(0, j)], exchanged[(1, j)], core, 0) for j in range(half)]
    )
    grouped = jnp.stack([pick(own_out, other_out, core, parity) for parity in range(sections)], 1)
    return grouped.reshape((1, micro_count) + grouped.shape[2:])


def solution(mesh):
    return jax.shard_map(
        shards,
        mesh=mesh,
        in_specs=(
            P("pipe", None, "space", None),
            P("pipe", None, None),
            P("pipe", None, None),
            P("pipe", None),
            P("pipe", None, "space", None),
            P(None, "space", None),
        ),
        out_specs=P("pipe", None, "space", None),
        check_vma=False,
    )
```

```python
import functools

import jax
import jax.numpy as jnp
from jax import lax
from jax.experimental import pallas as pl
from jax.experimental.pallas import tpu as pltpu
from jax.sharding import PartitionSpec as P

HEADS = 32
HD = 16
BLK = 128
REACH = 2


epsilon = 1e-05


def shifted(x, axis, by):
    peers = lax.axis_size(axis)
    pairs = [(i, i + by) for i in range(peers) if 0 <= i + by < peers]
    return lax.ppermute(x, axis, pairs)


def normalize(points, gain_row):
    values = points.astype(jnp.float32)
    centre = jnp.mean(values, axis=-1, keepdims=True)
    spread = jnp.mean(jnp.square(values - centre), axis=-1, keepdims=True)
    inverse = lax.rsqrt(spread + epsilon)
    scaled = (values - centre) * inverse
    return (scaled, inverse, (scaled * gain_row).astype(jnp.bfloat16))


def norm_backward(grad_normed, scaled, inverse, gain_row):
    weighted = grad_normed * gain_row
    return inverse * (
        weighted
        - jnp.mean(weighted, axis=-1, keepdims=True)
        - scaled * jnp.mean(weighted * scaled, axis=-1, keepdims=True)
    )


MESH = pl.DeviceIdType.MESH
OFFSETS = [shift_by for shift_by in range(-REACH, REACH + 1) if shift_by != 0]


def attention_body(q_ref, k_ref, v_ref, g_ref, dq_ref, dk_ref, dv_ref, after_first):
    factor = HD ** (-0.5)
    group = 128
    per_group = group // HD
    nt = (((1,), (1,)), ((), ()))
    tn = (((0,), (0,)), ((), ()))
    head_of = lax.broadcasted_iota(jnp.int32, (1, group), 1) // HD
    dq_ref[...] = jnp.zeros_like(dq_ref)
    dk_ref[...] = jnp.zeros_like(dk_ref)
    dv_ref[...] = jnp.zeros_like(dv_ref)

    def head(index, carry):
        cols = pl.ds(pl.multiple_of((index // per_group) * group, group), group)
        mask = head_of == index % per_group
        q = q_ref[:, cols]
        k = k_ref[:, cols]
        v = v_ref[:, cols]
        g = g_ref[:, cols]
        qm = jnp.where(mask, q, jnp.zeros_like(q))
        km = jnp.where(mask, k, jnp.zeros_like(k))
        gm = jnp.where(mask, g, jnp.zeros_like(g))
        scores = lax.dot_general(qm, k, nt, preferred_element_type=jnp.float32) * factor
        top = jnp.max(scores, axis=-1, keepdims=True)
        exps = jnp.exp(scores - top)
        attention = exps * (1.0 / jnp.sum(exps, axis=-1, keepdims=True))
        grad_probs = lax.dot_general(gm, v, nt, preferred_element_type=jnp.float32)
        row = jnp.sum(attention * grad_probs, axis=-1, keepdims=True)
        grad_scores = (attention * (grad_probs - row) * factor).astype(jnp.bfloat16)
        dq_ref[:, cols] += jnp.dot(grad_scores, km, preferred_element_type=jnp.float32)
        dk_ref[:, cols] += lax.dot_general(grad_scores, qm, tn, preferred_element_type=jnp.float32)
        dv_ref[:, cols] += lax.dot_general(
            attention.astype(jnp.bfloat16), gm, tn, preferred_element_type=jnp.float32
        )
        return carry

    heads = q_ref.shape[1] // HD
    split = min(heads, 2 * per_group)
    lax.fori_loop(0, split, head, 0, unroll=2)
    after_first()
    lax.fori_loop(split, heads, head, 0, unroll=2)


def exchange_start(spreads, payload_refs, out_refs, send_sems, recv_sems):
    core = lax.axis_index("pipe")
    me = lax.axis_index("space")
    peers = lax.axis_size("space")
    barrier = pltpu.get_barrier_semaphore()

    def exists(shift_by):
        return (me + shift_by >= 0) & (me + shift_by < peers)

    def slot(shift_by):
        return OFFSETS.index(shift_by)

    for shift_by in OFFSETS:

        @pl.when(exists(shift_by))
        def _():
            pl.semaphore_signal(barrier, 1, device_id=(core, me + shift_by), device_id_type=MESH)

    pl.semaphore_wait(barrier, sum(jnp.where(exists(shift_by), 1, 0) for shift_by in OFFSETS))

    def describe(which, source, landing, shift_by):
        return pltpu.make_async_remote_copy(
            src_ref=source,
            dst_ref=out_refs[which].at[landing],
            send_sem=send_sems.at[which, landing],
            recv_sem=recv_sems.at[which, landing],
            device_id=(core, me + shift_by),
            device_id_type=MESH,
        )

    def arrival(which, landing):
        return describe(which, out_refs[which].at[landing], landing, OFFSETS[landing])

    direct = []
    relayed = []
    relaying = not any(spreads)
    for which, spread in enumerate(spreads):
        x_ref = payload_refs[which]
        targets = OFFSETS if spread or not relaying else [-1, 1]
        for shift_by in targets:
            source = x_ref.at[slot(shift_by)] if spread else x_ref
            copy = describe(which, source, slot(-shift_by), shift_by)
            direct.append((copy, exists(shift_by)))

            @pl.when(exists(shift_by))
            def _():
                copy.start()

        for shift_by in OFFSETS:

            @pl.when(jnp.logical_not(exists(shift_by)))
            def _():
                out_refs[which][slot(shift_by)] = jnp.zeros(
                    out_refs[which].shape[1:], out_refs[which].dtype
                )

        if relaying and not spread:
            for shift_by in (-1, 1):
                forward = describe(
                    which, out_refs[which].at[slot(-shift_by)], slot(-2 * shift_by), shift_by
                )
                relayed.append((which, shift_by, forward, exists(shift_by) & exists(-shift_by)))

    def relay():
        for which, shift_by, forward, valid in relayed:

            @pl.when(exists(-shift_by))
            def _():
                arrival(which, slot(-shift_by)).wait_recv()

        for which, shift_by, forward, valid in relayed:

            @pl.when(valid)
            def _():
                forward.start()

    def finish():
        for copy, valid in direct:

            @pl.when(valid)
            def _():
                copy.wait_send()

        for which, shift_by, forward, valid in relayed:

            @pl.when(valid)
            def _():
                forward.wait_send()

        relayed_slots = {(which, slot(-shift_by)) for which, shift_by, _, _ in relayed}
        for which in range(len(spreads)):
            for landing, shift_by in enumerate(OFFSETS):
                if (which, landing) in relayed_slots:
                    continue

                @pl.when(exists(shift_by))
                def _():
                    arrival(which, landing).wait_recv()

    return relay, finish


def fused_kernel(spreads, with_attention, *refs):
    count = len(spreads)
    inputs = 4 if with_attention else 0
    outputs = 3 if with_attention else 0
    attention_in = refs[:inputs]
    payload_refs = refs[inputs : inputs + count]
    attention_out = refs[inputs + count : inputs + count + outputs]
    out_refs = refs[inputs + count + outputs : inputs + 2 * count + outputs]
    send_sems, recv_sems = refs[inputs + 2 * count + outputs :]
    relay, finish = exchange_start(spreads, payload_refs, out_refs, send_sems, recv_sems)
    if with_attention:
        attention_body(*attention_in, *attention_out, relay)
    else:
        relay()
    finish()


def fused_step(attention_args, payloads, spreads, collective_id):
    vmem = pl.BlockSpec(memory_space=pltpu.VMEM)
    out_shapes = []
    flops = 0
    if attention_args:
        queries, key_rows, value_rows, grad_attn = attention_args
        rows, width = queries.shape
        keys = key_rows.shape[0]
        out_shapes = [
            jax.ShapeDtypeStruct((rows, width), jnp.float32),
            jax.ShapeDtypeStruct((keys, width), jnp.float32),
            jax.ShapeDtypeStruct((keys, width), jnp.float32),
        ]
        flops = 2 * 5 * rows * keys * width * (128 // HD)
    for payload, spread in zip(payloads, spreads):
        shape = payload.shape[1:] if spread else payload.shape
        out_shapes.append(jax.ShapeDtypeStruct((len(OFFSETS),) + shape, payload.dtype))
    moved = sum(len(OFFSETS) * x.size * x.dtype.itemsize for x in payloads)
    outs = pl.pallas_call(
        functools.partial(fused_kernel, tuple(spreads), bool(attention_args)),
        out_shape=out_shapes,
        in_specs=[vmem] * (len(attention_args) + len(payloads)),
        out_specs=[vmem] * len(out_shapes),
        scratch_shapes=[
            pltpu.SemaphoreType.DMA((len(payloads), len(OFFSETS))),
            pltpu.SemaphoreType.DMA((len(payloads), len(OFFSETS))),
        ],
        compiler_params=pltpu.CompilerParams(
            collective_id=collective_id,
            has_side_effects=True,
            vmem_limit_bytes=48 * 1024 * 1024,
        ),
        cost_estimate=pl.CostEstimate(
            flops=flops, transcendentals=flops // 160, bytes_accessed=moved + 1
        ),
    )(*attention_args, *payloads)
    return list(outs)


def swap_cores(value):
    return lax.ppermute(value, "pipe", [(0, 1), (1, 0)])


def pick(own, other, core, section):
    return jnp.where(core == section, own, other)


def prepare(rows, lists, weight_in, gain_row, myself):
    points, model_width = rows.shape
    block_count = points // BLK
    scaled, inverse, normed = normalize(rows, gain_row)
    projected = jnp.dot(normed, weight_in, preferred_element_type=jnp.float32).astype(jnp.bfloat16)
    owners = lists // block_count
    within = lists % block_count
    distance = owners - myself
    slot = jnp.where(distance < 0, distance + REACH, distance + REACH - 1)
    window_at = slot * block_count + within
    return dict(
        scaled=scaled,
        inverse=inverse,
        normed=normed,
        queries=projected[:, :model_width],
        own_pairs=projected[:, model_width:],
        window_at=window_at,
    )


def attach(unit, received, weight_in):
    points, model_width = unit["queries"].shape
    received = received.reshape(len(OFFSETS) * (points // BLK), BLK, model_width)
    fetched = jnp.take(received, unit["window_at"], axis=0).reshape(-1, model_width)
    fetched_pairs = jnp.dot(
        fetched, weight_in[:, model_width:], preferred_element_type=jnp.float32
    ).astype(jnp.bfloat16)
    unit["pairs"] = jnp.concatenate([unit["own_pairs"], fetched_pairs], 0)


def outgoing(unit, grad_key, grad_value, weight_in):
    points, model_width = unit["queries"].shape
    block_count = points // BLK
    grad_pairs = jnp.concatenate([grad_key, grad_value], 1)
    grad_remote = jnp.dot(
        grad_pairs[points:].astype(jnp.bfloat16),
        weight_in[:, model_width:].T,
        preferred_element_type=jnp.float32,
    ).reshape(-1, BLK, model_width)
    slots = lax.broadcasted_iota(jnp.int32, (len(OFFSETS) * block_count, 1, 1), 0)
    window_grads = sum(
        jnp.where(slots == unit["window_at"][entry], grad_remote[entry][None], 0.0)
        for entry in range(grad_remote.shape[0])
    )
    unit["own_grad"] = grad_pairs[:points]
    return window_grads.astype(jnp.bfloat16).reshape(len(OFFSETS), points, model_width)


def complete(unit, grad_out, grad_query, returned, weight_in, gain_row):
    grad_project = jnp.concatenate([grad_query, unit["own_grad"]], 1).astype(jnp.bfloat16)
    grad_normed = jnp.dot(grad_project, weight_in.T, preferred_element_type=jnp.float32)
    grad_normed = grad_normed + jnp.sum(returned.astype(jnp.float32), axis=0)
    return (
        grad_out.astype(jnp.float32)
        + norm_backward(grad_normed, unit["scaled"], unit["inverse"], gain_row)
    ).astype(jnp.bfloat16)


def shards(saved_inputs, project_in, project_out, norm_gains, neighbour_blocks, cotangent):
    sections = lax.axis_size("pipe")
    core = lax.axis_index("pipe")
    other = sections - 1 - core
    myself = lax.axis_index("space")
    micro_count = cotangent.shape[0]
    half = micro_count // sections
    model_width = cotangent.shape[2]

    def mine(array, whose):
        grouped = array.reshape((half, sections) + array.shape[1:])
        return lax.dynamic_index_in_dim(grouped, whose, 1, keepdims=False)

    local_lists = neighbour_blocks[0, :, 0, :]
    own = (
        mine(saved_inputs[0], core),
        mine(local_lists, core),
        project_in[0],
        project_out[0],
        norm_gains[0],
    )
    got = swap_cores(
        (
            mine(saved_inputs[0], other),
            mine(local_lists, other),
            project_in[0],
            project_out[0],
            norm_gains[0],
        )
    )
    params = [
        [pick(own_part, got_part, core, section) for own_part, got_part in zip(own, got)]
        for section in range(sections)
    ]
    cotangent_mine = mine(cotangent, core)
    order = [(section, j) for section in range(sections - 1, -1, -1) for j in range(half)]
    units = [
        prepare(params[section][0][j], params[section][1][j], params[section][2], params[section][4], myself)
        for section, j in order
    ]
    results = {}
    exchanged = {}
    ids = iter(range(len(order) + 2))
    (first_received,) = fused_step((), [units[0]["normed"]], [False], next(ids))
    attach(units[0], first_received, params[order[0][0]][2])
    pending = None
    for step, (section, j) in enumerate(order):
        unit = units[step]
        _, _, weight_in, weight_out, gain_row = params[section]
        grad_out = cotangent_mine[j] if section == sections - 1 else results[(section + 1, j)]
        unit["grad_out"] = grad_out
        grad_attn = jnp.dot(grad_out, weight_out.T, preferred_element_type=jnp.float32).astype(
            jnp.bfloat16
        )
        payloads, spreads = [], []
        if pending is not None:
            payloads.append(pending[1])
            spreads.append(True)
        if step == 0:
            for later in units[1:]:
                payloads.append(later["normed"])
                spreads.append(False)
        outs = fused_step(
            (unit["queries"], unit["pairs"][:, :model_width], unit["pairs"][:, model_width:], grad_attn),
            payloads,
            spreads,
            next(ids),
        )
        grad_query, grad_key, grad_value = outs[:3]
        received = outs[3:]
        if pending is not None:
            done_step, _ = pending
            done_section, done_j = order[done_step]
            done_unit = units[done_step]
            results[(done_section, done_j)] = complete(
                done_unit,
                done_unit["grad_out"],
                done_unit["grad_query"],
                received[0],
                params[done_section][2],
                params[done_section][4],
            )
            exchanged[(done_section, done_j)] = swap_cores(results[(done_section, done_j)])
            received = received[1:]
        if step == 0:
            for later, (later_section, _), arrived in zip(units[1:], order[1:], received):
                attach(later, arrived, params[later_section][2])
        unit["grad_query"] = grad_query
        pending = (step, outgoing(unit, grad_key, grad_value, weight_in))
    done_step, window = pending
    done_section, done_j = order[done_step]
    done_unit = units[done_step]
    (returned,) = fused_step((), [window], [True], next(ids))
    results[(done_section, done_j)] = complete(
        done_unit,
        done_unit["grad_out"],
        done_unit["grad_query"],
        returned,
        params[done_section][2],
        params[done_section][4],
    )
    exchanged[(done_section, done_j)] = swap_cores(results[(done_section, done_j)])
    own_out = jnp.stack([pick(results[(0, j)], results[(1, j)], core, 0) for j in range(half)])
    other_out = jnp.stack(
        [pick(exchanged[(0, j)], exchanged[(1, j)], core, 0) for j in range(half)]
    )
    grouped = jnp.stack([pick(own_out, other_out, core, parity) for parity in range(sections)], 1)
    return grouped.reshape((1, micro_count) + grouped.shape[2:])


def solution(mesh):
    return jax.shard_map(
        shards,
        mesh=mesh,
        in_specs=(
            P("pipe", None, "space", None),
            P("pipe", None, None),
            P("pipe", None, None),
            P("pipe", None),
            P("pipe", None, "space", None),
            P(None, "space", None),
        ),
        out_specs=P("pipe", None, "space", None),
        check_vma=False,
    )
```

```python
import functools

import jax
import jax.numpy as jnp
from jax import lax
from jax.experimental import pallas as pl
from jax.experimental.pallas import tpu as pltpu
from jax.sharding import PartitionSpec as P

HEADS = 32
HD = 16
BLK = 128
REACH = 2


epsilon = 1e-05


def shifted(x, axis, by):
    peers = lax.axis_size(axis)
    pairs = [(i, i + by) for i in range(peers) if 0 <= i + by < peers]
    return lax.ppermute(x, axis, pairs)


def normalize(points, gain_row):
    values = points.astype(jnp.float32)
    centre = jnp.mean(values, axis=-1, keepdims=True)
    spread = jnp.mean(jnp.square(values - centre), axis=-1, keepdims=True)
    inverse = lax.rsqrt(spread + epsilon)
    scaled = (values - centre) * inverse
    return (scaled, inverse, (scaled * gain_row).astype(jnp.bfloat16))


def norm_backward(grad_normed, scaled, inverse, gain_row):
    weighted = grad_normed * gain_row
    return inverse * (
        weighted
        - jnp.mean(weighted, axis=-1, keepdims=True)
        - scaled * jnp.mean(weighted * scaled, axis=-1, keepdims=True)
    )


MESH = pl.DeviceIdType.MESH
OFFSETS = [shift_by for shift_by in range(-REACH, REACH + 1) if shift_by != 0]


def attention_body(q_ref, k_ref, v_ref, g_ref, dq_ref, dk_ref, dv_ref, after_first):
    factor = HD ** (-0.5)
    group = 128
    per_group = group // HD
    nt = (((1,), (1,)), ((), ()))
    tn = (((0,), (0,)), ((), ()))
    head_of = lax.broadcasted_iota(jnp.int32, (1, group), 1) // HD
    dq_ref[...] = jnp.zeros_like(dq_ref)
    dk_ref[...] = jnp.zeros_like(dk_ref)
    dv_ref[...] = jnp.zeros_like(dv_ref)

    def head(index, carry):
        cols = pl.ds(pl.multiple_of((index // per_group) * group, group), group)
        mask = head_of == index % per_group
        q = q_ref[:, cols]
        k = k_ref[:, cols]
        v = v_ref[:, cols]
        g = g_ref[:, cols]
        qm = jnp.where(mask, q, jnp.zeros_like(q))
        km = jnp.where(mask, k, jnp.zeros_like(k))
        gm = jnp.where(mask, g, jnp.zeros_like(g))
        scores = lax.dot_general(qm, k, nt, preferred_element_type=jnp.float32) * factor
        top = jnp.max(scores, axis=-1, keepdims=True)
        exps = jnp.exp(scores - top)
        attention = exps * (1.0 / jnp.sum(exps, axis=-1, keepdims=True))
        grad_probs = lax.dot_general(gm, v, nt, preferred_element_type=jnp.float32)
        row = jnp.sum(attention * grad_probs, axis=-1, keepdims=True)
        grad_scores = (attention * (grad_probs - row) * factor).astype(jnp.bfloat16)
        dq_ref[:, cols] += jnp.dot(grad_scores, km, preferred_element_type=jnp.float32)
        dk_ref[:, cols] += lax.dot_general(grad_scores, qm, tn, preferred_element_type=jnp.float32)
        dv_ref[:, cols] += lax.dot_general(
            attention.astype(jnp.bfloat16), gm, tn, preferred_element_type=jnp.float32
        )
        return carry

    heads = q_ref.shape[1] // HD
    split = min(heads, 2 * per_group)
    lax.fori_loop(0, split, head, 0, unroll=2)
    after_first()
    lax.fori_loop(split, heads, head, 0, unroll=2)


def exchange_start(spreads, payload_refs, out_refs, send_sems, recv_sems):
    core = lax.axis_index("pipe")
    me = lax.axis_index("space")
    peers = lax.axis_size("space")
    barrier = pltpu.get_barrier_semaphore()

    def exists(shift_by):
        return (me + shift_by >= 0) & (me + shift_by < peers)

    def slot(shift_by):
        return OFFSETS.index(shift_by)

    for shift_by in OFFSETS:

        @pl.when(exists(shift_by))
        def _():
            pl.semaphore_signal(barrier, 1, device_id=(core, me + shift_by), device_id_type=MESH)

    pl.semaphore_wait(barrier, sum(jnp.where(exists(shift_by), 1, 0) for shift_by in OFFSETS))

    def describe(which, source, landing, shift_by):
        return pltpu.make_async_remote_copy(
            src_ref=source,
            dst_ref=out_refs[which].at[landing],
            send_sem=send_sems.at[which, landing],
            recv_sem=recv_sems.at[which, landing],
            device_id=(core, me + shift_by),
            device_id_type=MESH,
        )

    def arrival(which, landing):
        return describe(which, out_refs[which].at[landing], landing, OFFSETS[landing])

    direct = []
    relayed = []
    relaying = not any(spreads)
    for which, spread in enumerate(spreads):
        x_ref = payload_refs[which]
        targets = OFFSETS if spread or not relaying else [-1, 1]
        for shift_by in targets:
            source = x_ref.at[slot(shift_by)] if spread else x_ref
            copy = describe(which, source, slot(-shift_by), shift_by)
            direct.append((copy, exists(shift_by)))

            @pl.when(exists(shift_by))
            def _():
                copy.start()

        for shift_by in OFFSETS:

            @pl.when(jnp.logical_not(exists(shift_by)))
            def _():
                out_refs[which][slot(shift_by)] = jnp.zeros(
                    out_refs[which].shape[1:], out_refs[which].dtype
                )

        if relaying and not spread:
            for shift_by in (-1, 1):
                forward = describe(
                    which, out_refs[which].at[slot(-shift_by)], slot(-2 * shift_by), shift_by
                )
                relayed.append((which, shift_by, forward, exists(shift_by) & exists(-shift_by)))

    def relay():
        for which, shift_by, forward, valid in relayed:

            @pl.when(exists(-shift_by))
            def _():
                arrival(which, slot(-shift_by)).wait_recv()

        for which, shift_by, forward, valid in relayed:

            @pl.when(valid)
            def _():
                forward.start()

    def finish():
        for copy, valid in direct:

            @pl.when(valid)
            def _():
                copy.wait_send()

        for which, shift_by, forward, valid in relayed:

            @pl.when(valid)
            def _():
                forward.wait_send()

        relayed_slots = {(which, slot(-shift_by)) for which, shift_by, _, _ in relayed}
        for which in range(len(spreads)):
            for landing, shift_by in enumerate(OFFSETS):
                if (which, landing) in relayed_slots:
                    continue

                @pl.when(exists(shift_by))
                def _():
                    arrival(which, landing).wait_recv()

    return relay, finish


def fused_kernel(spreads, with_attention, *refs):
    count = len(spreads)
    inputs = 4 if with_attention else 0
    outputs = 3 if with_attention else 0
    attention_in = refs[:inputs]
    payload_refs = refs[inputs : inputs + count]
    attention_out = refs[inputs + count : inputs + count + outputs]
    out_refs = refs[inputs + count + outputs : inputs + 2 * count + outputs]
    send_sems, recv_sems = refs[inputs + 2 * count + outputs :]
    relay, finish = exchange_start(spreads, payload_refs, out_refs, send_sems, recv_sems)
    if with_attention:
        attention_body(*attention_in, *attention_out, relay)
    else:
        relay()
    finish()


def fused_step(attention_args, payloads, spreads, collective_id):
    vmem = pl.BlockSpec(memory_space=pltpu.VMEM)
    out_shapes = []
    flops = 0
    if attention_args:
        queries, key_rows, value_rows, grad_attn = attention_args
        rows, width = queries.shape
        keys = key_rows.shape[0]
        out_shapes = [
            jax.ShapeDtypeStruct((rows, width), jnp.float32),
            jax.ShapeDtypeStruct((keys, width), jnp.float32),
            jax.ShapeDtypeStruct((keys, width), jnp.float32),
        ]
        flops = 2 * 5 * rows * keys * width * (128 // HD)
    for payload, spread in zip(payloads, spreads):
        shape = payload.shape[1:] if spread else payload.shape
        out_shapes.append(jax.ShapeDtypeStruct((len(OFFSETS),) + shape, payload.dtype))
    moved = sum(len(OFFSETS) * x.size * x.dtype.itemsize for x in payloads)
    outs = pl.pallas_call(
        functools.partial(fused_kernel, tuple(spreads), bool(attention_args)),
        out_shape=out_shapes,
        in_specs=[vmem] * (len(attention_args) + len(payloads)),
        out_specs=[vmem] * len(out_shapes),
        scratch_shapes=[
            pltpu.SemaphoreType.DMA((len(payloads), len(OFFSETS))),
            pltpu.SemaphoreType.DMA((len(payloads), len(OFFSETS))),
        ],
        compiler_params=pltpu.CompilerParams(
            collective_id=collective_id,
            has_side_effects=True,
            vmem_limit_bytes=48 * 1024 * 1024,
        ),
        cost_estimate=pl.CostEstimate(
            flops=flops, transcendentals=flops // 160, bytes_accessed=moved + 1
        ),
    )(*attention_args, *payloads)
    return list(outs)


def swap_cores(value):
    return lax.ppermute(value, "pipe", [(0, 1), (1, 0)])


def pick(own, other, core, section):
    return jnp.where(core == section, own, other)


def prepare(rows, lists, weight_in, gain_row, myself):
    points, model_width = rows.shape
    block_count = points // BLK
    scaled, inverse, normed = normalize(rows, gain_row)
    projected = jnp.dot(normed, weight_in, preferred_element_type=jnp.float32).astype(jnp.bfloat16)
    owners = lists // block_count
    within = lists % block_count
    distance = owners - myself
    slot = jnp.where(distance < 0, distance + REACH, distance + REACH - 1)
    window_at = slot * block_count + within
    return dict(
        scaled=scaled,
        inverse=inverse,
        normed=normed,
        queries=projected[:, :model_width],
        own_pairs=projected[:, model_width:],
        window_at=window_at,
    )


def attach(unit, received, weight_in):
    points, model_width = unit["queries"].shape
    received = received.reshape(len(OFFSETS) * (points // BLK), BLK, model_width)
    fetched = jnp.take(received, unit["window_at"], axis=0).reshape(-1, model_width)
    fetched_pairs = jnp.dot(
        fetched, weight_in[:, model_width:], preferred_element_type=jnp.float32
    ).astype(jnp.bfloat16)
    unit["pairs"] = jnp.concatenate([unit["own_pairs"], fetched_pairs], 0)


def outgoing(unit, grad_key, grad_value, weight_in):
    points, model_width = unit["queries"].shape
    block_count = points // BLK
    grad_pairs = jnp.concatenate([grad_key, grad_value], 1)
    grad_remote = jnp.dot(
        grad_pairs[points:].astype(jnp.bfloat16),
        weight_in[:, model_width:].T,
        preferred_element_type=jnp.float32,
    ).reshape(-1, BLK, model_width)
    slots = lax.broadcasted_iota(jnp.int32, (len(OFFSETS) * block_count, 1, 1), 0)
    window_grads = sum(
        jnp.where(slots == unit["window_at"][entry], grad_remote[entry][None], 0.0)
        for entry in range(grad_remote.shape[0])
    )
    unit["own_grad"] = grad_pairs[:points]
    return window_grads.astype(jnp.bfloat16).reshape(len(OFFSETS), points, model_width)


def complete(unit, grad_out, grad_query, returned, weight_in, gain_row):
    grad_project = jnp.concatenate([grad_query, unit["own_grad"]], 1).astype(jnp.bfloat16)
    grad_normed = jnp.dot(grad_project, weight_in.T, preferred_element_type=jnp.float32)
    grad_normed = grad_normed + jnp.sum(returned.astype(jnp.float32), axis=0)
    return (
        grad_out.astype(jnp.float32)
        + norm_backward(grad_normed, unit["scaled"], unit["inverse"], gain_row)
    ).astype(jnp.bfloat16)


def shards(saved_inputs, project_in, project_out, norm_gains, neighbour_blocks, cotangent):
    sections = lax.axis_size("pipe")
    core = lax.axis_index("pipe")
    other = sections - 1 - core
    myself = lax.axis_index("space")
    micro_count = cotangent.shape[0]
    half = micro_count // sections
    model_width = cotangent.shape[2]

    def mine(array, whose):
        grouped = array.reshape((half, sections) + array.shape[1:])
        return lax.dynamic_index_in_dim(grouped, whose, 1, keepdims=False)

    local_lists = neighbour_blocks[0, :, 0, :]
    own = (
        mine(saved_inputs[0], core),
        mine(local_lists, core),
        project_in[0],
        project_out[0],
        norm_gains[0],
    )
    got = swap_cores(
        (
            mine(saved_inputs[0], other),
            mine(local_lists, other),
            project_in[0],
            project_out[0],
            norm_gains[0],
        )
    )
    params = [
        [pick(own_part, got_part, core, section) for own_part, got_part in zip(own, got)]
        for section in range(sections)
    ]
    cotangent_mine = mine(cotangent, core)
    order = [(section, j) for section in range(sections - 1, -1, -1) for j in range(half)]
    units = [
        prepare(params[section][0][j], params[section][1][j], params[section][2], params[section][4], myself)
        for section, j in order
    ]
    results = {}
    ids = iter(range(len(order) + 2))
    (first_received,) = fused_step((), [units[0]["normed"]], [False], next(ids))
    attach(units[0], first_received, params[order[0][0]][2])
    pending = None
    for step, (section, j) in enumerate(order):
        unit = units[step]
        _, _, weight_in, weight_out, gain_row = params[section]
        grad_out = cotangent_mine[j] if section == sections - 1 else results[(section + 1, j)]
        unit["grad_out"] = grad_out
        grad_attn = jnp.dot(grad_out, weight_out.T, preferred_element_type=jnp.float32).astype(
            jnp.bfloat16
        )
        payloads, spreads = [], []
        if pending is not None:
            payloads.append(pending[1])
            spreads.append(True)
        if step == 0:
            for later in units[1:]:
                payloads.append(later["normed"])
                spreads.append(False)
        outs = fused_step(
            (unit["queries"], unit["pairs"][:, :model_width], unit["pairs"][:, model_width:], grad_attn),
            payloads,
            spreads,
            next(ids),
        )
        grad_query, grad_key, grad_value = outs[:3]
        received = outs[3:]
        if pending is not None:
            done_step, _ = pending
            done_section, done_j = order[done_step]
            done_unit = units[done_step]
            results[(done_section, done_j)] = complete(
                done_unit,
                done_unit["grad_out"],
                done_unit["grad_query"],
                received[0],
                params[done_section][2],
                params[done_section][4],
            )
            received = received[1:]
        if step == 0:
            for later, (later_section, _), arrived in zip(units[1:], order[1:], received):
                attach(later, arrived, params[later_section][2])
        unit["grad_query"] = grad_query
        pending = (step, outgoing(unit, grad_key, grad_value, weight_in))
    done_step, window = pending
    done_section, done_j = order[done_step]
    done_unit = units[done_step]
    (returned,) = fused_step((), [window], [True], next(ids))
    results[(done_section, done_j)] = complete(
        done_unit,
        done_unit["grad_out"],
        done_unit["grad_query"],
        returned,
        params[done_section][2],
        params[done_section][4],
    )
    own_out = jnp.stack([pick(results[(0, j)], results[(1, j)], core, 0) for j in range(half)])
    other_out = swap_cores(
        jnp.stack([pick(results[(1, j)], results[(0, j)], core, 0) for j in range(half)])
    )
    grouped = jnp.stack([pick(own_out, other_out, core, parity) for parity in range(sections)], 1)
    return grouped.reshape((1, micro_count) + grouped.shape[2:])


def solution(mesh):
    return jax.shard_map(
        shards,
        mesh=mesh,
        in_specs=(
            P("pipe", None, "space", None),
            P("pipe", None, None),
            P("pipe", None, None),
            P("pipe", None),
            P("pipe", None, "space", None),
            P(None, "space", None),
        ),
        out_specs=P("pipe", None, "space", None),
        check_vma=False,
    )
```

```python
import functools

import jax
import jax.numpy as jnp
from jax import lax
from jax.experimental import pallas as pl
from jax.experimental.pallas import tpu as pltpu
from jax.sharding import PartitionSpec as P

HEADS = 32
HD = 16
BLK = 128
REACH = 2


epsilon = 1e-05


def shifted(x, axis, by):
    peers = lax.axis_size(axis)
    pairs = [(i, i + by) for i in range(peers) if 0 <= i + by < peers]
    return lax.ppermute(x, axis, pairs)


def normalize(points, gain_row):
    values = points.astype(jnp.float32)
    centre = jnp.mean(values, axis=-1, keepdims=True)
    spread = jnp.mean(jnp.square(values - centre), axis=-1, keepdims=True)
    inverse = lax.rsqrt(spread + epsilon)
    scaled = (values - centre) * inverse
    return (scaled, inverse, (scaled * gain_row).astype(jnp.bfloat16))


def norm_backward(grad_normed, scaled, inverse, gain_row):
    weighted = grad_normed * gain_row
    return inverse * (
        weighted
        - jnp.mean(weighted, axis=-1, keepdims=True)
        - scaled * jnp.mean(weighted * scaled, axis=-1, keepdims=True)
    )


MESH = pl.DeviceIdType.MESH
OFFSETS = [shift_by for shift_by in range(-REACH, REACH + 1) if shift_by != 0]


def attention_body(q_ref, k_ref, v_ref, g_ref, dq_ref, dk_ref, dv_ref, after_first):
    factor = HD ** (-0.5)
    group = 128
    per_group = group // HD
    nt = (((1,), (1,)), ((), ()))
    tn = (((0,), (0,)), ((), ()))
    head_of = lax.broadcasted_iota(jnp.int32, (1, group), 1) // HD
    dq_ref[...] = jnp.zeros_like(dq_ref)
    dk_ref[...] = jnp.zeros_like(dk_ref)
    dv_ref[...] = jnp.zeros_like(dv_ref)

    def head(index, carry):
        cols = pl.ds(pl.multiple_of((index // per_group) * group, group), group)
        mask = head_of == index % per_group
        q = q_ref[:, cols]
        k = k_ref[:, cols]
        v = v_ref[:, cols]
        g = g_ref[:, cols]
        qm = jnp.where(mask, q, jnp.zeros_like(q))
        km = jnp.where(mask, k, jnp.zeros_like(k))
        gm = jnp.where(mask, g, jnp.zeros_like(g))
        scores = lax.dot_general(qm, k, nt, preferred_element_type=jnp.float32) * factor
        top = jnp.max(scores, axis=-1, keepdims=True)
        exps = jnp.exp(scores - top)
        attention = exps * (1.0 / jnp.sum(exps, axis=-1, keepdims=True))
        grad_probs = lax.dot_general(gm, v, nt, preferred_element_type=jnp.float32)
        row = jnp.sum(attention * grad_probs, axis=-1, keepdims=True)
        grad_scores = (attention * (grad_probs - row) * factor).astype(jnp.bfloat16)
        dq_ref[:, cols] += jnp.dot(grad_scores, km, preferred_element_type=jnp.float32)
        dk_ref[:, cols] += lax.dot_general(grad_scores, qm, tn, preferred_element_type=jnp.float32)
        dv_ref[:, cols] += lax.dot_general(
            attention.astype(jnp.bfloat16), gm, tn, preferred_element_type=jnp.float32
        )
        return carry

    heads = q_ref.shape[1] // HD
    if after_first is None:
        lax.fori_loop(0, heads, head, 0, unroll=4)
    else:
        split = min(heads, 2 * per_group)
        lax.fori_loop(0, split, head, 0, unroll=2)
        after_first()
        lax.fori_loop(split, heads, head, 0, unroll=2)


def exchange_start(spreads, payload_refs, out_refs, send_sems, recv_sems):
    core = lax.axis_index("pipe")
    me = lax.axis_index("space")
    peers = lax.axis_size("space")
    barrier = pltpu.get_barrier_semaphore()

    def exists(shift_by):
        return (me + shift_by >= 0) & (me + shift_by < peers)

    def slot(shift_by):
        return OFFSETS.index(shift_by)

    for shift_by in OFFSETS:

        @pl.when(exists(shift_by))
        def _():
            pl.semaphore_signal(barrier, 1, device_id=(core, me + shift_by), device_id_type=MESH)

    pl.semaphore_wait(barrier, sum(jnp.where(exists(shift_by), 1, 0) for shift_by in OFFSETS))

    def describe(which, source, landing, shift_by):
        return pltpu.make_async_remote_copy(
            src_ref=source,
            dst_ref=out_refs[which].at[landing],
            send_sem=send_sems.at[which, landing],
            recv_sem=recv_sems.at[which, landing],
            device_id=(core, me + shift_by),
            device_id_type=MESH,
        )

    def arrival(which, landing):
        return describe(which, out_refs[which].at[landing], landing, OFFSETS[landing])

    direct = []
    relayed = []
    relaying = not any(spreads)
    for which, spread in enumerate(spreads):
        x_ref = payload_refs[which]
        targets = OFFSETS if spread or not relaying else [-1, 1]
        for shift_by in targets:
            source = x_ref.at[slot(shift_by)] if spread else x_ref
            copy = describe(which, source, slot(-shift_by), shift_by)
            direct.append((copy, exists(shift_by)))

            @pl.when(exists(shift_by))
            def _():
                copy.start()

        for shift_by in OFFSETS:

            @pl.when(jnp.logical_not(exists(shift_by)))
            def _():
                out_refs[which][slot(shift_by)] = jnp.zeros(
                    out_refs[which].shape[1:], out_refs[which].dtype
                )

        if relaying and not spread:
            for shift_by in (-1, 1):
                forward = describe(
                    which, out_refs[which].at[slot(-shift_by)], slot(-2 * shift_by), shift_by
                )
                relayed.append((which, shift_by, forward, exists(shift_by) & exists(-shift_by)))

    def relay():
        for which, shift_by, forward, valid in relayed:

            @pl.when(exists(-shift_by))
            def _():
                arrival(which, slot(-shift_by)).wait_recv()

        for which, shift_by, forward, valid in relayed:

            @pl.when(valid)
            def _():
                forward.start()

    def finish():
        for copy, valid in direct:

            @pl.when(valid)
            def _():
                copy.wait_send()

        for which, shift_by, forward, valid in relayed:

            @pl.when(valid)
            def _():
                forward.wait_send()

        relayed_slots = {(which, slot(-shift_by)) for which, shift_by, _, _ in relayed}
        for which in range(len(spreads)):
            for landing, shift_by in enumerate(OFFSETS):
                if (which, landing) in relayed_slots:
                    continue

                @pl.when(exists(shift_by))
                def _():
                    arrival(which, landing).wait_recv()

    return relay, finish


def fused_kernel(spreads, with_attention, *refs):
    count = len(spreads)
    inputs = 4 if with_attention else 0
    outputs = 3 if with_attention else 0
    attention_in = refs[:inputs]
    payload_refs = refs[inputs : inputs + count]
    attention_out = refs[inputs + count : inputs + count + outputs]
    out_refs = refs[inputs + count + outputs : inputs + 2 * count + outputs]
    send_sems, recv_sems = refs[inputs + 2 * count + outputs :]
    relay, finish = exchange_start(spreads, payload_refs, out_refs, send_sems, recv_sems)
    if with_attention:
        attention_body(*attention_in, *attention_out, relay if not any(spreads) else None)
    else:
        relay()
    finish()


def fused_step(attention_args, payloads, spreads, collective_id):
    vmem = pl.BlockSpec(memory_space=pltpu.VMEM)
    out_shapes = []
    flops = 0
    if attention_args:
        queries, key_rows, value_rows, grad_attn = attention_args
        rows, width = queries.shape
        keys = key_rows.shape[0]
        out_shapes = [
            jax.ShapeDtypeStruct((rows, width), jnp.float32),
            jax.ShapeDtypeStruct((keys, width), jnp.float32),
            jax.ShapeDtypeStruct((keys, width), jnp.float32),
        ]
        flops = 2 * 5 * rows * keys * width * (128 // HD)
    for payload, spread in zip(payloads, spreads):
        shape = payload.shape[1:] if spread else payload.shape
        out_shapes.append(jax.ShapeDtypeStruct((len(OFFSETS),) + shape, payload.dtype))
    moved = sum(len(OFFSETS) * x.size * x.dtype.itemsize for x in payloads)
    outs = pl.pallas_call(
        functools.partial(fused_kernel, tuple(spreads), bool(attention_args)),
        out_shape=out_shapes,
        in_specs=[vmem] * (len(attention_args) + len(payloads)),
        out_specs=[vmem] * len(out_shapes),
        scratch_shapes=[
            pltpu.SemaphoreType.DMA((len(payloads), len(OFFSETS))),
            pltpu.SemaphoreType.DMA((len(payloads), len(OFFSETS))),
        ],
        compiler_params=pltpu.CompilerParams(
            collective_id=collective_id,
            has_side_effects=True,
            vmem_limit_bytes=48 * 1024 * 1024,
        ),
        cost_estimate=pl.CostEstimate(
            flops=flops, transcendentals=flops // 160, bytes_accessed=moved + 1
        ),
    )(*attention_args, *payloads)
    return list(outs)


def swap_cores(value):
    return lax.ppermute(value, "pipe", [(0, 1), (1, 0)])


def pick(own, other, core, section):
    return jnp.where(core == section, own, other)


def prepare(rows, lists, weight_in, gain_row, myself):
    points, model_width = rows.shape
    block_count = points // BLK
    scaled, inverse, normed = normalize(rows, gain_row)
    projected = jnp.dot(normed, weight_in, preferred_element_type=jnp.float32).astype(jnp.bfloat16)
    owners = lists // block_count
    within = lists % block_count
    distance = owners - myself
    slot = jnp.where(distance < 0, distance + REACH, distance + REACH - 1)
    window_at = slot * block_count + within
    return dict(
        scaled=scaled,
        inverse=inverse,
        normed=normed,
        queries=projected[:, :model_width],
        own_pairs=projected[:, model_width:],
        window_at=window_at,
    )


def attach(unit, received, weight_in):
    points, model_width = unit["queries"].shape
    received = received.reshape(len(OFFSETS) * (points // BLK), BLK, model_width)
    fetched = jnp.take(received, unit["window_at"], axis=0).reshape(-1, model_width)
    fetched_pairs = jnp.dot(
        fetched, weight_in[:, model_width:], preferred_element_type=jnp.float32
    ).astype(jnp.bfloat16)
    unit["pairs"] = jnp.concatenate([unit["own_pairs"], fetched_pairs], 0)


def outgoing(unit, grad_key, grad_value, weight_in):
    points, model_width = unit["queries"].shape
    block_count = points // BLK
    grad_pairs = jnp.concatenate([grad_key, grad_value], 1)
    grad_remote = jnp.dot(
        grad_pairs[points:].astype(jnp.bfloat16),
        weight_in[:, model_width:].T,
        preferred_element_type=jnp.float32,
    ).reshape(-1, BLK, model_width)
    slots = lax.broadcasted_iota(jnp.int32, (len(OFFSETS) * block_count, 1, 1), 0)
    window_grads = sum(
        jnp.where(slots == unit["window_at"][entry], grad_remote[entry][None], 0.0)
        for entry in range(grad_remote.shape[0])
    )
    unit["own_grad"] = grad_pairs[:points]
    return window_grads.astype(jnp.bfloat16).reshape(len(OFFSETS), points, model_width)


def complete(unit, grad_out, grad_query, returned, weight_in, gain_row):
    grad_project = jnp.concatenate([grad_query, unit["own_grad"]], 1).astype(jnp.bfloat16)
    grad_normed = jnp.dot(grad_project, weight_in.T, preferred_element_type=jnp.float32)
    grad_normed = grad_normed + jnp.sum(returned.astype(jnp.float32), axis=0)
    return (
        grad_out.astype(jnp.float32)
        + norm_backward(grad_normed, unit["scaled"], unit["inverse"], gain_row)
    ).astype(jnp.bfloat16)


def shards(saved_inputs, project_in, project_out, norm_gains, neighbour_blocks, cotangent):
    sections = lax.axis_size("pipe")
    core = lax.axis_index("pipe")
    other = sections - 1 - core
    myself = lax.axis_index("space")
    micro_count = cotangent.shape[0]
    half = micro_count // sections
    model_width = cotangent.shape[2]

    def mine(array, whose):
        grouped = array.reshape((half, sections) + array.shape[1:])
        return lax.dynamic_index_in_dim(grouped, whose, 1, keepdims=False)

    local_lists = neighbour_blocks[0, :, 0, :]
    own = (
        mine(saved_inputs[0], core),
        mine(local_lists, core),
        project_in[0],
        project_out[0],
        norm_gains[0],
    )
    got = swap_cores(
        (
            mine(saved_inputs[0], other),
            mine(local_lists, other),
            project_in[0],
            project_out[0],
            norm_gains[0],
        )
    )
    params = [
        [pick(own_part, got_part, core, section) for own_part, got_part in zip(own, got)]
        for section in range(sections)
    ]
    cotangent_mine = mine(cotangent, core)
    order = [(section, j) for section in range(sections - 1, -1, -1) for j in range(half)]
    units = [
        prepare(params[section][0][j], params[section][1][j], params[section][2], params[section][4], myself)
        for section, j in order
    ]
    results = {}
    ids = iter(range(len(order) + 2))
    (first_received,) = fused_step((), [units[0]["normed"]], [False], next(ids))
    attach(units[0], first_received, params[order[0][0]][2])
    pending = None
    for step, (section, j) in enumerate(order):
        unit = units[step]
        _, _, weight_in, weight_out, gain_row = params[section]
        grad_out = cotangent_mine[j] if section == sections - 1 else results[(section + 1, j)]
        unit["grad_out"] = grad_out
        grad_attn = jnp.dot(grad_out, weight_out.T, preferred_element_type=jnp.float32).astype(
            jnp.bfloat16
        )
        payloads, spreads = [], []
        if pending is not None:
            payloads.append(pending[1])
            spreads.append(True)
        if step == 0:
            for later in units[1:]:
                payloads.append(later["normed"])
                spreads.append(False)
        outs = fused_step(
            (unit["queries"], unit["pairs"][:, :model_width], unit["pairs"][:, model_width:], grad_attn),
            payloads,
            spreads,
            next(ids),
        )
        grad_query, grad_key, grad_value = outs[:3]
        received = outs[3:]
        if pending is not None:
            done_step, _ = pending
            done_section, done_j = order[done_step]
            done_unit = units[done_step]
            results[(done_section, done_j)] = complete(
                done_unit,
                done_unit["grad_out"],
                done_unit["grad_query"],
                received[0],
                params[done_section][2],
                params[done_section][4],
            )
            received = received[1:]
        if step == 0:
            for later, (later_section, _), arrived in zip(units[1:], order[1:], received):
                attach(later, arrived, params[later_section][2])
        unit["grad_query"] = grad_query
        pending = (step, outgoing(unit, grad_key, grad_value, weight_in))
    done_step, window = pending
    done_section, done_j = order[done_step]
    done_unit = units[done_step]
    (returned,) = fused_step((), [window], [True], next(ids))
    results[(done_section, done_j)] = complete(
        done_unit,
        done_unit["grad_out"],
        done_unit["grad_query"],
        returned,
        params[done_section][2],
        params[done_section][4],
    )
    own_out = jnp.stack([pick(results[(0, j)], results[(1, j)], core, 0) for j in range(half)])
    other_out = swap_cores(
        jnp.stack([pick(results[(1, j)], results[(0, j)], core, 0) for j in range(half)])
    )
    grouped = jnp.stack([pick(own_out, other_out, core, parity) for parity in range(sections)], 1)
    return grouped.reshape((1, micro_count) + grouped.shape[2:])


def solution(mesh):
    return jax.shard_map(
        shards,
        mesh=mesh,
        in_specs=(
            P("pipe", None, "space", None),
            P("pipe", None, None),
            P("pipe", None, None),
            P("pipe", None),
            P("pipe", None, "space", None),
            P(None, "space", None),
        ),
        out_specs=P("pipe", None, "space", None),
        check_vma=False,
    )
```

```python
import functools

import jax
import jax.numpy as jnp
from jax import lax
from jax.experimental import pallas as pl
from jax.experimental.pallas import tpu as pltpu
from jax.sharding import PartitionSpec as P

HEADS = 32
HD = 16
BLK = 128
REACH = 2


epsilon = 1e-05


def shifted(x, axis, by):
    peers = lax.axis_size(axis)
    pairs = [(i, i + by) for i in range(peers) if 0 <= i + by < peers]
    return lax.ppermute(x, axis, pairs)


def normalize(points, gain_row):
    values = points.astype(jnp.float32)
    centre = jnp.mean(values, axis=-1, keepdims=True)
    spread = jnp.mean(jnp.square(values - centre), axis=-1, keepdims=True)
    inverse = lax.rsqrt(spread + epsilon)
    scaled = (values - centre) * inverse
    return (scaled, inverse, (scaled * gain_row).astype(jnp.bfloat16))


def norm_backward(grad_normed, scaled, inverse, gain_row):
    weighted = grad_normed * gain_row
    return inverse * (
        weighted
        - jnp.mean(weighted, axis=-1, keepdims=True)
        - scaled * jnp.mean(weighted * scaled, axis=-1, keepdims=True)
    )


MESH = pl.DeviceIdType.MESH
OFFSETS = [shift_by for shift_by in range(-REACH, REACH + 1) if shift_by != 0]


def attention_body(q_ref, k_ref, v_ref, g_ref, dq_ref, dk_ref, dv_ref, hooks):
    factor = HD ** (-0.5)
    group = 128
    per_group = group // HD
    nt = (((1,), (1,)), ((), ()))
    tn = (((0,), (0,)), ((), ()))
    head_of = lax.broadcasted_iota(jnp.int32, (1, group), 1) // HD
    dq_ref[...] = jnp.zeros_like(dq_ref)
    dk_ref[...] = jnp.zeros_like(dk_ref)
    dv_ref[...] = jnp.zeros_like(dv_ref)

    def head(index, carry):
        cols = pl.ds(pl.multiple_of((index // per_group) * group, group), group)
        mask = head_of == index % per_group
        q = q_ref[:, cols]
        k = k_ref[:, cols]
        v = v_ref[:, cols]
        g = g_ref[:, cols]
        qm = jnp.where(mask, q, jnp.zeros_like(q))
        km = jnp.where(mask, k, jnp.zeros_like(k))
        gm = jnp.where(mask, g, jnp.zeros_like(g))
        scores = lax.dot_general(qm, k, nt, preferred_element_type=jnp.float32) * factor
        top = jnp.max(scores, axis=-1, keepdims=True)
        exps = jnp.exp(scores - top)
        attention = exps * (1.0 / jnp.sum(exps, axis=-1, keepdims=True))
        grad_probs = lax.dot_general(gm, v, nt, preferred_element_type=jnp.float32)
        row = jnp.sum(attention * grad_probs, axis=-1, keepdims=True)
        grad_scores = (attention * (grad_probs - row) * factor).astype(jnp.bfloat16)
        dq_ref[:, cols] += jnp.dot(grad_scores, km, preferred_element_type=jnp.float32)
        dk_ref[:, cols] += lax.dot_general(grad_scores, qm, tn, preferred_element_type=jnp.float32)
        dv_ref[:, cols] += lax.dot_general(
            attention.astype(jnp.bfloat16), gm, tn, preferred_element_type=jnp.float32
        )
        return carry

    heads = q_ref.shape[1] // HD
    if not hooks:
        lax.fori_loop(0, heads, head, 0, unroll=4)
    else:
        begin = 0
        for edge in sorted(hooks):
            lax.fori_loop(begin, edge, head, 0, unroll=2)
            hooks[edge]()
            begin = edge
        lax.fori_loop(begin, heads, head, 0, unroll=2)


def exchange_start(spreads, payload_refs, out_refs, send_sems, recv_sems):
    core = lax.axis_index("pipe")
    me = lax.axis_index("space")
    peers = lax.axis_size("space")
    barrier = pltpu.get_barrier_semaphore()

    def exists(shift_by):
        return (me + shift_by >= 0) & (me + shift_by < peers)

    def slot(shift_by):
        return OFFSETS.index(shift_by)

    for shift_by in OFFSETS:

        @pl.when(exists(shift_by))
        def _():
            pl.semaphore_signal(barrier, 1, device_id=(core, me + shift_by), device_id_type=MESH)

    pl.semaphore_wait(barrier, sum(jnp.where(exists(shift_by), 1, 0) for shift_by in OFFSETS))

    def describe(which, source, landing, shift_by):
        return pltpu.make_async_remote_copy(
            src_ref=source,
            dst_ref=out_refs[which].at[landing],
            send_sem=send_sems.at[which, landing],
            recv_sem=recv_sems.at[which, landing],
            device_id=(core, me + shift_by),
            device_id_type=MESH,
        )

    def arrival(which, landing):
        return describe(which, out_refs[which].at[landing], landing, OFFSETS[landing])

    direct = []
    relayed = []
    relaying = not any(spreads)
    for which, spread in enumerate(spreads):
        x_ref = payload_refs[which]
        targets = OFFSETS if spread or not relaying else [-1, 1]
        for shift_by in targets:
            source = x_ref.at[slot(shift_by)] if spread else x_ref
            copy = describe(which, source, slot(-shift_by), shift_by)
            direct.append((copy, exists(shift_by)))

            @pl.when(exists(shift_by))
            def _():
                copy.start()

        for shift_by in OFFSETS:

            @pl.when(jnp.logical_not(exists(shift_by)))
            def _():
                out_refs[which][slot(shift_by)] = jnp.zeros(
                    out_refs[which].shape[1:], out_refs[which].dtype
                )

        if relaying and not spread:
            for shift_by in (-1, 1):
                forward = describe(
                    which, out_refs[which].at[slot(-shift_by)], slot(-2 * shift_by), shift_by
                )
                relayed.append((which, shift_by, forward, exists(shift_by) & exists(-shift_by)))

    def relay(whiches):
        chosen = [entry for entry in relayed if entry[0] in whiches]
        for which, shift_by, forward, valid in chosen:

            @pl.when(exists(-shift_by))
            def _():
                arrival(which, slot(-shift_by)).wait_recv()

        for which, shift_by, forward, valid in chosen:

            @pl.when(valid)
            def _():
                forward.start()

    def finish():
        for copy, valid in direct:

            @pl.when(valid)
            def _():
                copy.wait_send()

        for which, shift_by, forward, valid in relayed:

            @pl.when(valid)
            def _():
                forward.wait_send()

        relayed_slots = {(which, slot(-shift_by)) for which, shift_by, _, _ in relayed}
        for which in range(len(spreads)):
            for landing, shift_by in enumerate(OFFSETS):
                if (which, landing) in relayed_slots:
                    continue

                @pl.when(exists(shift_by))
                def _():
                    arrival(which, landing).wait_recv()

    return relay, finish


def fused_kernel(spreads, with_attention, *refs):
    count = len(spreads)
    inputs = 4 if with_attention else 0
    outputs = 3 if with_attention else 0
    attention_in = refs[:inputs]
    payload_refs = refs[inputs : inputs + count]
    attention_out = refs[inputs + count : inputs + count + outputs]
    out_refs = refs[inputs + count + outputs : inputs + 2 * count + outputs]
    send_sems, recv_sems = refs[inputs + 2 * count + outputs :]
    relay, finish = exchange_start(spreads, payload_refs, out_refs, send_sems, recv_sems)
    if with_attention:
        hooks = {}
        if not any(spreads):
            heads = attention_in[0].shape[1] // HD
            for which in range(count):
                edge = (which + 1) * heads // (count + 1)
                hooks[edge] = functools.partial(relay, [which])
        attention_body(*attention_in, *attention_out, hooks)
    else:
        relay(list(range(count)))
    finish()


def fused_step(attention_args, payloads, spreads, collective_id):
    vmem = pl.BlockSpec(memory_space=pltpu.VMEM)
    out_shapes = []
    flops = 0
    if attention_args:
        queries, key_rows, value_rows, grad_attn = attention_args
        rows, width = queries.shape
        keys = key_rows.shape[0]
        out_shapes = [
            jax.ShapeDtypeStruct((rows, width), jnp.float32),
            jax.ShapeDtypeStruct((keys, width), jnp.float32),
            jax.ShapeDtypeStruct((keys, width), jnp.float32),
        ]
        flops = 2 * 5 * rows * keys * width * (128 // HD)
    for payload, spread in zip(payloads, spreads):
        shape = payload.shape[1:] if spread else payload.shape
        out_shapes.append(jax.ShapeDtypeStruct((len(OFFSETS),) + shape, payload.dtype))
    moved = sum(len(OFFSETS) * x.size * x.dtype.itemsize for x in payloads)
    outs = pl.pallas_call(
        functools.partial(fused_kernel, tuple(spreads), bool(attention_args)),
        out_shape=out_shapes,
        in_specs=[vmem] * (len(attention_args) + len(payloads)),
        out_specs=[vmem] * len(out_shapes),
        scratch_shapes=[
            pltpu.SemaphoreType.DMA((len(payloads), len(OFFSETS))),
            pltpu.SemaphoreType.DMA((len(payloads), len(OFFSETS))),
        ],
        compiler_params=pltpu.CompilerParams(
            collective_id=collective_id,
            has_side_effects=True,
            vmem_limit_bytes=48 * 1024 * 1024,
        ),
        cost_estimate=pl.CostEstimate(
            flops=flops, transcendentals=flops // 160, bytes_accessed=moved + 1
        ),
    )(*attention_args, *payloads)
    return list(outs)


def swap_cores(value):
    return lax.ppermute(value, "pipe", [(0, 1), (1, 0)])


def pick(own, other, core, section):
    return jnp.where(core == section, own, other)


def prepare(rows, lists, weight_in, gain_row, myself):
    points, model_width = rows.shape
    block_count = points // BLK
    scaled, inverse, normed = normalize(rows, gain_row)
    projected = jnp.dot(normed, weight_in, preferred_element_type=jnp.float32).astype(jnp.bfloat16)
    owners = lists // block_count
    within = lists % block_count
    distance = owners - myself
    slot = jnp.where(distance < 0, distance + REACH, distance + REACH - 1)
    window_at = slot * block_count + within
    return dict(
        scaled=scaled,
        inverse=inverse,
        normed=normed,
        queries=projected[:, :model_width],
        own_pairs=projected[:, model_width:],
        window_at=window_at,
    )


def attach(unit, received, weight_in):
    points, model_width = unit["queries"].shape
    received = received.reshape(len(OFFSETS) * (points // BLK), BLK, model_width)
    fetched = jnp.take(received, unit["window_at"], axis=0).reshape(-1, model_width)
    fetched_pairs = jnp.dot(
        fetched, weight_in[:, model_width:], preferred_element_type=jnp.float32
    ).astype(jnp.bfloat16)
    unit["pairs"] = jnp.concatenate([unit["own_pairs"], fetched_pairs], 0)


def outgoing(unit, grad_key, grad_value, weight_in):
    points, model_width = unit["queries"].shape
    block_count = points // BLK
    grad_pairs = jnp.concatenate([grad_key, grad_value], 1)
    grad_remote = jnp.dot(
        grad_pairs[points:].astype(jnp.bfloat16),
        weight_in[:, model_width:].T,
        preferred_element_type=jnp.float32,
    ).reshape(-1, BLK, model_width)
    slots = lax.broadcasted_iota(jnp.int32, (len(OFFSETS) * block_count, 1, 1), 0)
    window_grads = sum(
        jnp.where(slots == unit["window_at"][entry], grad_remote[entry][None], 0.0)
        for entry in range(grad_remote.shape[0])
    )
    unit["own_grad"] = grad_pairs[:points]
    return window_grads.astype(jnp.bfloat16).reshape(len(OFFSETS), points, model_width)


def complete(unit, grad_out, grad_query, returned, weight_in, gain_row):
    grad_project = jnp.concatenate([grad_query, unit["own_grad"]], 1).astype(jnp.bfloat16)
    grad_normed = jnp.dot(grad_project, weight_in.T, preferred_element_type=jnp.float32)
    grad_normed = grad_normed + jnp.sum(returned.astype(jnp.float32), axis=0)
    return (
        grad_out.astype(jnp.float32)
        + norm_backward(grad_normed, unit["scaled"], unit["inverse"], gain_row)
    ).astype(jnp.bfloat16)


def shards(saved_inputs, project_in, project_out, norm_gains, neighbour_blocks, cotangent):
    sections = lax.axis_size("pipe")
    core = lax.axis_index("pipe")
    other = sections - 1 - core
    myself = lax.axis_index("space")
    micro_count = cotangent.shape[0]
    half = micro_count // sections
    model_width = cotangent.shape[2]

    def mine(array, whose):
        grouped = array.reshape((half, sections) + array.shape[1:])
        return lax.dynamic_index_in_dim(grouped, whose, 1, keepdims=False)

    local_lists = neighbour_blocks[0, :, 0, :]
    own = (
        mine(saved_inputs[0], core),
        mine(local_lists, core),
        project_in[0],
        project_out[0],
        norm_gains[0],
    )
    got = swap_cores(
        (
            mine(saved_inputs[0], other),
            mine(local_lists, other),
            project_in[0],
            project_out[0],
            norm_gains[0],
        )
    )
    params = [
        [pick(own_part, got_part, core, section) for own_part, got_part in zip(own, got)]
        for section in range(sections)
    ]
    cotangent_mine = mine(cotangent, core)
    order = [(section, j) for section in range(sections - 1, -1, -1) for j in range(half)]
    units = [
        prepare(params[section][0][j], params[section][1][j], params[section][2], params[section][4], myself)
        for section, j in order
    ]
    results = {}
    ids = iter(range(len(order) + 2))
    (first_received,) = fused_step((), [units[0]["normed"]], [False], next(ids))
    attach(units[0], first_received, params[order[0][0]][2])
    pending = None
    for step, (section, j) in enumerate(order):
        unit = units[step]
        _, _, weight_in, weight_out, gain_row = params[section]
        grad_out = cotangent_mine[j] if section == sections - 1 else results[(section + 1, j)]
        unit["grad_out"] = grad_out
        grad_attn = jnp.dot(grad_out, weight_out.T, preferred_element_type=jnp.float32).astype(
            jnp.bfloat16
        )
        payloads, spreads = [], []
        if pending is not None:
            payloads.append(pending[1])
            spreads.append(True)
        if step == 0:
            for later in units[1:]:
                payloads.append(later["normed"])
                spreads.append(False)
        outs = fused_step(
            (unit["queries"], unit["pairs"][:, :model_width], unit["pairs"][:, model_width:], grad_attn),
            payloads,
            spreads,
            next(ids),
        )
        grad_query, grad_key, grad_value = outs[:3]
        received = outs[3:]
        if pending is not None:
            done_step, _ = pending
            done_section, done_j = order[done_step]
            done_unit = units[done_step]
            results[(done_section, done_j)] = complete(
                done_unit,
                done_unit["grad_out"],
                done_unit["grad_query"],
                received[0],
                params[done_section][2],
                params[done_section][4],
            )
            received = received[1:]
        if step == 0:
            for later, (later_section, _), arrived in zip(units[1:], order[1:], received):
                attach(later, arrived, params[later_section][2])
        unit["grad_query"] = grad_query
        pending = (step, outgoing(unit, grad_key, grad_value, weight_in))
    done_step, window = pending
    done_section, done_j = order[done_step]
    done_unit = units[done_step]
    (returned,) = fused_step((), [window], [True], next(ids))
    results[(done_section, done_j)] = complete(
        done_unit,
        done_unit["grad_out"],
        done_unit["grad_query"],
        returned,
        params[done_section][2],
        params[done_section][4],
    )
    own_out = jnp.stack([pick(results[(0, j)], results[(1, j)], core, 0) for j in range(half)])
    other_out = swap_cores(
        jnp.stack([pick(results[(1, j)], results[(0, j)], core, 0) for j in range(half)])
    )
    grouped = jnp.stack([pick(own_out, other_out, core, parity) for parity in range(sections)], 1)
    return grouped.reshape((1, micro_count) + grouped.shape[2:])


def solution(mesh):
    return jax.shard_map(
        shards,
        mesh=mesh,
        in_specs=(
            P("pipe", None, "space", None),
            P("pipe", None, None),
            P("pipe", None, None),
            P("pipe", None),
            P("pipe", None, "space", None),
            P(None, "space", None),
        ),
        out_specs=P("pipe", None, "space", None),
        check_vma=False,
    )
```

```python
import functools

import jax
import jax.numpy as jnp
from jax import lax
from jax.experimental import pallas as pl
from jax.experimental.pallas import tpu as pltpu
from jax.sharding import PartitionSpec as P

HEADS = 32
HD = 16
BLK = 128
REACH = 2


epsilon = 1e-05


def shifted(x, axis, by):
    peers = lax.axis_size(axis)
    pairs = [(i, i + by) for i in range(peers) if 0 <= i + by < peers]
    return lax.ppermute(x, axis, pairs)


def normalize(points, gain_row):
    values = points.astype(jnp.float32)
    centre = jnp.mean(values, axis=-1, keepdims=True)
    spread = jnp.mean(jnp.square(values - centre), axis=-1, keepdims=True)
    inverse = lax.rsqrt(spread + epsilon)
    scaled = (values - centre) * inverse
    return (scaled, inverse, (scaled * gain_row).astype(jnp.bfloat16))


def norm_backward(grad_normed, scaled, inverse, gain_row):
    weighted = grad_normed * gain_row
    return inverse * (
        weighted
        - jnp.mean(weighted, axis=-1, keepdims=True)
        - scaled * jnp.mean(weighted * scaled, axis=-1, keepdims=True)
    )


MESH = pl.DeviceIdType.MESH
OFFSETS = [shift_by for shift_by in range(-REACH, REACH + 1) if shift_by != 0]


def attention_body(q_ref, k_ref, v_ref, g_ref, dq_ref, dk_ref, dv_ref, hooks):
    factor = HD ** (-0.5)
    group = 128
    per_group = group // HD
    nt = (((1,), (1,)), ((), ()))
    tn = (((0,), (0,)), ((), ()))
    head_of = lax.broadcasted_iota(jnp.int32, (1, group), 1) // HD
    dq_ref[...] = jnp.zeros_like(dq_ref)
    dk_ref[...] = jnp.zeros_like(dk_ref)
    dv_ref[...] = jnp.zeros_like(dv_ref)

    def head(index, carry):
        cols = pl.ds(pl.multiple_of((index // per_group) * group, group), group)
        mask = head_of == index % per_group
        q = q_ref[:, cols]
        k = k_ref[:, cols]
        v = v_ref[:, cols]
        g = g_ref[:, cols]
        qm = jnp.where(mask, q, jnp.zeros_like(q))
        km = jnp.where(mask, k, jnp.zeros_like(k))
        gm = jnp.where(mask, g, jnp.zeros_like(g))
        scores = lax.dot_general(qm, k, nt, preferred_element_type=jnp.float32) * factor
        top = jnp.max(scores, axis=-1, keepdims=True)
        exps = jnp.exp(scores - top)
        attention = exps * (1.0 / jnp.sum(exps, axis=-1, keepdims=True))
        grad_probs = lax.dot_general(gm, v, nt, preferred_element_type=jnp.float32)
        row = jnp.sum(attention * grad_probs, axis=-1, keepdims=True)
        grad_scores = (attention * (grad_probs - row) * factor).astype(jnp.bfloat16)
        dq_ref[:, cols] += jnp.dot(grad_scores, km, preferred_element_type=jnp.float32)
        dk_ref[:, cols] += lax.dot_general(grad_scores, qm, tn, preferred_element_type=jnp.float32)
        dv_ref[:, cols] += lax.dot_general(
            attention.astype(jnp.bfloat16), gm, tn, preferred_element_type=jnp.float32
        )
        return carry

    heads = q_ref.shape[1] // HD
    if not hooks:
        lax.fori_loop(0, heads, head, 0, unroll=4)
    else:
        begin = 0
        for edge in sorted(hooks):
            lax.fori_loop(begin, edge, head, 0, unroll=2)
            hooks[edge]()
            begin = edge
        lax.fori_loop(begin, heads, head, 0, unroll=2)


def exchange_start(spreads, payload_refs, out_refs, send_sems, recv_sems):
    core = lax.axis_index("pipe")
    me = lax.axis_index("space")
    peers = lax.axis_size("space")
    barrier = pltpu.get_barrier_semaphore()

    def exists(shift_by):
        return (me + shift_by >= 0) & (me + shift_by < peers)

    def slot(shift_by):
        return OFFSETS.index(shift_by)

    for shift_by in OFFSETS:

        @pl.when(exists(shift_by))
        def _():
            pl.semaphore_signal(barrier, 1, device_id=(core, me + shift_by), device_id_type=MESH)

    pl.semaphore_wait(barrier, sum(jnp.where(exists(shift_by), 1, 0) for shift_by in OFFSETS))

    def describe(which, source, landing, shift_by):
        return pltpu.make_async_remote_copy(
            src_ref=source,
            dst_ref=out_refs[which].at[landing],
            send_sem=send_sems.at[which, landing],
            recv_sem=recv_sems.at[which, landing],
            device_id=(core, me + shift_by),
            device_id_type=MESH,
        )

    def arrival(which, landing):
        return describe(which, out_refs[which].at[landing], landing, OFFSETS[landing])

    direct = []
    relayed = []
    relaying = not any(spreads)
    for which, spread in enumerate(spreads):
        x_ref = payload_refs[which]
        targets = OFFSETS if spread or not relaying else [-1, 1]
        for shift_by in targets:
            source = x_ref.at[slot(shift_by)] if spread else x_ref
            copy = describe(which, source, slot(-shift_by), shift_by)
            direct.append((copy, exists(shift_by)))

            @pl.when(exists(shift_by))
            def _():
                copy.start()

        for shift_by in OFFSETS:

            @pl.when(jnp.logical_not(exists(shift_by)))
            def _():
                out_refs[which][slot(shift_by)] = jnp.zeros(
                    out_refs[which].shape[1:], out_refs[which].dtype
                )

        if relaying and not spread:
            for shift_by in (-1, 1):
                forward = describe(
                    which, out_refs[which].at[slot(-shift_by)], slot(-2 * shift_by), shift_by
                )
                relayed.append((which, shift_by, forward, exists(shift_by) & exists(-shift_by)))

    def relay(whiches):
        chosen = [entry for entry in relayed if entry[0] in whiches]
        for which, shift_by, forward, valid in chosen:

            @pl.when(exists(-shift_by))
            def _():
                arrival(which, slot(-shift_by)).wait_recv()

        for which, shift_by, forward, valid in chosen:

            @pl.when(valid)
            def _():
                forward.start()

    def finish():
        for copy, valid in direct:

            @pl.when(valid)
            def _():
                copy.wait_send()

        for which, shift_by, forward, valid in relayed:

            @pl.when(valid)
            def _():
                forward.wait_send()

        relayed_slots = {(which, slot(-shift_by)) for which, shift_by, _, _ in relayed}
        for which in range(len(spreads)):
            for landing, shift_by in enumerate(OFFSETS):
                if (which, landing) in relayed_slots:
                    continue

                @pl.when(exists(shift_by))
                def _():
                    arrival(which, landing).wait_recv()

    return relay, finish


def fused_kernel(spreads, with_attention, projection, *refs):
    count = len(spreads)
    inputs = 4 if with_attention else 0
    outputs = 3 if with_attention else 0
    extra_in = len(projection) + (max(projection) + 1 if projection else 0)
    extra_out = 1 if projection else 0
    position = 0

    def take(number):
        nonlocal position
        taken = refs[position : position + number]
        position += number
        return taken

    attention_in = take(inputs)
    payload_refs = take(count)
    project_in = take(extra_in)
    attention_out = take(outputs)
    out_refs = take(count)
    project_out = take(extra_out)
    send_sems, recv_sems = take(2)
    relay, finish = exchange_start(spreads, payload_refs, out_refs, send_sems, recv_sems)
    if projection:
        rows_refs = project_in[: len(projection)]
        weight_refs = project_in[len(projection) :]
        for unit, chosen in enumerate(projection):
            project_out[0][unit] = jnp.dot(
                rows_refs[unit][...], weight_refs[chosen][...], preferred_element_type=jnp.float32
            ).astype(project_out[0].dtype)
    if with_attention:
        hooks = {}
        if not any(spreads):
            heads = attention_in[0].shape[1] // HD
            for which in range(count):
                edge = (which + 1) * heads // (count + 1)
                hooks[edge] = functools.partial(relay, [which])
        attention_body(*attention_in, *attention_out, hooks)
    else:
        relay(list(range(count)))
    finish()


def fused_step(attention_args, payloads, spreads, collective_id, projection=None):
    vmem = pl.BlockSpec(memory_space=pltpu.VMEM)
    out_shapes = []
    flops = 0
    if attention_args:
        queries, key_rows, value_rows, grad_attn = attention_args
        rows, width = queries.shape
        keys = key_rows.shape[0]
        out_shapes = [
            jax.ShapeDtypeStruct((rows, width), jnp.float32),
            jax.ShapeDtypeStruct((keys, width), jnp.float32),
            jax.ShapeDtypeStruct((keys, width), jnp.float32),
        ]
        flops = 2 * 5 * rows * keys * width * (128 // HD)
    for payload, spread in zip(payloads, spreads):
        shape = payload.shape[1:] if spread else payload.shape
        out_shapes.append(jax.ShapeDtypeStruct((len(OFFSETS),) + shape, payload.dtype))
    moved = sum(len(OFFSETS) * x.size * x.dtype.itemsize for x in payloads)
    project_args = []
    chosen = ()
    if projection is not None:
        rows_list, weights, chosen = projection
        chosen = tuple(chosen)
        project_args = list(rows_list) + list(weights)
        rows, width = rows_list[0].shape
        out_shapes.append(
            jax.ShapeDtypeStruct((len(rows_list), rows, weights[0].shape[1]), jnp.bfloat16)
        )
        flops += 2 * len(rows_list) * rows * width * weights[0].shape[1]
    outs = pl.pallas_call(
        functools.partial(fused_kernel, tuple(spreads), bool(attention_args), chosen),
        out_shape=out_shapes,
        in_specs=[vmem] * (len(attention_args) + len(payloads) + len(project_args)),
        out_specs=[vmem] * len(out_shapes),
        scratch_shapes=[
            pltpu.SemaphoreType.DMA((len(payloads), len(OFFSETS))),
            pltpu.SemaphoreType.DMA((len(payloads), len(OFFSETS))),
        ],
        compiler_params=pltpu.CompilerParams(
            collective_id=collective_id,
            has_side_effects=True,
            vmem_limit_bytes=48 * 1024 * 1024,
        ),
        cost_estimate=pl.CostEstimate(
            flops=flops, transcendentals=flops // 160, bytes_accessed=moved + 1
        ),
    )(*attention_args, *payloads, *project_args)
    return list(outs)


def swap_cores(value):
    return lax.ppermute(value, "pipe", [(0, 1), (1, 0)])


def pick(own, other, core, section):
    return jnp.where(core == section, own, other)


def prepare(rows, lists, weight_in, gain_row, myself):
    points, model_width = rows.shape
    block_count = points // BLK
    scaled, inverse, normed = normalize(rows, gain_row)
    owners = lists // block_count
    within = lists % block_count
    distance = owners - myself
    slot = jnp.where(distance < 0, distance + REACH, distance + REACH - 1)
    window_at = slot * block_count + within
    return dict(
        scaled=scaled,
        inverse=inverse,
        normed=normed,
        window_at=window_at,
    )


def attach(unit, received, weight_in):
    points, model_width = unit["normed"].shape
    received = received.reshape(len(OFFSETS) * (points // BLK), BLK, model_width)
    fetched = jnp.take(received, unit["window_at"], axis=0).reshape(-1, model_width)
    fetched_pairs = jnp.dot(
        fetched, weight_in[:, model_width:], preferred_element_type=jnp.float32
    ).astype(jnp.bfloat16)
    unit["pairs"] = jnp.concatenate([unit["own_pairs"], fetched_pairs], 0)


def outgoing(unit, grad_key, grad_value, weight_in):
    points, model_width = unit["queries"].shape
    block_count = points // BLK
    grad_pairs = jnp.concatenate([grad_key, grad_value], 1)
    grad_remote = jnp.dot(
        grad_pairs[points:].astype(jnp.bfloat16),
        weight_in[:, model_width:].T,
        preferred_element_type=jnp.float32,
    ).reshape(-1, BLK, model_width)
    slots = lax.broadcasted_iota(jnp.int32, (len(OFFSETS) * block_count, 1, 1), 0)
    window_grads = sum(
        jnp.where(slots == unit["window_at"][entry], grad_remote[entry][None], 0.0)
        for entry in range(grad_remote.shape[0])
    )
    unit["own_grad"] = grad_pairs[:points]
    return window_grads.astype(jnp.bfloat16).reshape(len(OFFSETS), points, model_width)


def complete(unit, grad_out, grad_query, returned, weight_in, gain_row):
    grad_project = jnp.concatenate([grad_query, unit["own_grad"]], 1).astype(jnp.bfloat16)
    grad_normed = jnp.dot(grad_project, weight_in.T, preferred_element_type=jnp.float32)
    grad_normed = grad_normed + jnp.sum(returned.astype(jnp.float32), axis=0)
    return (
        grad_out.astype(jnp.float32)
        + norm_backward(grad_normed, unit["scaled"], unit["inverse"], gain_row)
    ).astype(jnp.bfloat16)


def shards(saved_inputs, project_in, project_out, norm_gains, neighbour_blocks, cotangent):
    sections = lax.axis_size("pipe")
    core = lax.axis_index("pipe")
    other = sections - 1 - core
    myself = lax.axis_index("space")
    micro_count = cotangent.shape[0]
    half = micro_count // sections
    model_width = cotangent.shape[2]

    def mine(array, whose):
        grouped = array.reshape((half, sections) + array.shape[1:])
        return lax.dynamic_index_in_dim(grouped, whose, 1, keepdims=False)

    local_lists = neighbour_blocks[0, :, 0, :]
    own = (
        mine(saved_inputs[0], core),
        mine(local_lists, core),
        project_in[0],
        project_out[0],
        norm_gains[0],
    )
    got = swap_cores(
        (
            mine(saved_inputs[0], other),
            mine(local_lists, other),
            project_in[0],
            project_out[0],
            norm_gains[0],
        )
    )
    params = [
        [pick(own_part, got_part, core, section) for own_part, got_part in zip(own, got)]
        for section in range(sections)
    ]
    cotangent_mine = mine(cotangent, core)
    order = [(section, j) for section in range(sections - 1, -1, -1) for j in range(half)]
    units = [
        prepare(params[section][0][j], params[section][1][j], params[section][2], params[section][4], myself)
        for section, j in order
    ]
    results = {}
    ids = iter(range(len(order) + 2))
    first_received, projected = fused_step(
        (),
        [units[0]["normed"]],
        [False],
        next(ids),
        projection=(
            [unit["normed"] for unit in units],
            [params[section][2] for section in range(sections)],
            [section for section, _ in order],
        ),
    )
    for unit, rows in zip(units, projected):
        unit["queries"] = rows[:, :model_width]
        unit["own_pairs"] = rows[:, model_width:]
    attach(units[0], first_received, params[order[0][0]][2])
    pending = None
    for step, (section, j) in enumerate(order):
        unit = units[step]
        _, _, weight_in, weight_out, gain_row = params[section]
        grad_out = cotangent_mine[j] if section == sections - 1 else results[(section + 1, j)]
        unit["grad_out"] = grad_out
        grad_attn = jnp.dot(grad_out, weight_out.T, preferred_element_type=jnp.float32).astype(
            jnp.bfloat16
        )
        payloads, spreads = [], []
        if pending is not None:
            payloads.append(pending[1])
            spreads.append(True)
        if step == 0:
            for later in units[1:]:
                payloads.append(later["normed"])
                spreads.append(False)
        outs = fused_step(
            (unit["queries"], unit["pairs"][:, :model_width], unit["pairs"][:, model_width:], grad_attn),
            payloads,
            spreads,
            next(ids),
        )
        grad_query, grad_key, grad_value = outs[:3]
        received = outs[3:]
        if pending is not None:
            done_step, _ = pending
            done_section, done_j = order[done_step]
            done_unit = units[done_step]
            results[(done_section, done_j)] = complete(
                done_unit,
                done_unit["grad_out"],
                done_unit["grad_query"],
                received[0],
                params[done_section][2],
                params[done_section][4],
            )
            received = received[1:]
        if step == 0:
            for later, (later_section, _), arrived in zip(units[1:], order[1:], received):
                attach(later, arrived, params[later_section][2])
        unit["grad_query"] = grad_query
        pending = (step, outgoing(unit, grad_key, grad_value, weight_in))
    done_step, window = pending
    done_section, done_j = order[done_step]
    done_unit = units[done_step]
    (returned,) = fused_step((), [window], [True], next(ids))
    results[(done_section, done_j)] = complete(
        done_unit,
        done_unit["grad_out"],
        done_unit["grad_query"],
        returned,
        params[done_section][2],
        params[done_section][4],
    )
    own_out = jnp.stack([pick(results[(0, j)], results[(1, j)], core, 0) for j in range(half)])
    other_out = swap_cores(
        jnp.stack([pick(results[(1, j)], results[(0, j)], core, 0) for j in range(half)])
    )
    grouped = jnp.stack([pick(own_out, other_out, core, parity) for parity in range(sections)], 1)
    return grouped.reshape((1, micro_count) + grouped.shape[2:])


def solution(mesh):
    return jax.shard_map(
        shards,
        mesh=mesh,
        in_specs=(
            P("pipe", None, "space", None),
            P("pipe", None, None),
            P("pipe", None, None),
            P("pipe", None),
            P("pipe", None, "space", None),
            P(None, "space", None),
        ),
        out_specs=P("pipe", None, "space", None),
        check_vma=False,
    )
```

```python
import functools

import jax
import jax.numpy as jnp
from jax import lax
from jax.experimental import pallas as pl
from jax.experimental.pallas import tpu as pltpu
from jax.sharding import PartitionSpec as P

HEADS = 32
HD = 16
BLK = 128
REACH = 2


epsilon = 1e-05


def shifted(x, axis, by):
    peers = lax.axis_size(axis)
    pairs = [(i, i + by) for i in range(peers) if 0 <= i + by < peers]
    return lax.ppermute(x, axis, pairs)


def normalize(points, gain_row):
    values = points.astype(jnp.float32)
    centre = jnp.mean(values, axis=-1, keepdims=True)
    spread = jnp.mean(jnp.square(values - centre), axis=-1, keepdims=True)
    inverse = lax.rsqrt(spread + epsilon)
    scaled = (values - centre) * inverse
    return (scaled, inverse, (scaled * gain_row).astype(jnp.bfloat16))


def norm_backward(grad_normed, scaled, inverse, gain_row):
    weighted = grad_normed * gain_row
    return inverse * (
        weighted
        - jnp.mean(weighted, axis=-1, keepdims=True)
        - scaled * jnp.mean(weighted * scaled, axis=-1, keepdims=True)
    )


MESH = pl.DeviceIdType.MESH
OFFSETS = [shift_by for shift_by in range(-REACH, REACH + 1) if shift_by != 0]


def attention_body(q_ref, k_ref, v_ref, g_ref, dq_ref, dk_ref, dv_ref, hooks):
    factor = HD ** (-0.5)
    group = 128
    per_group = group // HD
    nt = (((1,), (1,)), ((), ()))
    tn = (((0,), (0,)), ((), ()))
    head_of = lax.broadcasted_iota(jnp.int32, (1, group), 1) // HD
    dq_ref[...] = jnp.zeros_like(dq_ref)
    dk_ref[...] = jnp.zeros_like(dk_ref)
    dv_ref[...] = jnp.zeros_like(dv_ref)

    def head(index, carry):
        cols = pl.ds(pl.multiple_of((index // per_group) * group, group), group)
        mask = head_of == index % per_group
        q = q_ref[:, cols]
        k = k_ref[:, cols]
        v = v_ref[:, cols]
        g = g_ref[:, cols]
        qm = jnp.where(mask, q, jnp.zeros_like(q))
        km = jnp.where(mask, k, jnp.zeros_like(k))
        gm = jnp.where(mask, g, jnp.zeros_like(g))
        scores = lax.dot_general(qm, k, nt, preferred_element_type=jnp.float32) * factor
        top = jnp.max(scores, axis=-1, keepdims=True)
        exps = jnp.exp(scores - top)
        attention = exps * (1.0 / jnp.sum(exps, axis=-1, keepdims=True))
        grad_probs = lax.dot_general(gm, v, nt, preferred_element_type=jnp.float32)
        row = jnp.sum(attention * grad_probs, axis=-1, keepdims=True)
        grad_scores = (attention * (grad_probs - row) * factor).astype(jnp.bfloat16)
        dq_ref[:, cols] += jnp.dot(grad_scores, km, preferred_element_type=jnp.float32)
        dk_ref[:, cols] += lax.dot_general(grad_scores, qm, tn, preferred_element_type=jnp.float32)
        dv_ref[:, cols] += lax.dot_general(
            attention.astype(jnp.bfloat16), gm, tn, preferred_element_type=jnp.float32
        )
        return carry

    heads = q_ref.shape[1] // HD
    if not hooks:
        lax.fori_loop(0, heads, head, 0, unroll=4)
    else:
        begin = 0
        for edge in sorted(hooks):
            lax.fori_loop(begin, edge, head, 0, unroll=4)
            hooks[edge]()
            begin = edge
        lax.fori_loop(begin, heads, head, 0, unroll=4)


def exchange_start(spreads, payload_refs, out_refs, send_sems, recv_sems):
    core = lax.axis_index("pipe")
    me = lax.axis_index("space")
    peers = lax.axis_size("space")
    barrier = pltpu.get_barrier_semaphore()

    def exists(shift_by):
        return (me + shift_by >= 0) & (me + shift_by < peers)

    def slot(shift_by):
        return OFFSETS.index(shift_by)

    for shift_by in OFFSETS:

        @pl.when(exists(shift_by))
        def _():
            pl.semaphore_signal(barrier, 1, device_id=(core, me + shift_by), device_id_type=MESH)

    pl.semaphore_wait(barrier, sum(jnp.where(exists(shift_by), 1, 0) for shift_by in OFFSETS))

    def describe(which, source, landing, shift_by):
        return pltpu.make_async_remote_copy(
            src_ref=source,
            dst_ref=out_refs[which].at[landing],
            send_sem=send_sems.at[which, landing],
            recv_sem=recv_sems.at[which, landing],
            device_id=(core, me + shift_by),
            device_id_type=MESH,
        )

    def arrival(which, landing):
        return describe(which, out_refs[which].at[landing], landing, OFFSETS[landing])

    direct = []
    relayed = []
    relaying = not any(spreads)
    for which, spread in enumerate(spreads):
        x_ref = payload_refs[which]
        targets = OFFSETS if spread or not relaying else [-1, 1]
        for shift_by in targets:
            source = x_ref.at[slot(shift_by)] if spread else x_ref
            copy = describe(which, source, slot(-shift_by), shift_by)
            direct.append((copy, exists(shift_by)))

            @pl.when(exists(shift_by))
            def _():
                copy.start()

        for shift_by in OFFSETS:

            @pl.when(jnp.logical_not(exists(shift_by)))
            def _():
                out_refs[which][slot(shift_by)] = jnp.zeros(
                    out_refs[which].shape[1:], out_refs[which].dtype
                )

        if relaying and not spread:
            for shift_by in (-1, 1):
                forward = describe(
                    which, out_refs[which].at[slot(-shift_by)], slot(-2 * shift_by), shift_by
                )
                relayed.append((which, shift_by, forward, exists(shift_by) & exists(-shift_by)))

    def relay(whiches):
        chosen = [entry for entry in relayed if entry[0] in whiches]
        for which, shift_by, forward, valid in chosen:

            @pl.when(exists(-shift_by))
            def _():
                arrival(which, slot(-shift_by)).wait_recv()

        for which, shift_by, forward, valid in chosen:

            @pl.when(valid)
            def _():
                forward.start()

    def finish():
        for copy, valid in direct:

            @pl.when(valid)
            def _():
                copy.wait_send()

        for which, shift_by, forward, valid in relayed:

            @pl.when(valid)
            def _():
                forward.wait_send()

        relayed_slots = {(which, slot(-shift_by)) for which, shift_by, _, _ in relayed}
        for which in range(len(spreads)):
            for landing, shift_by in enumerate(OFFSETS):
                if (which, landing) in relayed_slots:
                    continue

                @pl.when(exists(shift_by))
                def _():
                    arrival(which, landing).wait_recv()

    return relay, finish


def fused_kernel(spreads, with_attention, *refs):
    count = len(spreads)
    inputs = 4 if with_attention else 0
    outputs = 3 if with_attention else 0
    attention_in = refs[:inputs]
    payload_refs = refs[inputs : inputs + count]
    attention_out = refs[inputs + count : inputs + count + outputs]
    out_refs = refs[inputs + count + outputs : inputs + 2 * count + outputs]
    send_sems, recv_sems = refs[inputs + 2 * count + outputs :]
    relay, finish = exchange_start(spreads, payload_refs, out_refs, send_sems, recv_sems)
    if with_attention:
        hooks = {}
        if not any(spreads):
            heads = attention_in[0].shape[1] // HD
            hooks[heads // 2] = functools.partial(relay, list(range(count)))
        attention_body(*attention_in, *attention_out, hooks)
    else:
        relay(list(range(count)))
    finish()


def fused_step(attention_args, payloads, spreads, collective_id):
    vmem = pl.BlockSpec(memory_space=pltpu.VMEM)
    out_shapes = []
    flops = 0
    if attention_args:
        queries, key_rows, value_rows, grad_attn = attention_args
        rows, width = queries.shape
        keys = key_rows.shape[0]
        out_shapes = [
            jax.ShapeDtypeStruct((rows, width), jnp.float32),
            jax.ShapeDtypeStruct((keys, width), jnp.float32),
            jax.ShapeDtypeStruct((keys, width), jnp.float32),
        ]
        flops = 2 * 5 * rows * keys * width * (128 // HD)
    for payload, spread in zip(payloads, spreads):
        shape = payload.shape[1:] if spread else payload.shape
        out_shapes.append(jax.ShapeDtypeStruct((len(OFFSETS),) + shape, payload.dtype))
    moved = sum(len(OFFSETS) * x.size * x.dtype.itemsize for x in payloads)
    outs = pl.pallas_call(
        functools.partial(fused_kernel, tuple(spreads), bool(attention_args)),
        out_shape=out_shapes,
        in_specs=[vmem] * (len(attention_args) + len(payloads)),
        out_specs=[vmem] * len(out_shapes),
        scratch_shapes=[
            pltpu.SemaphoreType.DMA((len(payloads), len(OFFSETS))),
            pltpu.SemaphoreType.DMA((len(payloads), len(OFFSETS))),
        ],
        compiler_params=pltpu.CompilerParams(
            collective_id=collective_id,
            has_side_effects=True,
            vmem_limit_bytes=48 * 1024 * 1024,
        ),
        cost_estimate=pl.CostEstimate(
            flops=flops, transcendentals=flops // 160, bytes_accessed=moved + 1
        ),
    )(*attention_args, *payloads)
    return list(outs)


def swap_cores(value):
    return lax.ppermute(value, "pipe", [(0, 1), (1, 0)])


def pick(own, other, core, section):
    return jnp.where(core == section, own, other)


def prepare(rows, lists, weight_in, gain_row, myself):
    points, model_width = rows.shape
    block_count = points // BLK
    scaled, inverse, normed = normalize(rows, gain_row)
    projected = jnp.dot(normed, weight_in, preferred_element_type=jnp.float32).astype(jnp.bfloat16)
    owners = lists // block_count
    within = lists % block_count
    distance = owners - myself
    slot = jnp.where(distance < 0, distance + REACH, distance + REACH - 1)
    window_at = slot * block_count + within
    return dict(
        scaled=scaled,
        inverse=inverse,
        normed=normed,
        queries=projected[:, :model_width],
        own_pairs=projected[:, model_width:],
        window_at=window_at,
    )


def attach(unit, received, weight_in):
    points, model_width = unit["queries"].shape
    received = received.reshape(len(OFFSETS) * (points // BLK), BLK, model_width)
    fetched = jnp.take(received, unit["window_at"], axis=0).reshape(-1, model_width)
    fetched_pairs = jnp.dot(
        fetched, weight_in[:, model_width:], preferred_element_type=jnp.float32
    ).astype(jnp.bfloat16)
    unit["pairs"] = jnp.concatenate([unit["own_pairs"], fetched_pairs], 0)


def outgoing(unit, grad_key, grad_value, weight_in):
    points, model_width = unit["queries"].shape
    block_count = points // BLK
    grad_pairs = jnp.concatenate([grad_key, grad_value], 1)
    grad_remote = jnp.dot(
        grad_pairs[points:].astype(jnp.bfloat16),
        weight_in[:, model_width:].T,
        preferred_element_type=jnp.float32,
    ).reshape(-1, BLK, model_width)
    slots = lax.broadcasted_iota(jnp.int32, (len(OFFSETS) * block_count, 1, 1), 0)
    window_grads = sum(
        jnp.where(slots == unit["window_at"][entry], grad_remote[entry][None], 0.0)
        for entry in range(grad_remote.shape[0])
    )
    unit["own_grad"] = grad_pairs[:points]
    return window_grads.astype(jnp.bfloat16).reshape(len(OFFSETS), points, model_width)


def complete(unit, grad_out, grad_query, returned, weight_in, gain_row):
    grad_project = jnp.concatenate([grad_query, unit["own_grad"]], 1).astype(jnp.bfloat16)
    grad_normed = jnp.dot(grad_project, weight_in.T, preferred_element_type=jnp.float32)
    grad_normed = grad_normed + jnp.sum(returned.astype(jnp.float32), axis=0)
    return (
        grad_out.astype(jnp.float32)
        + norm_backward(grad_normed, unit["scaled"], unit["inverse"], gain_row)
    ).astype(jnp.bfloat16)


def shards(saved_inputs, project_in, project_out, norm_gains, neighbour_blocks, cotangent):
    sections = lax.axis_size("pipe")
    core = lax.axis_index("pipe")
    other = sections - 1 - core
    myself = lax.axis_index("space")
    micro_count = cotangent.shape[0]
    half = micro_count // sections
    model_width = cotangent.shape[2]

    def mine(array, whose):
        grouped = array.reshape((half, sections) + array.shape[1:])
        return lax.dynamic_index_in_dim(grouped, whose, 1, keepdims=False)

    local_lists = neighbour_blocks[0, :, 0, :]
    own = (
        mine(saved_inputs[0], core),
        mine(local_lists, core),
        project_in[0],
        project_out[0],
        norm_gains[0],
    )
    got = swap_cores(
        (
            mine(saved_inputs[0], other),
            mine(local_lists, other),
            project_in[0],
            project_out[0],
            norm_gains[0],
        )
    )
    params = [
        [pick(own_part, got_part, core, section) for own_part, got_part in zip(own, got)]
        for section in range(sections)
    ]
    cotangent_mine = mine(cotangent, core)
    order = [(section, j) for section in range(sections - 1, -1, -1) for j in range(half)]
    units = [
        prepare(params[section][0][j], params[section][1][j], params[section][2], params[section][4], myself)
        for section, j in order
    ]
    results = {}
    ids = iter(range(len(order) + 2))
    (first_received,) = fused_step((), [units[0]["normed"]], [False], next(ids))
    attach(units[0], first_received, params[order[0][0]][2])
    pending = None
    for step, (section, j) in enumerate(order):
        unit = units[step]
        _, _, weight_in, weight_out, gain_row = params[section]
        grad_out = cotangent_mine[j] if section == sections - 1 else results[(section + 1, j)]
        unit["grad_out"] = grad_out
        grad_attn = jnp.dot(grad_out, weight_out.T, preferred_element_type=jnp.float32).astype(
            jnp.bfloat16
        )
        payloads, spreads = [], []
        if pending is not None:
            payloads.append(pending[1])
            spreads.append(True)
        if step == 0:
            for later in units[1:]:
                payloads.append(later["normed"])
                spreads.append(False)
        outs = fused_step(
            (unit["queries"], unit["pairs"][:, :model_width], unit["pairs"][:, model_width:], grad_attn),
            payloads,
            spreads,
            next(ids),
        )
        grad_query, grad_key, grad_value = outs[:3]
        received = outs[3:]
        if pending is not None:
            done_step, _ = pending
            done_section, done_j = order[done_step]
            done_unit = units[done_step]
            results[(done_section, done_j)] = complete(
                done_unit,
                done_unit["grad_out"],
                done_unit["grad_query"],
                received[0],
                params[done_section][2],
                params[done_section][4],
            )
            received = received[1:]
        if step == 0:
            for later, (later_section, _), arrived in zip(units[1:], order[1:], received):
                attach(later, arrived, params[later_section][2])
        unit["grad_query"] = grad_query
        pending = (step, outgoing(unit, grad_key, grad_value, weight_in))
    done_step, window = pending
    done_section, done_j = order[done_step]
    done_unit = units[done_step]
    (returned,) = fused_step((), [window], [True], next(ids))
    results[(done_section, done_j)] = complete(
        done_unit,
        done_unit["grad_out"],
        done_unit["grad_query"],
        returned,
        params[done_section][2],
        params[done_section][4],
    )
    own_out = jnp.stack([pick(results[(0, j)], results[(1, j)], core, 0) for j in range(half)])
    other_out = swap_cores(
        jnp.stack([pick(results[(1, j)], results[(0, j)], core, 0) for j in range(half)])
    )
    grouped = jnp.stack([pick(own_out, other_out, core, parity) for parity in range(sections)], 1)
    return grouped.reshape((1, micro_count) + grouped.shape[2:])


def solution(mesh):
    return jax.shard_map(
        shards,
        mesh=mesh,
        in_specs=(
            P("pipe", None, "space", None),
            P("pipe", None, None),
            P("pipe", None, None),
            P("pipe", None),
            P("pipe", None, "space", None),
            P(None, "space", None),
        ),
        out_specs=P("pipe", None, "space", None),
        check_vma=False,
    )
```

```python
import functools

import jax
import jax.numpy as jnp
from jax import lax
from jax.experimental import pallas as pl
from jax.experimental.pallas import tpu as pltpu
from jax.sharding import PartitionSpec as P

HEADS = 32
HD = 16
BLK = 128
REACH = 2


epsilon = 1e-05


def shifted(x, axis, by):
    peers = lax.axis_size(axis)
    pairs = [(i, i + by) for i in range(peers) if 0 <= i + by < peers]
    return lax.ppermute(x, axis, pairs)


def normalize(points, gain_row):
    values = points.astype(jnp.float32)
    centre = jnp.mean(values, axis=-1, keepdims=True)
    spread = jnp.mean(jnp.square(values - centre), axis=-1, keepdims=True)
    inverse = lax.rsqrt(spread + epsilon)
    scaled = (values - centre) * inverse
    return (scaled, inverse, (scaled * gain_row).astype(jnp.bfloat16))


def norm_backward(grad_normed, scaled, inverse, gain_row):
    weighted = grad_normed * gain_row
    return inverse * (
        weighted
        - jnp.mean(weighted, axis=-1, keepdims=True)
        - scaled * jnp.mean(weighted * scaled, axis=-1, keepdims=True)
    )


MESH = pl.DeviceIdType.MESH
OFFSETS = [shift_by for shift_by in range(-REACH, REACH + 1) if shift_by != 0]


def attention_body(q_ref, k_ref, v_ref, g_ref, dq_ref, dk_ref, dv_ref, hooks):
    factor = HD ** (-0.5)
    group = 128
    per_group = group // HD
    nt = (((1,), (1,)), ((), ()))
    tn = (((0,), (0,)), ((), ()))
    head_of = lax.broadcasted_iota(jnp.int32, (1, group), 1) // HD
    dq_ref[...] = jnp.zeros_like(dq_ref)
    dk_ref[...] = jnp.zeros_like(dk_ref)
    dv_ref[...] = jnp.zeros_like(dv_ref)

    def head(index, carry):
        cols = pl.ds(pl.multiple_of((index // per_group) * group, group), group)
        mask = head_of == index % per_group
        q = q_ref[:, cols]
        k = k_ref[:, cols]
        v = v_ref[:, cols]
        g = g_ref[:, cols]
        qm = jnp.where(mask, q, jnp.zeros_like(q))
        km = jnp.where(mask, k, jnp.zeros_like(k))
        gm = jnp.where(mask, g, jnp.zeros_like(g))
        scores = lax.dot_general(qm, k, nt, preferred_element_type=jnp.float32) * factor
        top = jnp.max(scores, axis=-1, keepdims=True)
        exps = jnp.exp(scores - top)
        attention = exps * (1.0 / jnp.sum(exps, axis=-1, keepdims=True))
        grad_probs = lax.dot_general(gm, v, nt, preferred_element_type=jnp.float32)
        row = jnp.sum(attention * grad_probs, axis=-1, keepdims=True)
        grad_scores = (attention * (grad_probs - row) * factor).astype(jnp.bfloat16)
        dq_ref[:, cols] += jnp.dot(grad_scores, km, preferred_element_type=jnp.float32)
        dk_ref[:, cols] += lax.dot_general(grad_scores, qm, tn, preferred_element_type=jnp.float32)
        dv_ref[:, cols] += lax.dot_general(
            attention.astype(jnp.bfloat16), gm, tn, preferred_element_type=jnp.float32
        )
        return carry

    heads = q_ref.shape[1] // HD
    if not hooks:
        lax.fori_loop(0, heads, head, 0, unroll=4)
    else:
        begin = 0
        for edge in sorted(hooks):
            lax.fori_loop(begin, edge, head, 0, unroll=4)
            hooks[edge]()
            begin = edge
        lax.fori_loop(begin, heads, head, 0, unroll=4)


def exchange_start(spreads, payload_refs, out_refs, send_sems, recv_sems):
    core = lax.axis_index("pipe")
    me = lax.axis_index("space")
    peers = lax.axis_size("space")
    barrier = pltpu.get_barrier_semaphore()

    def exists(shift_by):
        return (me + shift_by >= 0) & (me + shift_by < peers)

    def slot(shift_by):
        return OFFSETS.index(shift_by)

    for shift_by in OFFSETS:

        @pl.when(exists(shift_by))
        def _():
            pl.semaphore_signal(barrier, 1, device_id=(core, me + shift_by), device_id_type=MESH)

    pl.semaphore_wait(barrier, sum(jnp.where(exists(shift_by), 1, 0) for shift_by in OFFSETS))

    def describe(which, source, landing, shift_by):
        return pltpu.make_async_remote_copy(
            src_ref=source,
            dst_ref=out_refs[which].at[landing],
            send_sem=send_sems.at[which, landing],
            recv_sem=recv_sems.at[which, landing],
            device_id=(core, me + shift_by),
            device_id_type=MESH,
        )

    def arrival(which, landing):
        return describe(which, out_refs[which].at[landing], landing, OFFSETS[landing])

    direct = []
    relayed = []
    relaying = not any(spreads)
    for which, spread in enumerate(spreads):
        x_ref = payload_refs[which]
        targets = OFFSETS if spread or not relaying else [-1, 1]
        for shift_by in targets:
            source = x_ref.at[slot(shift_by)] if spread else x_ref
            copy = describe(which, source, slot(-shift_by), shift_by)
            direct.append((copy, exists(shift_by)))

            @pl.when(exists(shift_by))
            def _():
                copy.start()

        for shift_by in OFFSETS:

            @pl.when(jnp.logical_not(exists(shift_by)))
            def _():
                out_refs[which][slot(shift_by)] = jnp.zeros(
                    out_refs[which].shape[1:], out_refs[which].dtype
                )

        if relaying and not spread:
            for shift_by in (-1, 1):
                forward = describe(
                    which, out_refs[which].at[slot(-shift_by)], slot(-2 * shift_by), shift_by
                )
                relayed.append((which, shift_by, forward, exists(shift_by) & exists(-shift_by)))

    def relay(whiches):
        chosen = [entry for entry in relayed if entry[0] in whiches]
        for which, shift_by, forward, valid in chosen:

            @pl.when(exists(-shift_by))
            def _():
                arrival(which, slot(-shift_by)).wait_recv()

        for which, shift_by, forward, valid in chosen:

            @pl.when(valid)
            def _():
                forward.start()

    def finish():
        for copy, valid in direct:

            @pl.when(valid)
            def _():
                copy.wait_send()

        for which, shift_by, forward, valid in relayed:

            @pl.when(valid)
            def _():
                forward.wait_send()

        relayed_slots = {(which, slot(-shift_by)) for which, shift_by, _, _ in relayed}
        for which in range(len(spreads)):
            for landing, shift_by in enumerate(OFFSETS):
                if (which, landing) in relayed_slots:
                    continue

                @pl.when(exists(shift_by))
                def _():
                    arrival(which, landing).wait_recv()

    return relay, finish


def fused_kernel(spreads, with_attention, *refs):
    count = len(spreads)
    inputs = 4 if with_attention else 0
    outputs = 3 if with_attention else 0
    attention_in = refs[:inputs]
    payload_refs = refs[inputs : inputs + count]
    attention_out = refs[inputs + count : inputs + count + outputs]
    out_refs = refs[inputs + count + outputs : inputs + 2 * count + outputs]
    send_sems, recv_sems = refs[inputs + 2 * count + outputs :]
    relay, finish = exchange_start(spreads, payload_refs, out_refs, send_sems, recv_sems)
    if with_attention:
        hooks = {}
        if not any(spreads):
            heads = attention_in[0].shape[1] // HD
            hooks[heads // 2] = functools.partial(relay, list(range(count)))
        attention_body(*attention_in, *attention_out, hooks)
    else:
        for which in range(count):
            relay([which])
    finish()


def fused_step(attention_args, payloads, spreads, collective_id):
    vmem = pl.BlockSpec(memory_space=pltpu.VMEM)
    out_shapes = []
    flops = 0
    if attention_args:
        queries, key_rows, value_rows, grad_attn = attention_args
        rows, width = queries.shape
        keys = key_rows.shape[0]
        out_shapes = [
            jax.ShapeDtypeStruct((rows, width), jnp.float32),
            jax.ShapeDtypeStruct((keys, width), jnp.float32),
            jax.ShapeDtypeStruct((keys, width), jnp.float32),
        ]
        flops = 2 * 5 * rows * keys * width * (128 // HD)
    for payload, spread in zip(payloads, spreads):
        shape = payload.shape[1:] if spread else payload.shape
        out_shapes.append(jax.ShapeDtypeStruct((len(OFFSETS),) + shape, payload.dtype))
    moved = sum(len(OFFSETS) * x.size * x.dtype.itemsize for x in payloads)
    outs = pl.pallas_call(
        functools.partial(fused_kernel, tuple(spreads), bool(attention_args)),
        out_shape=out_shapes,
        in_specs=[vmem] * (len(attention_args) + len(payloads)),
        out_specs=[vmem] * len(out_shapes),
        scratch_shapes=[
            pltpu.SemaphoreType.DMA((len(payloads), len(OFFSETS))),
            pltpu.SemaphoreType.DMA((len(payloads), len(OFFSETS))),
        ],
        compiler_params=pltpu.CompilerParams(
            collective_id=collective_id,
            has_side_effects=True,
            vmem_limit_bytes=48 * 1024 * 1024,
        ),
        cost_estimate=pl.CostEstimate(
            flops=flops, transcendentals=flops // 160, bytes_accessed=moved + 1
        ),
    )(*attention_args, *payloads)
    return list(outs)


def swap_cores(value):
    return lax.ppermute(value, "pipe", [(0, 1), (1, 0)])


def pick(own, other, core, section):
    return jnp.where(core == section, own, other)


def prepare(rows, lists, weight_in, gain_row, myself):
    points, model_width = rows.shape
    block_count = points // BLK
    scaled, inverse, normed = normalize(rows, gain_row)
    projected = jnp.dot(normed, weight_in, preferred_element_type=jnp.float32).astype(jnp.bfloat16)
    owners = lists // block_count
    within = lists % block_count
    distance = owners - myself
    slot = jnp.where(distance < 0, distance + REACH, distance + REACH - 1)
    window_at = slot * block_count + within
    return dict(
        scaled=scaled,
        inverse=inverse,
        normed=normed,
        queries=projected[:, :model_width],
        own_pairs=projected[:, model_width:],
        window_at=window_at,
    )


def attach(unit, received, weight_in):
    points, model_width = unit["queries"].shape
    received = received.reshape(len(OFFSETS) * (points // BLK), BLK, model_width)
    fetched = jnp.take(received, unit["window_at"], axis=0).reshape(-1, model_width)
    fetched_pairs = jnp.dot(
        fetched, weight_in[:, model_width:], preferred_element_type=jnp.float32
    ).astype(jnp.bfloat16)
    unit["pairs"] = jnp.concatenate([unit["own_pairs"], fetched_pairs], 0)


def outgoing(unit, grad_key, grad_value, weight_in):
    points, model_width = unit["queries"].shape
    block_count = points // BLK
    grad_pairs = jnp.concatenate([grad_key, grad_value], 1)
    grad_remote = jnp.dot(
        grad_pairs[points:].astype(jnp.bfloat16),
        weight_in[:, model_width:].T,
        preferred_element_type=jnp.float32,
    ).reshape(-1, BLK, model_width)
    slots = lax.broadcasted_iota(jnp.int32, (len(OFFSETS) * block_count, 1, 1), 0)
    window_grads = sum(
        jnp.where(slots == unit["window_at"][entry], grad_remote[entry][None], 0.0)
        for entry in range(grad_remote.shape[0])
    )
    unit["own_grad"] = grad_pairs[:points]
    return window_grads.astype(jnp.bfloat16).reshape(len(OFFSETS), points, model_width)


def complete(unit, grad_out, grad_query, returned, weight_in, gain_row):
    grad_project = jnp.concatenate([grad_query, unit["own_grad"]], 1).astype(jnp.bfloat16)
    grad_normed = jnp.dot(grad_project, weight_in.T, preferred_element_type=jnp.float32)
    grad_normed = grad_normed + jnp.sum(returned.astype(jnp.float32), axis=0)
    return (
        grad_out.astype(jnp.float32)
        + norm_backward(grad_normed, unit["scaled"], unit["inverse"], gain_row)
    ).astype(jnp.bfloat16)


def shards(saved_inputs, project_in, project_out, norm_gains, neighbour_blocks, cotangent):
    sections = lax.axis_size("pipe")
    core = lax.axis_index("pipe")
    other = sections - 1 - core
    myself = lax.axis_index("space")
    micro_count = cotangent.shape[0]
    half = micro_count // sections
    model_width = cotangent.shape[2]

    def mine(array, whose):
        grouped = array.reshape((half, sections) + array.shape[1:])
        return lax.dynamic_index_in_dim(grouped, whose, 1, keepdims=False)

    local_lists = neighbour_blocks[0, :, 0, :]
    own = (
        mine(saved_inputs[0], core),
        mine(local_lists, core),
        project_in[0],
        project_out[0],
        norm_gains[0],
    )
    got = swap_cores(
        (
            mine(saved_inputs[0], other),
            mine(local_lists, other),
            project_in[0],
            project_out[0],
            norm_gains[0],
        )
    )
    params = [
        [pick(own_part, got_part, core, section) for own_part, got_part in zip(own, got)]
        for section in range(sections)
    ]
    cotangent_mine = mine(cotangent, core)
    order = [(section, j) for section in range(sections - 1, -1, -1) for j in range(half)]
    units = [
        prepare(params[section][0][j], params[section][1][j], params[section][2], params[section][4], myself)
        for section, j in order
    ]
    results = {}
    ids = iter(range(len(order) + 2))
    first_rows = units[0]["normed"].shape[0] // 2
    first_parts = fused_step(
        (),
        [units[0]["normed"][:first_rows], units[0]["normed"][first_rows:]],
        [False, False],
        next(ids),
    )
    first_received = jnp.concatenate(first_parts, axis=1)
    attach(units[0], first_received, params[order[0][0]][2])
    pending = None
    for step, (section, j) in enumerate(order):
        unit = units[step]
        _, _, weight_in, weight_out, gain_row = params[section]
        grad_out = cotangent_mine[j] if section == sections - 1 else results[(section + 1, j)]
        unit["grad_out"] = grad_out
        grad_attn = jnp.dot(grad_out, weight_out.T, preferred_element_type=jnp.float32).astype(
            jnp.bfloat16
        )
        payloads, spreads = [], []
        if pending is not None:
            payloads.append(pending[1])
            spreads.append(True)
        if step == 0:
            for later in units[1:]:
                payloads.append(later["normed"])
                spreads.append(False)
        outs = fused_step(
            (unit["queries"], unit["pairs"][:, :model_width], unit["pairs"][:, model_width:], grad_attn),
            payloads,
            spreads,
            next(ids),
        )
        grad_query, grad_key, grad_value = outs[:3]
        received = outs[3:]
        if pending is not None:
            done_step, _ = pending
            done_section, done_j = order[done_step]
            done_unit = units[done_step]
            results[(done_section, done_j)] = complete(
                done_unit,
                done_unit["grad_out"],
                done_unit["grad_query"],
                received[0],
                params[done_section][2],
                params[done_section][4],
            )
            received = received[1:]
        if step == 0:
            for later, (later_section, _), arrived in zip(units[1:], order[1:], received):
                attach(later, arrived, params[later_section][2])
        unit["grad_query"] = grad_query
        pending = (step, outgoing(unit, grad_key, grad_value, weight_in))
    done_step, window = pending
    done_section, done_j = order[done_step]
    done_unit = units[done_step]
    (returned,) = fused_step((), [window], [True], next(ids))
    results[(done_section, done_j)] = complete(
        done_unit,
        done_unit["grad_out"],
        done_unit["grad_query"],
        returned,
        params[done_section][2],
        params[done_section][4],
    )
    own_out = jnp.stack([pick(results[(0, j)], results[(1, j)], core, 0) for j in range(half)])
    other_out = swap_cores(
        jnp.stack([pick(results[(1, j)], results[(0, j)], core, 0) for j in range(half)])
    )
    grouped = jnp.stack([pick(own_out, other_out, core, parity) for parity in range(sections)], 1)
    return grouped.reshape((1, micro_count) + grouped.shape[2:])


def solution(mesh):
    return jax.shard_map(
        shards,
        mesh=mesh,
        in_specs=(
            P("pipe", None, "space", None),
            P("pipe", None, None),
            P("pipe", None, None),
            P("pipe", None),
            P("pipe", None, "space", None),
            P(None, "space", None),
        ),
        out_specs=P("pipe", None, "space", None),
        check_vma=False,
    )
```

```python
import functools

import jax
import jax.numpy as jnp
from jax import lax
from jax.experimental import pallas as pl
from jax.experimental.pallas import tpu as pltpu
from jax.sharding import PartitionSpec as P

HEADS = 32
HD = 16
BLK = 128
REACH = 2


epsilon = 1e-05


def shifted(x, axis, by):
    peers = lax.axis_size(axis)
    pairs = [(i, i + by) for i in range(peers) if 0 <= i + by < peers]
    return lax.ppermute(x, axis, pairs)


def normalize(points, gain_row):
    values = points.astype(jnp.float32)
    centre = jnp.mean(values, axis=-1, keepdims=True)
    spread = jnp.mean(jnp.square(values - centre), axis=-1, keepdims=True)
    inverse = lax.rsqrt(spread + epsilon)
    scaled = (values - centre) * inverse
    return (scaled, inverse, (scaled * gain_row).astype(jnp.bfloat16))


def norm_backward(grad_normed, scaled, inverse, gain_row):
    weighted = grad_normed * gain_row
    return inverse * (
        weighted
        - jnp.mean(weighted, axis=-1, keepdims=True)
        - scaled * jnp.mean(weighted * scaled, axis=-1, keepdims=True)
    )


MESH = pl.DeviceIdType.MESH
OFFSETS = [shift_by for shift_by in range(-REACH, REACH + 1) if shift_by != 0]


def attention_body(q_ref, k_ref, v_ref, g_ref, dq_ref, dk_ref, dv_ref, hooks):
    factor = HD ** (-0.5)
    group = 128
    per_group = group // HD
    nt = (((1,), (1,)), ((), ()))
    tn = (((0,), (0,)), ((), ()))
    head_of = lax.broadcasted_iota(jnp.int32, (1, group), 1) // HD
    dq_ref[...] = jnp.zeros_like(dq_ref)
    dk_ref[...] = jnp.zeros_like(dk_ref)
    dv_ref[...] = jnp.zeros_like(dv_ref)

    def head(index, carry):
        cols = pl.ds(pl.multiple_of((index // per_group) * group, group), group)
        mask = head_of == index % per_group
        q = q_ref[:, cols]
        k = k_ref[:, cols]
        v = v_ref[:, cols]
        g = g_ref[:, cols]
        qm = jnp.where(mask, q, jnp.zeros_like(q))
        km = jnp.where(mask, k, jnp.zeros_like(k))
        gm = jnp.where(mask, g, jnp.zeros_like(g))
        scores = lax.dot_general(qm, k, nt, preferred_element_type=jnp.float32) * factor
        top = jnp.max(scores, axis=-1, keepdims=True)
        exps = jnp.exp(scores - top)
        attention = exps * (1.0 / jnp.sum(exps, axis=-1, keepdims=True))
        grad_probs = lax.dot_general(gm, v, nt, preferred_element_type=jnp.float32)
        row = jnp.sum(attention * grad_probs, axis=-1, keepdims=True)
        grad_scores = (attention * (grad_probs - row) * factor).astype(jnp.bfloat16)
        dq_ref[:, cols] += jnp.dot(grad_scores, km, preferred_element_type=jnp.float32)
        dk_ref[:, cols] += lax.dot_general(grad_scores, qm, tn, preferred_element_type=jnp.float32)
        dv_ref[:, cols] += lax.dot_general(
            attention.astype(jnp.bfloat16), gm, tn, preferred_element_type=jnp.float32
        )
        return carry

    heads = q_ref.shape[1] // HD
    if not hooks:
        lax.fori_loop(0, heads, head, 0, unroll=4)
    else:
        begin = 0
        for edge in sorted(hooks):
            lax.fori_loop(begin, edge, head, 0, unroll=4)
            hooks[edge]()
            begin = edge
        lax.fori_loop(begin, heads, head, 0, unroll=4)


def exchange_start(spreads, payload_refs, out_refs, send_sems, recv_sems):
    core = lax.axis_index("pipe")
    me = lax.axis_index("space")
    peers = lax.axis_size("space")
    barrier = pltpu.get_barrier_semaphore()

    def exists(shift_by):
        return (me + shift_by >= 0) & (me + shift_by < peers)

    def slot(shift_by):
        return OFFSETS.index(shift_by)

    for shift_by in OFFSETS:

        @pl.when(exists(shift_by))
        def _():
            pl.semaphore_signal(barrier, 1, device_id=(core, me + shift_by), device_id_type=MESH)

    pl.semaphore_wait(barrier, sum(jnp.where(exists(shift_by), 1, 0) for shift_by in OFFSETS))

    def describe(which, source, landing, shift_by):
        return pltpu.make_async_remote_copy(
            src_ref=source,
            dst_ref=out_refs[which].at[landing],
            send_sem=send_sems.at[which, landing],
            recv_sem=recv_sems.at[which, landing],
            device_id=(core, me + shift_by),
            device_id_type=MESH,
        )

    def arrival(which, landing):
        return describe(which, out_refs[which].at[landing], landing, OFFSETS[landing])

    direct = []
    relayed = []
    relaying = not any(spreads)
    for which, spread in enumerate(spreads):
        x_ref = payload_refs[which]
        targets = OFFSETS if spread or not relaying else [-1, 1]
        for shift_by in targets:
            source = x_ref.at[slot(shift_by)] if spread else x_ref
            copy = describe(which, source, slot(-shift_by), shift_by)
            direct.append((copy, exists(shift_by)))

            @pl.when(exists(shift_by))
            def _():
                copy.start()

        for shift_by in OFFSETS:

            @pl.when(jnp.logical_not(exists(shift_by)))
            def _():
                out_refs[which][slot(shift_by)] = jnp.zeros(
                    out_refs[which].shape[1:], out_refs[which].dtype
                )

        if relaying and not spread:
            for shift_by in (-1, 1):
                forward = describe(
                    which, out_refs[which].at[slot(-shift_by)], slot(-2 * shift_by), shift_by
                )
                relayed.append((which, shift_by, forward, exists(shift_by) & exists(-shift_by)))

    def relay(whiches):
        chosen = [entry for entry in relayed if entry[0] in whiches]
        for which, shift_by, forward, valid in chosen:

            @pl.when(exists(-shift_by))
            def _():
                arrival(which, slot(-shift_by)).wait_recv()

        for which, shift_by, forward, valid in chosen:

            @pl.when(valid)
            def _():
                forward.start()

    def finish():
        for copy, valid in direct:

            @pl.when(valid)
            def _():
                copy.wait_send()

        for which, shift_by, forward, valid in relayed:

            @pl.when(valid)
            def _():
                forward.wait_send()

        relayed_slots = {(which, slot(-shift_by)) for which, shift_by, _, _ in relayed}
        for which in range(len(spreads)):
            for landing, shift_by in enumerate(OFFSETS):
                if (which, landing) in relayed_slots:
                    continue

                @pl.when(exists(shift_by))
                def _():
                    arrival(which, landing).wait_recv()

    return relay, finish


def fused_kernel(spreads, with_attention, *refs):
    count = len(spreads)
    inputs = 4 if with_attention else 0
    outputs = 3 if with_attention else 0
    attention_in = refs[:inputs]
    payload_refs = refs[inputs : inputs + count]
    attention_out = refs[inputs + count : inputs + count + outputs]
    out_refs = refs[inputs + count + outputs : inputs + 2 * count + outputs]
    send_sems, recv_sems = refs[inputs + 2 * count + outputs :]
    relay, finish = exchange_start(spreads, payload_refs, out_refs, send_sems, recv_sems)
    if with_attention:
        hooks = {}
        if not any(spreads):
            heads = attention_in[0].shape[1] // HD
            hooks[heads // 2] = functools.partial(relay, list(range(count)))
        attention_body(*attention_in, *attention_out, hooks)
    else:
        relay(list(range(count)))
    finish()


def fused_step(attention_args, payloads, spreads, collective_id):
    vmem = pl.BlockSpec(memory_space=pltpu.VMEM)
    out_shapes = []
    flops = 0
    if attention_args:
        queries, key_rows, value_rows, grad_attn = attention_args
        rows, width = queries.shape
        keys = key_rows.shape[0]
        out_shapes = [
            jax.ShapeDtypeStruct((rows, width), jnp.float32),
            jax.ShapeDtypeStruct((keys, width), jnp.float32),
            jax.ShapeDtypeStruct((keys, width), jnp.float32),
        ]
        flops = 2 * 5 * rows * keys * width * (128 // HD)
    for payload, spread in zip(payloads, spreads):
        shape = payload.shape[1:] if spread else payload.shape
        out_shapes.append(jax.ShapeDtypeStruct((len(OFFSETS),) + shape, payload.dtype))
    moved = sum(len(OFFSETS) * x.size * x.dtype.itemsize for x in payloads)
    outs = pl.pallas_call(
        functools.partial(fused_kernel, tuple(spreads), bool(attention_args)),
        out_shape=out_shapes,
        in_specs=[vmem] * (len(attention_args) + len(payloads)),
        out_specs=[vmem] * len(out_shapes),
        scratch_shapes=[
            pltpu.SemaphoreType.DMA((len(payloads), len(OFFSETS))),
            pltpu.SemaphoreType.DMA((len(payloads), len(OFFSETS))),
        ],
        compiler_params=pltpu.CompilerParams(
            collective_id=collective_id,
            has_side_effects=True,
            vmem_limit_bytes=48 * 1024 * 1024,
        ),
        cost_estimate=pl.CostEstimate(
            flops=flops, transcendentals=flops // 160, bytes_accessed=moved + 1
        ),
    )(*attention_args, *payloads)
    return list(outs)


def swap_cores(value):
    return lax.ppermute(value, "pipe", [(0, 1), (1, 0)])


def pick(own, other, core, section):
    return jnp.where(core == section, own, other)


def prepare(rows, lists, weight_in, gain_row, myself):
    points, model_width = rows.shape
    block_count = points // BLK
    scaled, inverse, normed = normalize(rows, gain_row)
    projected = jnp.dot(normed, weight_in, preferred_element_type=jnp.float32).astype(jnp.bfloat16)
    owners = lists // block_count
    within = lists % block_count
    distance = owners - myself
    slot = jnp.where(distance < 0, distance + REACH, distance + REACH - 1)
    window_at = slot * block_count + within
    return dict(
        scaled=scaled,
        inverse=inverse,
        normed=normed,
        queries=projected[:, :model_width],
        own_pairs=projected[:, model_width:],
        window_at=window_at,
    )


def attach(unit, received, weight_in):
    points, model_width = unit["queries"].shape
    received = received.reshape(len(OFFSETS) * (points // BLK), BLK, model_width)
    fetched = jnp.take(received, unit["window_at"], axis=0).reshape(-1, model_width)
    fetched_pairs = jnp.dot(
        fetched, weight_in[:, model_width:], preferred_element_type=jnp.float32
    ).astype(jnp.bfloat16)
    unit["pairs"] = jnp.concatenate([unit["own_pairs"], fetched_pairs], 0)


def outgoing(unit, grad_key, grad_value, weight_in):
    points, model_width = unit["queries"].shape
    block_count = points // BLK
    grad_pairs = jnp.concatenate([grad_key, grad_value], 1)
    grad_remote = jnp.dot(
        grad_pairs[points:].astype(jnp.bfloat16),
        weight_in[:, model_width:].T,
        preferred_element_type=jnp.float32,
    ).reshape(-1, BLK, model_width)
    slots = lax.broadcasted_iota(jnp.int32, (len(OFFSETS) * block_count, 1, 1), 0)
    window_grads = sum(
        jnp.where(slots == unit["window_at"][entry], grad_remote[entry][None], 0.0)
        for entry in range(grad_remote.shape[0])
    )
    unit["own_grad"] = grad_pairs[:points]
    return window_grads.astype(jnp.bfloat16).reshape(len(OFFSETS), points, model_width)


def complete(unit, grad_out, grad_query, returned, weight_in, gain_row):
    grad_project = jnp.concatenate([grad_query, unit["own_grad"]], 1).astype(jnp.bfloat16)
    grad_normed = jnp.dot(grad_project, weight_in.T, preferred_element_type=jnp.float32)
    grad_normed = grad_normed + jnp.sum(returned.astype(jnp.float32), axis=0)
    return (
        grad_out.astype(jnp.float32)
        + norm_backward(grad_normed, unit["scaled"], unit["inverse"], gain_row)
    ).astype(jnp.bfloat16)


def shards(saved_inputs, project_in, project_out, norm_gains, neighbour_blocks, cotangent):
    sections = lax.axis_size("pipe")
    core = lax.axis_index("pipe")
    other = sections - 1 - core
    myself = lax.axis_index("space")
    micro_count = cotangent.shape[0]
    half = micro_count // sections
    model_width = cotangent.shape[2]

    def mine(array, whose):
        grouped = array.reshape((half, sections) + array.shape[1:])
        return lax.dynamic_index_in_dim(grouped, whose, 1, keepdims=False)

    local_lists = neighbour_blocks[0, :, 0, :]
    own = (
        mine(saved_inputs[0], core),
        mine(local_lists, core),
        project_in[0],
        project_out[0],
        norm_gains[0],
    )
    got = swap_cores(
        (
            mine(saved_inputs[0], other),
            mine(local_lists, other),
            project_in[0],
            project_out[0],
            norm_gains[0],
        )
    )
    params = [
        list(
            lax.optimization_barrier(
                tuple(pick(own_part, got_part, core, section) for own_part, got_part in zip(own, got))
            )
        )
        for section in range(sections)
    ]
    cotangent_mine = mine(cotangent, core)
    order = [(section, j) for section in range(sections - 1, -1, -1) for j in range(half)]
    units = [
        prepare(params[section][0][j], params[section][1][j], params[section][2], params[section][4], myself)
        for section, j in order
    ]
    results = {}
    ids = iter(range(len(order) + 2))
    (first_received,) = fused_step((), [units[0]["normed"]], [False], next(ids))
    attach(units[0], first_received, params[order[0][0]][2])
    pending = None
    for step, (section, j) in enumerate(order):
        unit = units[step]
        _, _, weight_in, weight_out, gain_row = params[section]
        grad_out = cotangent_mine[j] if section == sections - 1 else results[(section + 1, j)]
        unit["grad_out"] = grad_out
        grad_attn = jnp.dot(grad_out, weight_out.T, preferred_element_type=jnp.float32).astype(
            jnp.bfloat16
        )
        payloads, spreads = [], []
        if pending is not None:
            payloads.append(pending[1])
            spreads.append(True)
        if step == 0:
            for later in units[1:]:
                payloads.append(later["normed"])
                spreads.append(False)
        outs = fused_step(
            (unit["queries"], unit["pairs"][:, :model_width], unit["pairs"][:, model_width:], grad_attn),
            payloads,
            spreads,
            next(ids),
        )
        grad_query, grad_key, grad_value = outs[:3]
        received = outs[3:]
        if pending is not None:
            done_step, _ = pending
            done_section, done_j = order[done_step]
            done_unit = units[done_step]
            results[(done_section, done_j)] = complete(
                done_unit,
                done_unit["grad_out"],
                done_unit["grad_query"],
                received[0],
                params[done_section][2],
                params[done_section][4],
            )
            received = received[1:]
        if step == 0:
            for later, (later_section, _), arrived in zip(units[1:], order[1:], received):
                attach(later, arrived, params[later_section][2])
        unit["grad_query"] = grad_query
        pending = (step, outgoing(unit, grad_key, grad_value, weight_in))
    done_step, window = pending
    done_section, done_j = order[done_step]
    done_unit = units[done_step]
    (returned,) = fused_step((), [window], [True], next(ids))
    results[(done_section, done_j)] = complete(
        done_unit,
        done_unit["grad_out"],
        done_unit["grad_query"],
        returned,
        params[done_section][2],
        params[done_section][4],
    )
    own_out = jnp.stack([pick(results[(0, j)], results[(1, j)], core, 0) for j in range(half)])
    other_out = swap_cores(
        jnp.stack([pick(results[(1, j)], results[(0, j)], core, 0) for j in range(half)])
    )
    grouped = jnp.stack([pick(own_out, other_out, core, parity) for parity in range(sections)], 1)
    return grouped.reshape((1, micro_count) + grouped.shape[2:])


def solution(mesh):
    return jax.shard_map(
        shards,
        mesh=mesh,
        in_specs=(
            P("pipe", None, "space", None),
            P("pipe", None, None),
            P("pipe", None, None),
            P("pipe", None),
            P("pipe", None, "space", None),
            P(None, "space", None),
        ),
        out_specs=P("pipe", None, "space", None),
        check_vma=False,
    )
```

```python
import functools

import jax
import jax.numpy as jnp
from jax import lax
from jax.experimental import pallas as pl
from jax.experimental.pallas import tpu as pltpu
from jax.sharding import PartitionSpec as P

HEADS = 32
HD = 16
BLK = 128
REACH = 2


epsilon = 1e-05


def shifted(x, axis, by):
    peers = lax.axis_size(axis)
    pairs = [(i, i + by) for i in range(peers) if 0 <= i + by < peers]
    return lax.ppermute(x, axis, pairs)


def normalize(points, gain_row):
    values = points.astype(jnp.float32)
    centre = jnp.mean(values, axis=-1, keepdims=True)
    spread = jnp.mean(jnp.square(values - centre), axis=-1, keepdims=True)
    inverse = lax.rsqrt(spread + epsilon)
    scaled = (values - centre) * inverse
    return (scaled, inverse, (scaled * gain_row).astype(jnp.bfloat16))


def norm_backward(grad_normed, scaled, inverse, gain_row):
    weighted = grad_normed * gain_row
    return inverse * (
        weighted
        - jnp.mean(weighted, axis=-1, keepdims=True)
        - scaled * jnp.mean(weighted * scaled, axis=-1, keepdims=True)
    )


MESH = pl.DeviceIdType.MESH
OFFSETS = [shift_by for shift_by in range(-REACH, REACH + 1) if shift_by != 0]


def attention_body(q_ref, k_ref, v_ref, g_ref, dq_ref, dk_ref, dv_ref, hooks):
    factor = HD ** (-0.5)
    group = 128
    per_group = group // HD
    nt = (((1,), (1,)), ((), ()))
    tn = (((0,), (0,)), ((), ()))
    head_of = lax.broadcasted_iota(jnp.int32, (1, group), 1) // HD
    dq_ref[...] = jnp.zeros_like(dq_ref)
    dk_ref[...] = jnp.zeros_like(dk_ref)
    dv_ref[...] = jnp.zeros_like(dv_ref)

    def head(index, carry):
        cols = pl.ds(pl.multiple_of((index // per_group) * group, group), group)
        mask = head_of == index % per_group
        q = q_ref[:, cols]
        k = k_ref[:, cols]
        v = v_ref[:, cols]
        g = g_ref[:, cols]
        qm = jnp.where(mask, q, jnp.zeros_like(q))
        km = jnp.where(mask, k, jnp.zeros_like(k))
        gm = jnp.where(mask, g, jnp.zeros_like(g))
        scores = lax.dot_general(qm, k, nt, preferred_element_type=jnp.float32) * factor
        top = jnp.max(scores, axis=-1, keepdims=True)
        exps = jnp.exp(scores - top)
        attention = exps * (1.0 / jnp.sum(exps, axis=-1, keepdims=True))
        grad_probs = lax.dot_general(gm, v, nt, preferred_element_type=jnp.float32)
        row = jnp.sum(attention * grad_probs, axis=-1, keepdims=True)
        grad_scores = (attention * (grad_probs - row) * factor).astype(jnp.bfloat16)
        dq_ref[:, cols] += jnp.dot(grad_scores, km, preferred_element_type=jnp.float32)
        dk_ref[:, cols] += lax.dot_general(grad_scores, qm, tn, preferred_element_type=jnp.float32)
        dv_ref[:, cols] += lax.dot_general(
            attention.astype(jnp.bfloat16), gm, tn, preferred_element_type=jnp.float32
        )
        return carry

    heads = q_ref.shape[1] // HD
    if not hooks:
        lax.fori_loop(0, heads, head, 0, unroll=4)
    else:
        begin = 0
        for edge in sorted(hooks):
            lax.fori_loop(begin, edge, head, 0, unroll=4)
            hooks[edge]()
            begin = edge
        lax.fori_loop(begin, heads, head, 0, unroll=4)


def exchange_start(spreads, payload_refs, out_refs, send_sems, recv_sems):
    core = lax.axis_index("pipe")
    me = lax.axis_index("space")
    peers = lax.axis_size("space")
    barrier = pltpu.get_barrier_semaphore()

    def exists(shift_by):
        return (me + shift_by >= 0) & (me + shift_by < peers)

    def slot(shift_by):
        return OFFSETS.index(shift_by)

    for shift_by in OFFSETS:

        @pl.when(exists(shift_by))
        def _():
            pl.semaphore_signal(barrier, 1, device_id=(core, me + shift_by), device_id_type=MESH)

    pl.semaphore_wait(barrier, sum(jnp.where(exists(shift_by), 1, 0) for shift_by in OFFSETS))

    def describe(which, source, landing, shift_by):
        return pltpu.make_async_remote_copy(
            src_ref=source,
            dst_ref=out_refs[which].at[landing],
            send_sem=send_sems.at[which, landing],
            recv_sem=recv_sems.at[which, landing],
            device_id=(core, me + shift_by),
            device_id_type=MESH,
        )

    def arrival(which, landing):
        return describe(which, out_refs[which].at[landing], landing, OFFSETS[landing])

    direct = []
    relayed = []
    relaying = not any(spreads)
    for which, spread in enumerate(spreads):
        x_ref = payload_refs[which]
        targets = OFFSETS if spread or not relaying else [-1, 1]
        for shift_by in targets:
            source = x_ref.at[slot(shift_by)] if spread else x_ref
            copy = describe(which, source, slot(-shift_by), shift_by)
            direct.append((copy, exists(shift_by)))

            @pl.when(exists(shift_by))
            def _():
                copy.start()

        for shift_by in OFFSETS:

            @pl.when(jnp.logical_not(exists(shift_by)))
            def _():
                out_refs[which][slot(shift_by)] = jnp.zeros(
                    out_refs[which].shape[1:], out_refs[which].dtype
                )

        if relaying and not spread:
            for shift_by in (-1, 1):
                forward = describe(
                    which, out_refs[which].at[slot(-shift_by)], slot(-2 * shift_by), shift_by
                )
                relayed.append((which, shift_by, forward, exists(shift_by) & exists(-shift_by)))

    def relay(whiches):
        chosen = [entry for entry in relayed if entry[0] in whiches]
        for which, shift_by, forward, valid in chosen:

            @pl.when(exists(-shift_by))
            def _():
                arrival(which, slot(-shift_by)).wait_recv()

        for which, shift_by, forward, valid in chosen:

            @pl.when(valid)
            def _():
                forward.start()

    def finish():
        for copy, valid in direct:

            @pl.when(valid)
            def _():
                copy.wait_send()

        for which, shift_by, forward, valid in relayed:

            @pl.when(valid)
            def _():
                forward.wait_send()

        relayed_slots = {(which, slot(-shift_by)) for which, shift_by, _, _ in relayed}
        for which in range(len(spreads)):
            for landing, shift_by in enumerate(OFFSETS):
                if (which, landing) in relayed_slots:
                    continue

                @pl.when(exists(shift_by))
                def _():
                    arrival(which, landing).wait_recv()

    return relay, finish


def fused_kernel(spreads, with_attention, *refs):
    count = len(spreads)
    inputs = 4 if with_attention else 0
    outputs = 3 if with_attention else 0
    attention_in = refs[:inputs]
    payload_refs = refs[inputs : inputs + count]
    attention_out = refs[inputs + count : inputs + count + outputs]
    out_refs = refs[inputs + count + outputs : inputs + 2 * count + outputs]
    send_sems, recv_sems = refs[inputs + 2 * count + outputs :]
    relay, finish = exchange_start(spreads, payload_refs, out_refs, send_sems, recv_sems)
    if with_attention:
        hooks = {}
        if not any(spreads):
            heads = attention_in[0].shape[1] // HD
            hooks[heads // 2] = functools.partial(relay, list(range(count)))
        attention_body(*attention_in, *attention_out, hooks)
    else:
        for which in range(count):
            relay([which])
    finish()


def fused_step(attention_args, payloads, spreads, collective_id):
    vmem = pl.BlockSpec(memory_space=pltpu.VMEM)
    out_shapes = []
    flops = 0
    if attention_args:
        queries, key_rows, value_rows, grad_attn = attention_args
        rows, width = queries.shape
        keys = key_rows.shape[0]
        out_shapes = [
            jax.ShapeDtypeStruct((rows, width), jnp.float32),
            jax.ShapeDtypeStruct((keys, width), jnp.float32),
            jax.ShapeDtypeStruct((keys, width), jnp.float32),
        ]
        flops = 2 * 5 * rows * keys * width * (128 // HD)
    for payload, spread in zip(payloads, spreads):
        shape = payload.shape[1:] if spread else payload.shape
        out_shapes.append(jax.ShapeDtypeStruct((len(OFFSETS),) + shape, payload.dtype))
    moved = sum(len(OFFSETS) * x.size * x.dtype.itemsize for x in payloads)
    outs = pl.pallas_call(
        functools.partial(fused_kernel, tuple(spreads), bool(attention_args)),
        out_shape=out_shapes,
        in_specs=[vmem] * (len(attention_args) + len(payloads)),
        out_specs=[vmem] * len(out_shapes),
        scratch_shapes=[
            pltpu.SemaphoreType.DMA((len(payloads), len(OFFSETS))),
            pltpu.SemaphoreType.DMA((len(payloads), len(OFFSETS))),
        ],
        compiler_params=pltpu.CompilerParams(
            collective_id=collective_id,
            has_side_effects=True,
            vmem_limit_bytes=48 * 1024 * 1024,
        ),
        cost_estimate=pl.CostEstimate(
            flops=flops, transcendentals=flops // 160, bytes_accessed=moved + 1
        ),
    )(*attention_args, *payloads)
    return list(outs)


def swap_cores(value):
    return lax.ppermute(value, "pipe", [(0, 1), (1, 0)])


def pick(own, other, core, section):
    return jnp.where(core == section, own, other)


def prepare(rows, lists, weight_in, gain_row, myself):
    points, model_width = rows.shape
    block_count = points // BLK
    scaled, inverse, normed = normalize(rows, gain_row)
    projected = jnp.dot(normed, weight_in, preferred_element_type=jnp.float32).astype(jnp.bfloat16)
    owners = lists // block_count
    within = lists % block_count
    distance = owners - myself
    slot = jnp.where(distance < 0, distance + REACH, distance + REACH - 1)
    window_at = slot * block_count + within
    return dict(
        scaled=scaled,
        inverse=inverse,
        normed=normed,
        queries=projected[:, :model_width],
        own_pairs=projected[:, model_width:],
        window_at=window_at,
    )


def attach(unit, received, weight_in):
    points, model_width = unit["queries"].shape
    received = received.reshape(len(OFFSETS) * (points // BLK), BLK, model_width)
    fetched = jnp.take(received, unit["window_at"], axis=0).reshape(-1, model_width)
    fetched_pairs = jnp.dot(
        fetched, weight_in[:, model_width:], preferred_element_type=jnp.float32
    ).astype(jnp.bfloat16)
    unit["pairs"] = jnp.concatenate([unit["own_pairs"], fetched_pairs], 0)


def outgoing(unit, grad_key, grad_value, weight_in):
    points, model_width = unit["queries"].shape
    block_count = points // BLK
    grad_pairs = jnp.concatenate([grad_key, grad_value], 1)
    grad_remote = jnp.dot(
        grad_pairs[points:].astype(jnp.bfloat16),
        weight_in[:, model_width:].T,
        preferred_element_type=jnp.float32,
    ).reshape(-1, BLK, model_width)
    slots = lax.broadcasted_iota(jnp.int32, (len(OFFSETS) * block_count, 1, 1), 0)
    window_grads = sum(
        jnp.where(slots == unit["window_at"][entry], grad_remote[entry][None], 0.0)
        for entry in range(grad_remote.shape[0])
    )
    unit["own_grad"] = grad_pairs[:points]
    return window_grads.astype(jnp.bfloat16).reshape(len(OFFSETS), points, model_width)


def complete(unit, grad_out, grad_query, returned, weight_in, gain_row):
    grad_project = jnp.concatenate([grad_query, unit["own_grad"]], 1).astype(jnp.bfloat16)
    grad_normed = jnp.dot(grad_project, weight_in.T, preferred_element_type=jnp.float32)
    grad_normed = grad_normed + jnp.sum(returned.astype(jnp.float32), axis=0)
    return (
        grad_out.astype(jnp.float32)
        + norm_backward(grad_normed, unit["scaled"], unit["inverse"], gain_row)
    ).astype(jnp.bfloat16)


def shards(saved_inputs, project_in, project_out, norm_gains, neighbour_blocks, cotangent):
    sections = lax.axis_size("pipe")
    core = lax.axis_index("pipe")
    other = sections - 1 - core
    myself = lax.axis_index("space")
    micro_count = cotangent.shape[0]
    half = micro_count // sections
    model_width = cotangent.shape[2]

    def mine(array, whose):
        grouped = array.reshape((half, sections) + array.shape[1:])
        return lax.dynamic_index_in_dim(grouped, whose, 1, keepdims=False)

    local_lists = neighbour_blocks[0, :, 0, :]
    own = (
        mine(saved_inputs[0], core),
        mine(local_lists, core),
        project_in[0],
        project_out[0],
        norm_gains[0],
    )
    got = swap_cores(
        (
            mine(saved_inputs[0], other),
            mine(local_lists, other),
            project_in[0],
            project_out[0],
            norm_gains[0],
        )
    )
    params = [
        [pick(own_part, got_part, core, section) for own_part, got_part in zip(own, got)]
        for section in range(sections)
    ]
    cotangent_mine = mine(cotangent, core)
    order = [(section, j) for section in range(sections - 1, -1, -1) for j in range(half)]
    units = [
        prepare(params[section][0][j], params[section][1][j], params[section][2], params[section][4], myself)
        for section, j in order
    ]
    results = {}
    ids = iter(range(len(order) + 2))
    early = min(2, len(units))
    first_received = fused_step((), [unit["normed"] for unit in units[:early]], [False] * early, next(ids))
    for unit, (unit_section, _), arrived in zip(units[:early], order[:early], first_received):
        attach(unit, arrived, params[unit_section][2])
    pending = None
    for step, (section, j) in enumerate(order):
        unit = units[step]
        _, _, weight_in, weight_out, gain_row = params[section]
        grad_out = cotangent_mine[j] if section == sections - 1 else results[(section + 1, j)]
        unit["grad_out"] = grad_out
        grad_attn = jnp.dot(grad_out, weight_out.T, preferred_element_type=jnp.float32).astype(
            jnp.bfloat16
        )
        payloads, spreads = [], []
        if pending is not None:
            payloads.append(pending[1])
            spreads.append(True)
        if step == 0:
            for later in units[early:]:
                payloads.append(later["normed"])
                spreads.append(False)
        outs = fused_step(
            (unit["queries"], unit["pairs"][:, :model_width], unit["pairs"][:, model_width:], grad_attn),
            payloads,
            spreads,
            next(ids),
        )
        grad_query, grad_key, grad_value = outs[:3]
        received = outs[3:]
        if pending is not None:
            done_step, _ = pending
            done_section, done_j = order[done_step]
            done_unit = units[done_step]
            results[(done_section, done_j)] = complete(
                done_unit,
                done_unit["grad_out"],
                done_unit["grad_query"],
                received[0],
                params[done_section][2],
                params[done_section][4],
            )
            received = received[1:]
        if step == 0:
            for later, (later_section, _), arrived in zip(units[early:], order[early:], received):
                attach(later, arrived, params[later_section][2])
        unit["grad_query"] = grad_query
        pending = (step, outgoing(unit, grad_key, grad_value, weight_in))
    done_step, window = pending
    done_section, done_j = order[done_step]
    done_unit = units[done_step]
    (returned,) = fused_step((), [window], [True], next(ids))
    results[(done_section, done_j)] = complete(
        done_unit,
        done_unit["grad_out"],
        done_unit["grad_query"],
        returned,
        params[done_section][2],
        params[done_section][4],
    )
    own_out = jnp.stack([pick(results[(0, j)], results[(1, j)], core, 0) for j in range(half)])
    other_out = swap_cores(
        jnp.stack([pick(results[(1, j)], results[(0, j)], core, 0) for j in range(half)])
    )
    grouped = jnp.stack([pick(own_out, other_out, core, parity) for parity in range(sections)], 1)
    return grouped.reshape((1, micro_count) + grouped.shape[2:])


def solution(mesh):
    return jax.shard_map(
        shards,
        mesh=mesh,
        in_specs=(
            P("pipe", None, "space", None),
            P("pipe", None, None),
            P("pipe", None, None),
            P("pipe", None),
            P("pipe", None, "space", None),
            P(None, "space", None),
        ),
        out_specs=P("pipe", None, "space", None),
        check_vma=False,
    )
```
